32 devices in a mesh: fsdp: 4 (over z), ctx: 2 (over y), tp: 4 (over x, core).
Axes of the slice: x: 2, y: 2, z: 4, core: 2. Of those that a mesh axis runs over, the one named last changes fastest.
Arguments:
- inputs: bfloat16 [6144, 2048], P(('fsdp', 'ctx')), may hold values from -6 to 6
- loss_sensitivity: bfloat16 [6144, 2048], P(('fsdp', 'ctx')), may hold values from -6 to 6
- parent_block: int32 [4, 6], P('fsdp'), may hold values from -1 to 4, as said below
- adapter_of: int32 [8], replicated, may hold values from 0 to 7, each once
- w_qkv: bfloat16 [3, 2048, 2048], P(None, 'fsdp', 'tp'), may hold values from -0.125 to 0.125
- bias_qv: float32 [2, 2048], P(None, 'tp'), may hold values from -3 to 3
- w_o: bfloat16 [2048, 2048], P('tp', 'fsdp'), may hold values from -1 to 1
- exit_offsets: float32 [2, 2048], replicated, may hold values from -3 to 3
- ln_gain: float32 [2, 2048], replicated, may hold values from 0.5 to 1.5
- ln_bias: float32 [2, 2048], replicated, may hold values from -2 to 2
- w_in: bfloat16 [2048, 8192], P('fsdp', 'tp'), may hold values from -0.125 to 0.125
- hidden_offset_frozen: float32 [8192], P('tp'), may hold values from -3 to 3
- w_out: bfloat16 [8192, 2048], P('tp', 'fsdp'), may hold values from -0.0625 to 0.0625
- a_attn: float32 [4, 8, 2048, 16], replicated, may hold values from -0.25 to 0.25
- b_attn: float32 [4, 8, 16, 2048], replicated, may hold values from -1.5 to 1.5
- a_up: float32 [8, 2048, 16], replicated, may hold values from -0.25 to 0.25
- b_up: float32 [8, 16, 8192], P(None, None, 'tp'), may hold values from -1.5 to 1.5
- a_down: float32 [8, 8192, 16], P(None, 'tp'), may hold values from -0.125 to 0.125
- b_down: float32 [8, 16, 2048], replicated, may hold values from -1.5 to 1.5
Outputs:
- layer_out: bfloat16 [6144, 2048], P(('fsdp', 'ctx'))
- grad_inputs: bfloat16 [6144, 2048], P(('fsdp', 'ctx'))
- grad_a_attn: float32 [4, 8, 2048, 16], P(None, None, ('tp', 'fsdp', 'ctx'))
- grad_b_attn: float32 [4, 8, 16, 2048], P(None, None, None, ('tp', 'fsdp', 'ctx'))
- grad_a_up: float32 [8, 2048, 16], P(None, ('tp', 'fsdp', 'ctx'))
- grad_b_up: float32 [8, 16, 8192], P(None, None, ('tp', 'fsdp', 'ctx'))
- grad_a_down: float32 [8, 8192, 16], P(None, ('tp', 'fsdp', 'ctx'))
- grad_b_down: float32 [8, 16, 2048], P(None, None, ('tp', 'fsdp', 'ctx'))
The draws below stay inside these ranges and needn't reach their ends.
Inputs may be any that keep to these rules, and one draw needn't show every extreme that they name: parent_block[g, b] is -1 where block b is the first block of one of group g's 2 trees, else an earlier block of the same tree; trees are numbered by the order of their first blocks. adapter_of[g * 2 + t] is the adapter set of tree t of group g; the entries are a permutation.
All inputs are finite; a program needn't handle non-finite values.
Results may differ from the reference program's by a relative error of at most 0.025.
Values may be sent and summed in bfloat16 or wider, within the bound.
No kernel may reach another device: no remote copies, remote signals or barrier semaphores. Data moves between devices by JAX's collectives and lax.ppermute only.
A program may use at most 256 MiB of HBM per device.

```python
import math
import jax
import jax.numpy as jnp
from jax import lax

D = 2048
HEADS = 16
HD = 128
FF = 8192
RANK = 16
ADAPTERS = 8
TREES_GROUP = 2
BLOCK = 256
BLOCKS_GROUP = 6
GROUP_TOKENS = 1536
GROUPS = 4
TOKENS = 6144


def one_group(group_key):
    key_long, key_member, key_choice, key_chain = jax.random.split(group_key, 4)
    block_total = BLOCKS_GROUP
    position = jnp.arange(block_total, dtype=jnp.int32)
    long_tree = jax.random.randint(key_long, (), 0, TREES_GROUP)
    member = jax.random.randint(key_member, (block_total,), 0, TREES_GROUP)
    forced = (position == block_total // 2) | (position >= block_total - 2)
    member = jnp.where(forced, long_tree, member)
    member = jnp.where(position < TREES_GROUP, position, member)
    same_tree = (member[:, None] == member[None, :]) & (position[None, :] < position[:, None])
    nearest = jnp.max(jnp.where(same_tree, position[None, :], -1), axis=1)
    choice_scores = jax.random.randint(key_choice, (block_total, block_total), 0, 1 << 16) * block_total + position[None, :]
    choice_scores = jnp.where(same_tree, choice_scores, -1)
    chosen = lax.top_k(choice_scores, 1)[1][:, 0].astype(jnp.int32)
    chained = jax.random.randint(key_chain, (block_total,), 0, 2) > 0
    parent = jnp.where(chained | (position == block_total - 1), nearest, chosen)
    parent = jnp.where(nearest < 0, -1, parent)
    return parent.astype(jnp.int32)


def draw_parent_block(key, part):
    base = jax.random.fold_in(key, 7919)
    return jax.vmap(one_group)(jax.random.split(base, GROUPS))


def shard_levels(key, dims, shards, smallest, high):
    gain = 1.0
    for dim, parts in shards:
        draws = jax.random.uniform(jax.random.fold_in(jax.random.fold_in(key, 6), dim), (parts,), jnp.float32, smallest / len(shards), high / len(shards))
        gain = gain * jnp.repeat(jnp.exp(draws), dims[dim] // parts).reshape((-1,) + (1,) * (len(dims) - 1 - dim))
    return gain


def noise(key, shape, scale, most, cuts=(), held_as=jnp.bfloat16):
    loudness = shard_levels(key, shape, cuts, -0.22, 0.18) if cuts else 1.0
    result = jax.random.normal(key, shape, jnp.float32) * scale * loudness
    return jnp.minimum(jnp.maximum(result, -most), most).astype(held_as)


def setup_inputs(seed: int = 0) -> dict:
    seeds = jax.random.split(jax.random.key(seed), 20)
    return {
        "inputs": noise(seeds[0], (TOKENS, D), 1.0, 6.0, ((0, 8),)),
        "loss_sensitivity": noise(seeds[1], (TOKENS, D), 1.0, 6.0, ((0, 8),)),
        "parent_block": draw_parent_block(jax.random.fold_in(seeds[19], 71), 0),
        "adapter_of": jax.random.permutation(seeds[3], ADAPTERS).astype(jnp.int32),
        "w_qkv": noise(seeds[4], (3, D, D), D ** -0.5, 0.125, ((1, 4), (2, 4))),
        "bias_qv": noise(seeds[5], (2, D), 0.5, 3.0, ((1, 4),), jnp.float32),
        "w_o": noise(seeds[6], (D, D), (D // 64) ** -0.5, 1.0, ((0, 4), (1, 4))),
        "exit_offsets": noise(seeds[7], (2, D), 0.5, 3.0, (), jnp.float32),
        "ln_gain": jnp.clip(jax.random.uniform(seeds[8], (2, D), jnp.float32, 0.5, 1.5), 0.5, 1.5),
        "ln_bias": noise(seeds[9], (2, D), 0.3, 2.0, (), jnp.float32),
        "w_in": noise(seeds[10], (D, FF), D ** -0.5, 0.125, ((0, 4), (1, 4))),
        "hidden_offset_frozen": noise(seeds[11], (FF,), 0.5, 3.0, ((0, 4),), jnp.float32),
        "w_out": noise(seeds[12], (FF, D), FF ** -0.5, 0.0625, ((0, 4), (1, 4))),
        "a_attn": noise(seeds[13], (4, ADAPTERS, D, RANK), (D // 4) ** -0.5, 0.25, (), jnp.float32),
        "b_attn": noise(seeds[14], (4, ADAPTERS, RANK, D), RANK ** -0.5, 1.5, (), jnp.float32),
        "a_up": noise(seeds[15], (ADAPTERS, D, RANK), (D // 4) ** -0.5, 0.25, (), jnp.float32),
        "b_up": noise(seeds[16], (ADAPTERS, RANK, FF), RANK ** -0.5, 1.5, ((2, 4),), jnp.float32),
        "a_down": noise(seeds[17], (ADAPTERS, FF, RANK), (FF // 4) ** -0.5, 0.125, ((1, 4),), jnp.float32),
        "b_down": noise(seeds[18], (ADAPTERS, RANK, D), RANK ** -0.5, 1.5, (), jnp.float32),
    }


layer_eps = 1e-05
adaptive_factor = 0.5
neg_fill = -1e+30
highest = lax.Precision.HIGHEST

@jax.custom_vjp
def low(v):
    return lax.optimization_barrier(v.astype(jnp.bfloat16)).astype(jnp.float32)

@jax.custom_vjp
def low_back(v):
    return v

def low_keep(v):
    return (low(v), None)

def low_pass(kept, grad):
    return (grad,)

def back_keep(v):
    return (v, None)

def back_low(kept, grad):
    return (low(grad),)
low.defvjp(low_keep, low_pass)
low_back.defvjp(back_keep, back_low)

def matmul(operand, other):
    return jnp.dot(operand, other, precision=highest)

def layer_norm(vector_rows, gain_row, shift_row):
    centre = vector_rows - lax.optimization_barrier(jnp.mean(vector_rows, axis=-1, keepdims=True))
    spread = lax.optimization_barrier(jnp.mean(centre * centre, axis=-1, keepdims=True))
    return centre * lax.rsqrt(spread + layer_eps) * gain_row + shift_row

def ancestry(parents):
    block_total = parents.shape[0]
    position = jnp.arange(block_total, dtype=jnp.int32)

    def extend(block_step, carry):
        reach, current, root_block = carry
        valid = current >= 0
        reach = reach | valid[:, None] & (position[None, :] == current[:, None])
        root_block = jnp.where(valid, current, root_block)
        upward = jnp.take(parents, jnp.maximum(current, 0).astype(jnp.int32), axis=0)
        current = jnp.where(valid, upward, -1).astype(jnp.int32)
        return (reach, current, root_block)
    start = (jnp.zeros((block_total, block_total), dtype=bool), position, position)
    reach, current, root_block = lax.fori_loop(0, block_total, extend, start)
    root_order = jnp.cumsum((parents < 0).astype(jnp.int32)) - 1
    tree_slot = jnp.take(root_order, root_block.astype(jnp.int32), axis=0).astype(jnp.int32)
    return (reach.astype(jnp.float32), tree_slot)

def adapted(source, down_pair, up_pair, select_tok):
    accumulated_total = jnp.zeros((source.shape[0], up_pair.shape[2]), jnp.float32)
    for slot_index in range(TREES_GROUP):
        down_proj = low(low_back(matmul(source, low(down_pair[slot_index]))))
        accumulated_total = accumulated_total + select_tok[:, slot_index:slot_index + 1] * matmul(down_proj, low(up_pair[slot_index]))
    return adaptive_factor * accumulated_total

def attend(queries, key_vectors, values, ancestors):
    total_rows = queries.shape[0]
    block_rows = math.gcd(512, total_rows)
    score_scale = HD ** (-0.5)
    query_heads = queries.reshape(total_rows, HEADS, HD)
    key_heads = key_vectors.reshape(total_rows, HEADS, HD)
    value_heads = values.reshape(total_rows, HEADS, HD)
    key_pos = jnp.arange(total_rows, dtype=jnp.int32)
    key_block = key_pos // BLOCK

    def one_block(first_row):
        query_rows = lax.dynamic_slice_in_dim(query_heads, first_row, block_rows, 0)
        query_pos = first_row + jnp.arange(block_rows, dtype=jnp.int32)
        query_block = query_pos // BLOCK
        reach_rows = ancestors[query_block]
        allowed = (reach_rows[:, key_block] > 0.5) & ((query_block[:, None] != key_block[None, :]) | (key_pos[None, :] <= query_pos[:, None]))
        scores = low_back(jnp.einsum('qhd,khd->hqk', query_rows, key_heads, precision=highest) * score_scale)
        scores = jnp.where(allowed[None], scores, neg_fill)
        running_max = lax.optimization_barrier(jnp.max(scores, axis=-1, keepdims=True))
        weights = jnp.exp(scores - running_max)
        weights = weights / lax.optimization_barrier(jnp.sum(weights, axis=-1, keepdims=True))
        weights = low(weights)
        return jnp.einsum('hqk,khd->qhd', weights, value_heads, precision=highest)
    starts = jnp.arange(0, total_rows, block_rows, dtype=jnp.int32)
    blocks = lax.map(jax.checkpoint(one_block), starts)
    return blocks.reshape(total_rows, HEADS * HD)

def forward_group(piece_lines, adapters, frozen, ancestors, select_tok, adapter_pair):
    a_attn, b_attn, a_up, b_up, a_down, b_down = adapters
    w_qkv, bias_qv, w_o, exit_offsets, ln_gain, ln_bias, w_in, hidden_offset_frozen, w_out = frozen
    normed = low(layer_norm(piece_lines, ln_gain[0], ln_bias[0]))

    def project(which_linear_map, bias_row):
        accumulated_total = matmul(normed, w_qkv[which_linear_map]) + adapted(normed, a_attn[which_linear_map][adapter_pair], b_attn[which_linear_map][adapter_pair], select_tok)
        return low(low_back(accumulated_total + bias_row))
    queries = project(0, bias_qv[0])
    key_vectors = project(1, 0.0)
    values = project(2, bias_qv[1])
    attended = low(low_back(attend(queries, key_vectors, values, ancestors)))
    branch = low_back(matmul(attended, w_o) + exit_offsets[0] + adapted(attended, a_attn[3][adapter_pair], b_attn[3][adapter_pair], select_tok))
    hidden_state = piece_lines + branch
    normed_two = low(layer_norm(hidden_state, ln_gain[1], ln_bias[1]))
    pre_act = low_back(matmul(normed_two, w_in) + hidden_offset_frozen + adapted(normed_two, a_up[adapter_pair], b_up[adapter_pair], select_tok))
    hidden = low(jax.nn.gelu(pre_act, approximate=False))
    output_branch = low_back(matmul(hidden, w_out) + exit_offsets[1] + adapted(hidden, a_down[adapter_pair], b_down[adapter_pair], select_tok))
    return hidden_state + output_branch

def reference(inputs, loss_sensitivity, parent_block, adapter_of, w_qkv, bias_qv, w_o, exit_offsets, ln_gain, ln_bias, w_in, hidden_offset_frozen, w_out, a_attn, b_attn, a_up, b_up, a_down, b_down):
    frozen = (w_qkv.astype(jnp.float32), bias_qv, w_o.astype(jnp.float32), exit_offsets, ln_gain, ln_bias, w_in.astype(jnp.float32), hidden_offset_frozen, w_out.astype(jnp.float32))
    adapters = (a_attn, b_attn, a_up, b_up, a_down, b_down)
    group_inputs = inputs.astype(jnp.float32).reshape(GROUPS, GROUP_TOKENS, D)
    group_cot = loss_sensitivity.astype(jnp.float32).reshape(GROUPS, GROUP_TOKENS, D)

    def per_group(grad_sums, packed):
        piece_lines, cotangent_rows, parents, group_index = packed
        ancestors, tree_slot = ancestry(parents)
        adapter_pair = lax.dynamic_slice_in_dim(adapter_of, group_index * TREES_GROUP, TREES_GROUP)
        slot_tok = jnp.repeat(tree_slot, BLOCK, total_repeat_length=GROUP_TOKENS)
        select_tok = (slot_tok[:, None] == jnp.arange(TREES_GROUP, dtype=jnp.int32)[None, :]).astype(jnp.float32)

        def forward_fn(token_input, adapter_set):
            return forward_group(token_input, adapter_set, frozen, ancestors, select_tok, adapter_pair)
        returned_value, pullback = jax.vjp(forward_fn, piece_lines, adapters)
        grad_rows, grad_adapters = pullback(cotangent_rows)
        grad_sums = jax.tree.map(jnp.add, grad_sums, grad_adapters)
        return (grad_sums, (returned_value, grad_rows))
    zero_grads = jax.tree.map(jnp.zeros_like, adapters)
    grad_sums, (results, grad_all) = lax.scan(per_group, zero_grads, (group_inputs, group_cot, parent_block, jnp.arange(GROUPS, dtype=jnp.int32)))
    layer_out = results.reshape(TOKENS, D).astype(jnp.bfloat16)
    grad_inputs = grad_all.reshape(TOKENS, D).astype(jnp.bfloat16)
    return (layer_out, grad_inputs, grad_sums[0], grad_sums[1], grad_sums[2], grad_sums[3], grad_sums[4], grad_sums[5])
```

```python
import jax
import jax.numpy as jnp
from jax import lax
from jax.experimental import pallas as pl
from jax.experimental.pallas import tpu as pltpu
from jax.sharding import PartitionSpec as P

HD = 128
RANK = 16
ADAPTERS = 8
SLOTS = 2
PAIR = SLOTS * RANK
BLOCK = 256
AUG = 128

layer_eps = 1e-05
factor = 0.5
neg_fill = -1e30
bf16 = jnp.bfloat16
f32 = jnp.float32

CORE_SWAP = [(0, 1), (1, 0), (2, 3), (3, 2)]
X_SWAP = [(0, 2), (2, 0), (1, 3), (3, 1)]


def dot_nn(a, b):
    return lax.dot_general(a, b, (((1,), (0,)), ((), ())), preferred_element_type=f32)


def dot_nt(a, b):
    return lax.dot_general(a, b, (((1,), (1,)), ((), ())), preferred_element_type=f32)


def dot_tn(a, b):
    return lax.dot_general(a, b, (((0,), (0,)), ((), ())), preferred_element_type=f32)


def round_low(v):
    return lax.reduce_precision(v, 8, 7).astype(bf16)


def standardize(rows):
    centre = rows - jnp.mean(rows, axis=-1, keepdims=True)
    spread = jnp.mean(centre * centre, axis=-1, keepdims=True)
    inverse = lax.rsqrt(spread + layer_eps)
    return centre * inverse, inverse


def norm_back(grad_scaled, unit, inverse):
    first = jnp.mean(grad_scaled, axis=-1, keepdims=True)
    second = jnp.mean(grad_scaled * unit, axis=-1, keepdims=True)
    return inverse * (grad_scaled - first - unit * second)


def ancestry(parents):
    total = parents.shape[0]
    position = jnp.arange(total, dtype=jnp.int32)
    reach = (
        (parents[:, None] == position[None, :]) | (position[:, None] == position[None, :])
    ).astype(f32)
    span = 1
    while span < total:
        reach = jnp.minimum(jnp.sum(reach[:, :, None] * reach[None, :, :], axis=1), 1.0)
        span *= 2
    roots = (parents < 0).astype(f32)
    order = jnp.sum(jnp.where(position[None, :] <= position[:, None], roots[None, :], 0.0), axis=1)
    slot = jnp.sum(reach * (roots * (order - 1.0))[None, :], axis=1)
    return reach, slot


def attend_forward(qkv, far, far_bias, own_bias, heads, scale):
    tokens = qkv.shape[0]
    far_rows = far.shape[0]
    blocks = tokens // BLOCK

    def kernel(q_ref, k_ref, v_ref, fk_ref, fv_ref, fb_ref, ob_ref, o_ref, pf_ref, po_ref):
        far_k = fk_ref[...]
        far_v = fv_ref[...]
        for b in range(blocks):
            rows = slice(b * BLOCK, (b + 1) * BLOCK)
            width = (b + 1) * BLOCK
            q = q_ref[rows, :]
            s_far = dot_nt(q, far_k) * scale + fb_ref[b : b + 1, :]
            s_own = dot_nt(q, k_ref[:width, :]) * scale + ob_ref[b : b + 1, :width]
            q_pos = lax.broadcasted_iota(jnp.int32, (BLOCK, width), 0) + b * BLOCK
            k_pos = lax.broadcasted_iota(jnp.int32, (BLOCK, width), 1)
            s_own = jnp.where(k_pos <= q_pos, s_own, neg_fill)
            top = jnp.maximum(
                jnp.max(s_far, axis=1, keepdims=True), jnp.max(s_own, axis=1, keepdims=True)
            )
            p_far = jnp.exp(s_far - top)
            p_own = jnp.exp(s_own - top)
            total = jnp.sum(p_far, axis=1, keepdims=True) + jnp.sum(p_own, axis=1, keepdims=True)
            inverse = 1.0 / total
            p_far = (p_far * inverse).astype(bf16)
            p_own = (p_own * inverse).astype(bf16)
            pf_ref[0, rows, :] = p_far
            po_ref[0, rows, :width] = p_own
            o_ref[rows, :] = dot_nn(p_far, far_v) + dot_nn(p_own, v_ref[:width, :])

    return pl.pallas_call(
        kernel,
        grid=(heads,),
        in_specs=[
            pl.BlockSpec((tokens, HD), lambda h: (0, h)),
            pl.BlockSpec((tokens, HD), lambda h: (0, heads + h)),
            pl.BlockSpec((tokens, HD), lambda h: (0, 2 * heads + h)),
            pl.BlockSpec((far_rows, HD), lambda h: (0, h)),
            pl.BlockSpec((far_rows, HD), lambda h: (0, heads + h)),
            pl.BlockSpec((blocks, far_rows), lambda h: (0, 0)),
            pl.BlockSpec((blocks, tokens), lambda h: (0, 0)),
        ],
        out_specs=[
            pl.BlockSpec((tokens, HD), lambda h: (0, h)),
            pl.BlockSpec((1, tokens, far_rows), lambda h: (h, 0, 0)),
            pl.BlockSpec((1, tokens, tokens), lambda h: (h, 0, 0)),
        ],
        out_shape=[
            jax.ShapeDtypeStruct((tokens, heads * HD), f32),
            jax.ShapeDtypeStruct((heads, tokens, far_rows), bf16),
            jax.ShapeDtypeStruct((heads, tokens, tokens), bf16),
        ],
        compiler_params=pltpu.CompilerParams(vmem_limit_bytes=56 << 20),
        name="attend_forward",
    )(qkv, qkv, qkv, far, far, far_bias, own_bias)


def attend_backward(qkv, far, grad_attended, attended, probs_far, probs_own, heads, scale):
    tokens = qkv.shape[0]
    far_rows = far.shape[0]
    blocks = tokens // BLOCK

    def kernel(
        q_ref, k_ref, v_ref, fk_ref, fv_ref, g_ref, o_ref, pf_ref, po_ref,
        dq_ref, dk_ref, dv_ref, dfk_ref, dfv_ref,
        dk_acc, dv_acc, dfk_acc, dfv_acc,
    ):
        far_k = fk_ref[...]
        far_v = fv_ref[...]
        for b in reversed(range(blocks)):
            first = b == blocks - 1
            rows = slice(b * BLOCK, (b + 1) * BLOCK)
            width = (b + 1) * BLOCK
            q = q_ref[rows, :]
            g = g_ref[rows, :]
            row_dot = jnp.sum(g.astype(f32) * o_ref[rows, :], axis=1, keepdims=True)
            p_far = pf_ref[0, rows, :]
            p_own = po_ref[0, rows, :width]
            d_far = (p_far.astype(f32) * (dot_nt(g, far_v) - row_dot)).astype(bf16)
            d_own = (p_own.astype(f32) * (dot_nt(g, v_ref[:width, :]) - row_dot)).astype(bf16)
            dq_ref[rows, :] = (
                (dot_nn(d_far, far_k) + dot_nn(d_own, k_ref[:width, :])) * scale
            ).astype(bf16)
            if first:
                dfk_acc[...] = dot_tn(d_far, q)
                dfv_acc[...] = dot_tn(p_far, g)
                dk_acc[...] = dot_tn(d_own, q)
                dv_acc[...] = dot_tn(p_own, g)
            else:
                dfk_acc[...] += dot_tn(d_far, q)
                dfv_acc[...] += dot_tn(p_far, g)
                dk_acc[:width, :] += dot_tn(d_own, q)
                dv_acc[:width, :] += dot_tn(p_own, g)
        dk_ref[...] = (dk_acc[...] * scale).astype(bf16)
        dv_ref[...] = dv_acc[...].astype(bf16)
        dfk_ref[...] = (dfk_acc[...] * scale).astype(bf16)
        dfv_ref[...] = dfv_acc[...].astype(bf16)

    head_spec = pl.BlockSpec((tokens, HD), lambda h: (0, h))
    far_spec = pl.BlockSpec((far_rows, HD), lambda h: (0, h))
    own_shape = jax.ShapeDtypeStruct((tokens, heads * HD), bf16)
    far_shape = jax.ShapeDtypeStruct((far_rows, heads * HD), bf16)
    return pl.pallas_call(
        kernel,
        grid=(heads,),
        in_specs=[
            head_spec,
            pl.BlockSpec((tokens, HD), lambda h: (0, heads + h)),
            pl.BlockSpec((tokens, HD), lambda h: (0, 2 * heads + h)),
            far_spec,
            pl.BlockSpec((far_rows, HD), lambda h: (0, heads + h)),
            head_spec,
            head_spec,
            pl.BlockSpec((1, tokens, far_rows), lambda h: (h, 0, 0)),
            pl.BlockSpec((1, tokens, tokens), lambda h: (h, 0, 0)),
        ],
        out_specs=[head_spec, head_spec, head_spec, far_spec, far_spec],
        out_shape=[own_shape, own_shape, own_shape, far_shape, far_shape],
        scratch_shapes=[
            pltpu.VMEM((tokens, HD), f32),
            pltpu.VMEM((tokens, HD), f32),
            pltpu.VMEM((far_rows, HD), f32),
            pltpu.VMEM((far_rows, HD), f32),
        ],
        compiler_params=pltpu.CompilerParams(vmem_limit_bytes=56 << 20),
        name="attend_backward",
    )(qkv, qkv, qkv, far, far, grad_attended, attended, probs_far, probs_own)


def gate(value, *waits):
    return lax.optimization_barrier((value,) + waits)[0]


def make_body(ctx_size):
    pair_ctx = ctx_size == 2

    def body(
        inputs,
        loss_sensitivity,
        parent_block,
        adapter_of,
        w_qkv,
        bias_qv,
        w_o,
        exit_offsets,
        ln_gain,
        ln_bias,
        w_in,
        hidden_offset_frozen,
        w_out,
        a_attn,
        b_attn,
        a_up,
        b_up,
        a_down,
        b_down,
    ):
        group = lax.axis_index("fsdp")
        context = lax.axis_index("ctx")
        tensor = lax.axis_index("tp")
        core = tensor % 2
        tokens, width = inputs.shape
        half = tokens // 2
        local = w_qkv.shape[2]
        shard = w_qkv.shape[1]
        hidden_local = w_in.shape[1]
        heads = local // HD
        blocks = tokens // BLOCK
        scale = HD ** (-0.5)
        wide = width + AUG

        def on(value, axis, pairs):
            return lax.ppermute(value, axis, pairs)

        def own_rows(matrix):
            return lax.dynamic_slice_in_dim(matrix, core * half, half, 0)

        def other_rows(matrix):
            return lax.dynamic_slice_in_dim(matrix, (1 - core) * half, half, 0)

        def natural(own, other):
            return jnp.concatenate(
                [jnp.where(core == 0, own, other), jnp.where(core == 0, other, own)], axis=0
            )

        def local_lanes(matrix):
            return lax.dynamic_slice_in_dim(matrix, tensor * local, local, matrix.ndim - 1)

        def put(buffer, piece, row, column):
            return lax.dynamic_update_slice(buffer, piece, (row, column))

        swap_y = [(0, 1), (1, 0)]

        def spread_weight(buffer, own, half_axis, row_step, col_step, row_half, col_half, waits):
            size = own.shape[half_axis] // 2
            part = lax.dynamic_slice_in_dim(own, context * size, size, half_axis)
            part = gate(part, *waits) if waits else part
            from_two = on(part, "fsdp", [(0, 2), (2, 0), (1, 3), (3, 1)])
            from_one = on(part, "fsdp", [(0, 1), (1, 0), (2, 3), (3, 2)])
            middle = on(part, "fsdp", [(1, 2), (2, 1)])
            ends = on(from_two, "fsdp", [(2, 3), (1, 0)])
            y_one = on(from_one, "ctx", swap_y)
            y_two = on(from_two, "ctx", swap_y)
            both = ("fsdp", "ctx")
            y_middle = on(middle, both, [(2, 3), (3, 2), (4, 5), (5, 4)])
            y_ends = on(ends, both, [(0, 1), (1, 0), (6, 7), (7, 6)])
            inner = (group == 1) | (group == 2)
            buffer = put(buffer, own, group * row_step, group * col_step)

            def both_halves(buffer, piece, other, source):
                row = source * row_step
                col = source * col_step
                buffer = put(buffer, piece, row + context * row_half, col + context * col_half)
                return put(
                    buffer,
                    other,
                    row + (1 - context) * row_half,
                    col + (1 - context) * col_half,
                )

            buffer = both_halves(buffer, from_one, y_one, group ^ 1)
            buffer = both_halves(buffer, from_two, y_two, group ^ 2)
            buffer = both_halves(
                buffer,
                jnp.where(inner, middle, ends),
                jnp.where(inner, y_middle, y_ends),
                group ^ 3,
            )
            return buffer, (from_one, from_two)

        def sum_tp(other_low, own_full):
            got = on(other_low, "tp", CORE_SWAP)
            mine = round_low(own_full + got.astype(f32))
            far = on(mine, "tp", X_SWAP)
            return mine.astype(f32) + far.astype(f32)

        pair = lax.dynamic_slice_in_dim(adapter_of, group * SLOTS, SLOTS)

        def pick_pair(array, axis):
            return jnp.concatenate(
                [lax.dynamic_slice_in_dim(array, pair[s], 1, axis) for s in range(SLOTS)], axis
            )

        a_pair = jnp.swapaxes(pick_pair(a_attn, 1), 2, 3)
        a_qkv_rows = a_pair[:3].reshape(3 * PAIR, width).astype(bf16)
        a_o_rows = local_lanes(a_pair[3].reshape(PAIR, width)).astype(bf16)
        b_pair = pick_pair(b_attn, 1)
        b_qkv_rows = local_lanes(b_pair[:3]).reshape(3, PAIR, local).astype(bf16)
        b_o_rows = b_pair[3].reshape(PAIR, width).astype(bf16)
        a_up_rows = jnp.swapaxes(pick_pair(a_up, 0), 1, 2).reshape(PAIR, width).astype(bf16)
        b_up_rows = pick_pair(b_up, 0).reshape(PAIR, hidden_local).astype(bf16)
        a_down_rows = (
            jnp.swapaxes(pick_pair(a_down, 0), 1, 2).reshape(PAIR, hidden_local).astype(bf16)
        )
        b_down_rows = pick_pair(b_down, 0).reshape(PAIR, width).astype(bf16)

        q_aug = jnp.concatenate(
            [jnp.pad(b_qkv_rows[i], ((0, 0), (i * local, (2 - i) * local))) for i in range(3)]
            + [jnp.zeros((AUG - 3 * PAIR, 3 * local), bf16)],
            axis=0,
        )
        q_start = jnp.concatenate([jnp.zeros((width, 3 * local), bf16), q_aug], axis=0)
        o_aug = jnp.pad(a_o_rows.T, ((0, 0), (0, AUG - PAIR)))
        o_start = jnp.concatenate([jnp.zeros((local, width), bf16), o_aug], axis=1)
        in_aug = jnp.pad(b_up_rows, ((0, AUG - PAIR), (0, 0)))
        in_start = jnp.concatenate([jnp.zeros((width, hidden_local), bf16), in_aug], axis=0)
        out_aug = jnp.pad(a_down_rows.T, ((0, 0), (0, AUG - PAIR)))
        out_start = jnp.concatenate([jnp.zeros((hidden_local, width), bf16), out_aug], axis=1)
        own_q = jnp.transpose(w_qkv, (1, 0, 2)).reshape(shard, 3 * local)
        if pair_ctx:
            quarter = tokens // 4
            sent = lax.dynamic_slice_in_dim(inputs, tensor * quarter, quarter, 0)
            far_quarter = on(sent, "ctx", [(0, 1)])
            far_x = on(far_quarter, "tp", X_SWAP)
            far_core = on(far_quarter, "tp", CORE_SWAP)
            far_both = on(far_x, "tp", CORE_SWAP)
            far_inputs = jnp.zeros((tokens, width), bf16)
            for piece, place in (
                (far_quarter, tensor),
                (far_x, tensor ^ 2),
                (far_core, tensor ^ 1),
                (far_both, tensor ^ 3),
            ):
                far_inputs = put(far_inputs, piece, place * quarter, 0)
            q_full, q_done = spread_weight(q_start, own_q, 0, shard, 0, shard // 2, 0, ())
            o_full, o_done = spread_weight(o_start, w_o, 0, 0, shard, local // 2, 0, q_done)
            in_full, in_done = spread_weight(in_start, w_in, 0, shard, 0, shard // 2, 0, o_done)
            out_full, _ = spread_weight(out_start, w_out, 0, 0, shard, hidden_local // 2, 0, in_done)
        else:
            q_full = put(q_start, lax.all_gather(own_q, "fsdp", axis=0, tiled=True), 0, 0)
            o_full = put(o_start, lax.all_gather(w_o, "fsdp", axis=1, tiled=True), 0, 0)
            in_full = put(in_start, lax.all_gather(w_in, "fsdp", axis=0, tiled=True), 0, 0)
            out_full = put(out_start, lax.all_gather(w_out, "fsdp", axis=1, tiled=True), 0, 0)

        reach, slot = ancestry(parent_block[0])
        all_blocks = reach.shape[0]
        first_block = context * blocks
        far_blocks = blocks if pair_ctx else all_blocks
        reach_rows = lax.dynamic_slice_in_dim(reach, first_block, blocks, 0)
        block_ids = jnp.arange(far_blocks, dtype=jnp.int32)
        far_open = (reach_rows[:, :far_blocks] > 0.5) & (block_ids[None, :] < first_block)
        own_open = lax.dynamic_slice_in_dim(reach_rows, first_block, blocks, 1) > 0.5
        far_bias = jnp.repeat(jnp.where(far_open, 0.0, neg_fill).astype(f32), BLOCK, axis=1)
        own_bias = jnp.repeat(jnp.where(own_open, 0.0, neg_fill).astype(f32), BLOCK, axis=1)

        def picks(slots):
            select = (slots[:, None] == jnp.arange(SLOTS, dtype=f32)[None, :]).astype(f32)
            return jnp.repeat(jnp.repeat(select, RANK, axis=1), BLOCK, axis=0)

        pick = picks(lax.dynamic_slice_in_dim(slot, first_block, blocks))
        pick_own = own_rows(pick)

        gain_one, shift_one = ln_gain[0][None, :], ln_bias[0][None, :]
        gain_two, shift_two = ln_gain[1][None, :], ln_bias[1][None, :]

        def widen(low, *extra):
            spare = AUG - sum(e.shape[1] for e in extra)
            tail = [jnp.zeros((low.shape[0], spare), bf16)] if spare else []
            return jnp.concatenate([low, *extra, *tail], axis=1)

        def first_norm(rows, pick_rows):
            low = (standardize(rows.astype(f32))[0] * gain_one + shift_one).astype(bf16)
            reduced = (dot_nt(low, a_qkv_rows) * jnp.tile(pick_rows, (1, 3))).astype(bf16)
            return low, widen(low, factor * reduced)

        normed, normed_wide = first_norm(inputs, pick)
        zero_bias = jnp.zeros((local,), f32)
        q_bias = jnp.concatenate([bias_qv[0], zero_bias, bias_qv[1]])[None, :]
        qkv = (dot_nn(normed_wide, q_full) + q_bias).astype(bf16)
        if pair_ctx:
            _, far_wide = first_norm(far_inputs, picks(slot[:blocks]))
            far_kv = (dot_nn(far_wide, q_full[:, local:]) + q_bias[:, local:]).astype(bf16)
        else:
            far_kv = lax.all_gather(qkv[:, local:], "ctx", axis=0, tiled=True)

        attended_f, probs_far, probs_own = attend_forward(
            qkv, far_kv, far_bias, own_bias, heads, scale
        )
        attended = attended_f.astype(bf16)
        attended_own = own_rows(attended)
        attended_other = other_rows(attended)
        branch = sum_tp(
            dot_nn(attended_other, o_full).astype(bf16), dot_nn(attended_own, o_full)
        )
        down_o = factor * (branch[:, width : width + PAIR] * pick_own).astype(bf16)
        middle = (
            own_rows(inputs).astype(f32)
            + branch[:, :width]
            + exit_offsets[0][None, :]
            + dot_nn(down_o, b_o_rows)
        )
        unit_two, inverse_two = standardize(middle)
        normed_two = (unit_two * gain_two + shift_two).astype(bf16)
        down_up = factor * (dot_nt(normed_two, a_up_rows) * pick_own).astype(bf16)
        two_own = widen(normed_two, down_up, down_o)
        two_other = on(two_own, "tp", CORE_SWAP)
        two_wide = jnp.concatenate([two_own, two_other], axis=0)

        pre_act = dot_nn(two_wide, in_full) + hidden_offset_frozen[None, :]
        phi = 0.5 * (1.0 + lax.erf(pre_act * (2.0 ** -0.5)))
        hidden = (pre_act * phi).astype(bf16)
        slope = (
            phi + pre_act * jnp.exp(-0.5 * pre_act * pre_act) * (0.5 / jnp.pi) ** 0.5
        ).astype(bf16)

        loss_own = own_rows(loss_sensitivity)
        loss_rel = jnp.concatenate([loss_own, other_rows(loss_sensitivity)], axis=0)
        pick_rel = jnp.concatenate([pick_own, other_rows(pick)], axis=0)
        grad_down_down = (factor * dot_nt(loss_rel, b_down_rows) * pick_rel).astype(bf16)
        loss_wide = widen(loss_rel, grad_down_down)
        grad_pre = (dot_nt(loss_wide, out_full) * slope.astype(f32)).astype(bf16)
        grad_two = sum_tp(
            dot_nt(grad_pre[half:], in_full).astype(bf16), dot_nt(grad_pre[:half], in_full)
        )
        grad_down_up = (factor * grad_two[:, width : width + PAIR] * pick_own).astype(bf16)
        grad_normed_two = grad_two[:, :width] + dot_nn(grad_down_up, a_up_rows)
        grad_middle = loss_own.astype(f32) + norm_back(
            grad_normed_two * gain_two, unit_two, inverse_two
        )
        grad_branch = grad_middle.astype(bf16)
        grad_down_o = (factor * dot_nt(grad_branch, b_o_rows) * pick_own).astype(bf16)
        back_own = widen(grad_branch, grad_down_o, grad_down_up)
        back_other = on(back_own, "tp", CORE_SWAP)
        grad_attended = natural(
            dot_nt(back_own, o_full).astype(bf16), dot_nt(back_other, o_full).astype(bf16)
        )

        exit_part = sum_tp(
            dot_nn(hidden[half:], out_full).astype(bf16), dot_nn(hidden[:half], out_full)
        )
        down_down = factor * (exit_part[:, width : width + PAIR] * pick_own).astype(bf16)
        layer_own = (
            middle
            + exit_part[:, :width]
            + exit_offsets[1][None, :]
            + dot_nn(down_down, b_down_rows)
        ).astype(bf16)
        layer_wide = widen(layer_own, down_down)
        layer_other = on(layer_wide, "tp", CORE_SWAP)
        layer_out = natural(layer_own, layer_other[:, :width])
        down_down_rel = jnp.concatenate([down_down, layer_other[:, width : width + PAIR]], axis=0)

        grad_q, grad_k, grad_v, far_grad_k, far_grad_v = attend_backward(
            qkv, far_kv, grad_attended, attended_f, probs_far, probs_own, heads, scale
        )
        if pair_ctx:
            more_k = on(far_grad_k, "ctx", [(1, 0)])
            more_v = on(far_grad_v, "ctx", [(1, 0)])
        else:
            more_k = lax.psum_scatter(far_grad_k, "ctx", scatter_dimension=0, tiled=True)
            more_v = lax.psum_scatter(far_grad_v, "ctx", scatter_dimension=0, tiled=True)
        grad_qkv = jnp.concatenate(
            [
                grad_q,
                (grad_k.astype(f32) + more_k.astype(f32)).astype(bf16),
                (grad_v.astype(f32) + more_v.astype(f32)).astype(bf16),
            ],
            axis=1,
        )
        grad_one = sum_tp(
            dot_nt(other_rows(grad_qkv), q_full).astype(bf16), dot_nt(own_rows(grad_qkv), q_full)
        )
        grad_down_qkv = (
            factor * grad_one[:, width : width + 3 * PAIR] * jnp.tile(pick_own, (1, 3))
        ).astype(bf16)
        other_down_qkv = on(grad_down_qkv, "tp", CORE_SWAP)
        grad_normed = grad_one[:, :width] + dot_nn(grad_down_qkv, a_qkv_rows)
        unit_one, inverse_one = standardize(own_rows(inputs).astype(f32))
        grad_own = (
            grad_middle + norm_back(grad_normed * gain_one, unit_one, inverse_one)
        ).astype(bf16)
        grad_other = on(grad_own, "tp", CORE_SWAP)
        grad_inputs = natural(grad_own, grad_other)

        attended_rel = jnp.concatenate([attended_own, attended_other], axis=0)
        back_rel = jnp.concatenate([back_own, back_other], axis=0)
        term_a_o = dot_tn(back_rel[:, width : width + PAIR], attended_rel)
        term_b_o = dot_tn(two_wide[:, width + PAIR : width + 2 * PAIR], local_lanes(back_rel[:, :width]))
        term_a_up = dot_tn(
            back_rel[:, width + PAIR : width + 2 * PAIR], local_lanes(two_wide[:, :width])
        )
        term_b_up = dot_tn(two_wide[:, width : width + PAIR], grad_pre)
        term_a_down = dot_tn(grad_down_down, hidden)
        term_b_down = dot_tn(down_down_rel, local_lanes(loss_rel))
        reduced_qkv = normed_wide[:, width : width + 3 * PAIR]
        term_b_qkv = [
            dot_tn(
                reduced_qkv[:, i * PAIR : (i + 1) * PAIR],
                grad_qkv[:, i * local : (i + 1) * local],
            )
            for i in range(3)
        ]
        natural_down = natural(grad_down_qkv, other_down_qkv)
        term_a_qkv = dot_tn(natural_down, local_lanes(normed))

        holder = jnp.stack([group ^ k for k in range(4)])
        owner = adapter_of.reshape(4, SLOTS)[holder].reshape(4 * SLOTS)
        place = (jnp.arange(ADAPTERS, dtype=jnp.int32)[:, None] == owner[None, :]).astype(f32)

        def deliver(terms):
            lanes = []
            for term in terms:
                cut = term.shape[1] // 4
                lanes.append(term.astype(bf16).reshape(term.shape[0], 4, cut // AUG, AUG))
            received = []
            for k in range(4):
                target = group ^ k
                piece = jnp.concatenate(
                    [
                        lax.dynamic_slice_in_dim(lane, target, 1, 1).reshape(-1, AUG)
                        for lane in lanes
                    ],
                    axis=0,
                )
                if k:
                    piece = on(piece, "fsdp", [(i, i ^ k) for i in range(4)])
                received.append(piece)
            stacked = jnp.stack(received)
            if pair_ctx:
                stacked = stacked.astype(f32) + on(stacked, "ctx", swap_y).astype(f32)
            else:
                stacked = lax.psum(stacked.astype(f32), "ctx")
            results = []
            start = 0
            for lane in lanes:
                rows, _, tiles, _ = lane.shape
                items = rows // PAIR
                count = rows * tiles
                part = stacked[:, start : start + count].reshape(
                    4, items, SLOTS, RANK, tiles * AUG
                )
                start += count
                part = jnp.transpose(part, (0, 2, 1, 3, 4)).reshape(
                    4 * SLOTS, items, RANK, tiles * AUG
                )
                spread = jnp.sum(place[:, :, None, None, None] * part[None], axis=1)
                size = tiles * AUG // ctx_size
                results.append(
                    jnp.swapaxes(
                        lax.dynamic_slice_in_dim(spread, context * size, size, 3), 0, 1
                    )
                )
            return results

        out_a_o, out_b_o, out_a_up, out_b_down, out_b_up, out_a_down = deliver(
            [term_a_o, term_b_o, term_a_up, term_b_down, term_b_up, term_a_down]
        )
        (out_b_qkv,) = deliver([jnp.concatenate(term_b_qkv, axis=0)])
        (out_a_qkv,) = deliver([term_a_qkv])
        grad_a_attn = jnp.swapaxes(jnp.concatenate([out_a_qkv, out_a_o], axis=0), 2, 3)
        grad_b_attn = jnp.concatenate([out_b_qkv, out_b_o], axis=0)
        return (
            layer_out,
            grad_inputs,
            grad_a_attn,
            grad_b_attn,
            jnp.swapaxes(out_a_up[0], 1, 2),
            out_b_up[0],
            jnp.swapaxes(out_a_down[0], 1, 2),
            out_b_down[0],
        )

    return body


def solution(mesh):
    in_specs = (
        P(("fsdp", "ctx"), None),
        P(("fsdp", "ctx"), None),
        P("fsdp", None),
        P(),
        P(None, "fsdp", "tp"),
        P(None, "tp"),
        P("tp", "fsdp"),
        P(),
        P(),
        P(),
        P("fsdp", "tp"),
        P("tp"),
        P("tp", "fsdp"),
        P(),
        P(),
        P(),
        P(None, None, "tp"),
        P(None, "tp", None),
        P(),
    )
    out_specs = (
        P(("fsdp", "ctx"), None),
        P(("fsdp", "ctx"), None),
        P(None, None, ("tp", "fsdp", "ctx"), None),
        P(None, None, None, ("tp", "fsdp", "ctx")),
        P(None, ("tp", "fsdp", "ctx"), None),
        P(None, None, ("tp", "fsdp", "ctx")),
        P(None, ("tp", "fsdp", "ctx"), None),
        P(None, None, ("tp", "fsdp", "ctx")),
    )
    return jax.shard_map(
        make_body(mesh.shape["ctx"]),
        mesh=mesh,
        in_specs=in_specs,
        out_specs=out_specs,
        check_vma=False,
    )
```

```python
import jax
import jax.numpy as jnp
from jax import lax
from jax.experimental import pallas as pl
from jax.experimental.pallas import tpu as pltpu
from jax.sharding import PartitionSpec as P

HD = 128
RANK = 16
ADAPTERS = 8
SLOTS = 2
PAIR = SLOTS * RANK
BLOCK = 256
AUG = 128
ROW_CHUNK = 128

layer_eps = 1e-05
factor = 0.5
neg_fill = -1e30
bf16 = jnp.bfloat16
f32 = jnp.float32

CORE_SWAP = [(0, 1), (1, 0), (2, 3), (3, 2)]
X_SWAP = [(0, 2), (2, 0), (1, 3), (3, 1)]


def dot_nn(a, b):
    return lax.dot_general(a, b, (((1,), (0,)), ((), ())), preferred_element_type=f32)


def dot_nt(a, b):
    return lax.dot_general(a, b, (((1,), (1,)), ((), ())), preferred_element_type=f32)


def dot_tn(a, b):
    return lax.dot_general(a, b, (((0,), (0,)), ((), ())), preferred_element_type=f32)


def round_low(v):
    return lax.reduce_precision(v, 8, 7).astype(bf16)


def standardize(rows):
    centre = rows - jnp.mean(rows, axis=-1, keepdims=True)
    spread = jnp.mean(centre * centre, axis=-1, keepdims=True)
    inverse = lax.rsqrt(spread + layer_eps)
    return centre * inverse, inverse


def norm_back(grad_scaled, unit, inverse):
    first = jnp.mean(grad_scaled, axis=-1, keepdims=True)
    second = jnp.mean(grad_scaled * unit, axis=-1, keepdims=True)
    return inverse * (grad_scaled - first - unit * second)


def ancestry(parents):
    total = parents.shape[0]
    position = jnp.arange(total, dtype=jnp.int32)
    reach = (
        (parents[:, None] == position[None, :]) | (position[:, None] == position[None, :])
    ).astype(f32)
    span = 1
    while span < total:
        reach = jnp.minimum(jnp.sum(reach[:, :, None] * reach[None, :, :], axis=1), 1.0)
        span *= 2
    roots = (parents < 0).astype(f32)
    order = jnp.sum(jnp.where(position[None, :] <= position[:, None], roots[None, :], 0.0), axis=1)
    slot = jnp.sum(reach * (roots * (order - 1.0))[None, :], axis=1)
    return reach, slot


def attend_forward(qkv, far, far_bias, own_bias, heads, scale):
    tokens = qkv.shape[0]
    far_rows = far.shape[0]
    blocks = tokens // BLOCK

    def kernel(q_ref, k_ref, v_ref, fk_ref, fv_ref, fb_ref, ob_ref, o_ref, pf_ref, po_ref):
        far_k = fk_ref[...]
        far_v = fv_ref[...]
        for b in range(blocks):
            rows = slice(b * BLOCK, (b + 1) * BLOCK)
            width = (b + 1) * BLOCK
            q = q_ref[rows, :]
            s_far = dot_nt(q, far_k) * scale + fb_ref[b : b + 1, :]
            s_own = dot_nt(q, k_ref[:width, :]) * scale + ob_ref[b : b + 1, :width]
            q_pos = lax.broadcasted_iota(jnp.int32, (BLOCK, width), 0) + b * BLOCK
            k_pos = lax.broadcasted_iota(jnp.int32, (BLOCK, width), 1)
            s_own = jnp.where(k_pos <= q_pos, s_own, neg_fill)
            top = jnp.maximum(
                jnp.max(s_far, axis=1, keepdims=True), jnp.max(s_own, axis=1, keepdims=True)
            )
            p_far = jnp.exp(s_far - top)
            p_own = jnp.exp(s_own - top)
            total = jnp.sum(p_far, axis=1, keepdims=True) + jnp.sum(p_own, axis=1, keepdims=True)
            inverse = 1.0 / total
            p_far = (p_far * inverse).astype(bf16)
            p_own = (p_own * inverse).astype(bf16)
            pf_ref[0, rows, :] = p_far
            po_ref[0, rows, :width] = p_own
            o_ref[rows, :] = dot_nn(p_far, far_v) + dot_nn(p_own, v_ref[:width, :])

    return pl.pallas_call(
        kernel,
        grid=(heads,),
        in_specs=[
            pl.BlockSpec((tokens, HD), lambda h: (0, h)),
            pl.BlockSpec((tokens, HD), lambda h: (0, heads + h)),
            pl.BlockSpec((tokens, HD), lambda h: (0, 2 * heads + h)),
            pl.BlockSpec((far_rows, HD), lambda h: (0, h)),
            pl.BlockSpec((far_rows, HD), lambda h: (0, heads + h)),
            pl.BlockSpec((blocks, far_rows), lambda h: (0, 0)),
            pl.BlockSpec((blocks, tokens), lambda h: (0, 0)),
        ],
        out_specs=[
            pl.BlockSpec((tokens, HD), lambda h: (0, h)),
            pl.BlockSpec((1, tokens, far_rows), lambda h: (h, 0, 0)),
            pl.BlockSpec((1, tokens, tokens), lambda h: (h, 0, 0)),
        ],
        out_shape=[
            jax.ShapeDtypeStruct((tokens, heads * HD), f32),
            jax.ShapeDtypeStruct((heads, tokens, far_rows), bf16),
            jax.ShapeDtypeStruct((heads, tokens, tokens), bf16),
        ],
        compiler_params=pltpu.CompilerParams(vmem_limit_bytes=56 << 20),
        name="attend_forward",
    )(qkv, qkv, qkv, far, far, far_bias, own_bias)


def attend_backward(qkv, far, grad_attended, attended, probs_far, probs_own, heads, scale):
    tokens = qkv.shape[0]
    far_rows = far.shape[0]
    blocks = tokens // BLOCK

    def kernel(
        q_ref, k_ref, v_ref, fk_ref, fv_ref, g_ref, o_ref, pf_ref, po_ref,
        dq_ref, dk_ref, dv_ref, dfk_ref, dfv_ref,
        dk_acc, dv_acc, dfk_acc, dfv_acc,
    ):
        far_k = fk_ref[...]
        far_v = fv_ref[...]
        for b in reversed(range(blocks)):
            first = b == blocks - 1
            rows = slice(b * BLOCK, (b + 1) * BLOCK)
            width = (b + 1) * BLOCK
            q = q_ref[rows, :]
            g = g_ref[rows, :]
            row_dot = jnp.sum(g.astype(f32) * o_ref[rows, :], axis=1, keepdims=True)
            p_far = pf_ref[0, rows, :]
            p_own = po_ref[0, rows, :width]
            d_far = (p_far.astype(f32) * (dot_nt(g, far_v) - row_dot)).astype(bf16)
            d_own = (p_own.astype(f32) * (dot_nt(g, v_ref[:width, :]) - row_dot)).astype(bf16)
            dq_ref[rows, :] = (
                (dot_nn(d_far, far_k) + dot_nn(d_own, k_ref[:width, :])) * scale
            ).astype(bf16)
            if first:
                dfk_acc[...] = dot_tn(d_far, q)
                dfv_acc[...] = dot_tn(p_far, g)
                dk_acc[...] = dot_tn(d_own, q)
                dv_acc[...] = dot_tn(p_own, g)
            else:
                dfk_acc[...] += dot_tn(d_far, q)
                dfv_acc[...] += dot_tn(p_far, g)
                dk_acc[:width, :] += dot_tn(d_own, q)
                dv_acc[:width, :] += dot_tn(p_own, g)
        dk_ref[...] = (dk_acc[...] * scale).astype(bf16)
        dv_ref[...] = dv_acc[...].astype(bf16)
        dfk_ref[...] = (dfk_acc[...] * scale).astype(bf16)
        dfv_ref[...] = dfv_acc[...].astype(bf16)

    head_spec = pl.BlockSpec((tokens, HD), lambda h: (0, h))
    far_spec = pl.BlockSpec((far_rows, HD), lambda h: (0, h))
    own_shape = jax.ShapeDtypeStruct((tokens, heads * HD), bf16)
    far_shape = jax.ShapeDtypeStruct((far_rows, heads * HD), bf16)
    return pl.pallas_call(
        kernel,
        grid=(heads,),
        in_specs=[
            head_spec,
            pl.BlockSpec((tokens, HD), lambda h: (0, heads + h)),
            pl.BlockSpec((tokens, HD), lambda h: (0, 2 * heads + h)),
            far_spec,
            pl.BlockSpec((far_rows, HD), lambda h: (0, heads + h)),
            head_spec,
            head_spec,
            pl.BlockSpec((1, tokens, far_rows), lambda h: (h, 0, 0)),
            pl.BlockSpec((1, tokens, tokens), lambda h: (h, 0, 0)),
        ],
        out_specs=[head_spec, head_spec, head_spec, far_spec, far_spec],
        out_shape=[own_shape, own_shape, own_shape, far_shape, far_shape],
        scratch_shapes=[
            pltpu.VMEM((tokens, HD), f32),
            pltpu.VMEM((tokens, HD), f32),
            pltpu.VMEM((far_rows, HD), f32),
            pltpu.VMEM((far_rows, HD), f32),
        ],
        compiler_params=pltpu.CompilerParams(vmem_limit_bytes=56 << 20),
        name="attend_backward",
    )(qkv, qkv, qkv, far, far, grad_attended, attended, probs_far, probs_own)


def assemble(spot, pieces, tail, rows, columns, step, parts):
    direction, shard, half_rows = step
    count = max(parts, 1)
    part_columns = columns // count if parts else columns
    tail_rows, tail_columns = tail.shape

    def kernel(spot_ref, *refs):
        own, one, y_one = refs[:3]
        in_two, y_in_two, out_two, y_out_two, in_far, y_in_far, out_far, y_out_far = refs[3:11]
        tail_ref, out, sem = refs[11:]
        group = spot_ref[0]
        context = spot_ref[1]
        inner = (group == 1) | (group == 2)

        def moves(piece, source, which, first):
            made = []
            for i in range(count):
                src = piece.at[i] if parts else piece
                n, m = src.shape
                if direction == "rows":
                    row = pl.multiple_of(source * shard + which * half_rows, half_rows)
                    dst = out.at[pl.ds(row, n), pl.ds(i * part_columns, m)]
                else:
                    row = pl.multiple_of(which * half_rows, half_rows)
                    col = pl.multiple_of(source * shard, shard)
                    dst = out.at[pl.ds(row, n), pl.ds(col, m)]
                made.append(pltpu.make_async_copy(src, dst, sem.at[first + i]))
            return made

        fixed = moves(own, group, 0, 0)
        fixed += moves(one, group ^ 1, context, count)
        fixed += moves(y_one, group ^ 1, 1 - context, 2 * count)
        row0 = rows - tail_rows if direction == "rows" else 0
        col0 = 0 if direction == "rows" else columns - tail_columns
        fixed.append(
            pltpu.make_async_copy(
                tail_ref,
                out.at[pl.ds(row0, tail_rows), pl.ds(col0, tail_columns)],
                sem.at[7 * count],
            )
        )
        inside = moves(in_two, group ^ 2, context, 3 * count)
        inside += moves(y_in_two, group ^ 2, 1 - context, 4 * count)
        inside += moves(in_far, group ^ 3, context, 5 * count)
        inside += moves(y_in_far, group ^ 3, 1 - context, 6 * count)
        outside = moves(out_two, group ^ 2, context, 3 * count)
        outside += moves(y_out_two, group ^ 2, 1 - context, 4 * count)
        outside += moves(out_far, group ^ 3, context, 5 * count)
        outside += moves(y_out_far, group ^ 3, 1 - context, 6 * count)
        for move in fixed:
            move.start()

        @pl.when(inner)
        def _():
            for move in inside:
                move.start()
            for move in inside:
                move.wait()

        @pl.when(jnp.logical_not(inner))
        def _():
            for move in outside:
                move.start()
            for move in outside:
                move.wait()

        for move in fixed:
            move.wait()

    return pl.pallas_call(
        kernel,
        grid_spec=pltpu.PrefetchScalarGridSpec(
            num_scalar_prefetch=1,
            grid=(),
            in_specs=[pl.BlockSpec(memory_space=pl.ANY)] * 12,
            out_specs=pl.BlockSpec(memory_space=pltpu.VMEM),
            scratch_shapes=[pltpu.SemaphoreType.DMA((7 * count + 1,))],
        ),
        out_shape=jax.ShapeDtypeStruct((rows, columns), bf16),
        compiler_params=pltpu.CompilerParams(vmem_limit_bytes=24 << 20),
        name="assemble",
    )(spot, *pieces, tail)


def assemble_gathered(spot, own, gathered, swapped, tail, rows, columns, direction):
    shard_rows, shard_columns = own.shape
    shard = shard_rows if direction == "rows" else shard_columns
    half = shard_rows // 2
    chunks = len(gathered)
    size = half // chunks
    tail_rows, tail_columns = tail.shape
    copies = 7 * chunks + 2

    def kernel(spot_ref, *refs):
        own_ref = refs[0]
        near = refs[1 : 1 + chunks]
        cross = refs[1 + chunks : 1 + 2 * chunks]
        tail_ref, out, sem = refs[1 + 2 * chunks :]
        group = spot_ref[0]
        context = spot_ref[1]
        moves = []

        def move(src, source, which, chunk_row):
            count, width = src.shape
            row = which * half + chunk_row
            if direction == "rows":
                dst = out.at[
                    pl.ds(pl.multiple_of(source * shard + row, size), count), pl.ds(0, width)
                ]
            else:
                dst = out.at[
                    pl.ds(pl.multiple_of(row, size), count),
                    pl.ds(pl.multiple_of(source * shard, shard), width),
                ]
            moves.append(pltpu.make_async_copy(src, dst, sem.at[len(moves)]))

        for j in range(chunks):
            for g in range(4):
                move(near[j].at[pl.ds(g * size, size)], g, context, j * size)
            for i in range(3):
                move(
                    cross[j].at[pl.ds(i * size, size)], group ^ (i + 1), 1 - context, j * size
                )
        move(
            own_ref.at[pl.ds(pl.multiple_of((1 - context) * half, half), half)],
            group,
            1 - context,
            0,
        )
        row0 = rows - tail_rows if direction == "rows" else 0
        col0 = 0 if direction == "rows" else columns - tail_columns
        moves.append(
            pltpu.make_async_copy(
                tail_ref,
                out.at[pl.ds(row0, tail_rows), pl.ds(col0, tail_columns)],
                sem.at[len(moves)],
            )
        )
        for m in moves:
            m.start()
        for m in moves:
            m.wait()

    return pl.pallas_call(
        kernel,
        grid_spec=pltpu.PrefetchScalarGridSpec(
            num_scalar_prefetch=1,
            grid=(),
            in_specs=[pl.BlockSpec(memory_space=pl.ANY)] * (2 + 2 * chunks),
            out_specs=pl.BlockSpec(memory_space=pltpu.VMEM),
            scratch_shapes=[pltpu.SemaphoreType.DMA((copies,))],
        ),
        out_shape=jax.ShapeDtypeStruct((rows, columns), bf16),
        compiler_params=pltpu.CompilerParams(vmem_limit_bytes=24 << 20),
        name="assemble_gathered",
    )(spot, own, *gathered, *swapped, tail)


def norm_wide(pieces, places, slots, down_rows, gain, shift, tokens):
    width = gain.shape[1]
    blocks = tokens // BLOCK
    count = len(pieces)
    quarter = tokens // 4
    steps = 4 // count

    def kernel(place_ref, slot_ref, *refs):
        down_ref, gain_ref, shift_ref, out_ref = refs[count:]
        for i in range(4):
            x_ref = refs[i // steps]
            first = (i % steps) * quarter
            rows = x_ref[first : first + quarter, :].astype(f32)
            start = pl.multiple_of(place_ref[i] * quarter, quarter)
            unit, _ = standardize(rows)
            low = (unit * gain_ref[...] + shift_ref[...]).astype(bf16)
            block = (lax.broadcasted_iota(jnp.int32, (quarter, AUG), 0) + start) // BLOCK
            lane_slot = (lax.broadcasted_iota(jnp.int32, (quarter, AUG), 1) // RANK) % SLOTS
            slot = jnp.zeros((quarter, AUG), jnp.int32)
            for b in range(blocks):
                slot = jnp.where(block == b, slot_ref[b], slot)
            down = jnp.where(slot == lane_slot, dot_nt(low, down_ref[...]), 0.0)
            out_ref[pl.ds(start, quarter), :width] = low
            out_ref[pl.ds(start, quarter), width:] = factor * down.astype(bf16)

    whole = pl.BlockSpec(memory_space=pltpu.VMEM)
    return pl.pallas_call(
        kernel,
        grid_spec=pltpu.PrefetchScalarGridSpec(
            num_scalar_prefetch=2,
            grid=(),
            in_specs=[whole] * (count + 3),
            out_specs=whole,
        ),
        out_shape=jax.ShapeDtypeStruct((tokens, width + AUG), bf16),
        compiler_params=pltpu.CompilerParams(vmem_limit_bytes=32 << 20),
        name="norm_wide",
    )(places, slots, *pieces, down_rows, gain, shift)


def own_pick(first_row, count, slot_ref, blocks):
    block = (lax.broadcasted_iota(jnp.int32, (count, AUG), 0) + first_row) // BLOCK
    lane_slot = (lax.broadcasted_iota(jnp.int32, (count, AUG), 1) // RANK) % SLOTS
    slot = jnp.zeros((count, AUG), jnp.int32)
    for b in range(blocks):
        slot = jnp.where(block == b, slot_ref[b], slot)
    return slot == lane_slot


def row_call(body, name, core, slots, rows, moving, fixed, outs):
    chunk = ROW_CHUNK
    steps = rows // chunk
    blocks = slots.shape[0]
    n_in = len(moving) + len(fixed)

    def kernel(core_ref, slot_ref, *refs):
        first = core_ref[0] * rows + pl.program_id(0) * chunk
        pick = own_pick(first, chunk, slot_ref, blocks)
        results = body(pick, *[r[...] for r in refs[:n_in]])
        for ref, value in zip(refs[n_in:], results):
            ref[...] = value

    specs = []
    for array, offset in moving:
        if offset:
            specs.append(
                pl.BlockSpec((chunk, array.shape[1]), lambda i, c, s: (c[0] * steps + i, 0))
            )
        else:
            specs.append(pl.BlockSpec((chunk, array.shape[1]), lambda i, c, s: (i, 0)))
    for array in fixed:
        specs.append(pl.BlockSpec(array.shape, lambda i, c, s: (0, 0)))
    return pl.pallas_call(
        kernel,
        grid_spec=pltpu.PrefetchScalarGridSpec(
            num_scalar_prefetch=2,
            grid=(steps,),
            in_specs=specs,
            out_specs=[pl.BlockSpec((chunk, c), lambda i, c_, s: (i, 0)) for c, _ in outs],
        ),
        out_shape=[jax.ShapeDtypeStruct((rows, c), d) for c, d in outs],
        compiler_params=pltpu.CompilerParams(vmem_limit_bytes=40 << 20),
        name=name,
    )(core, slots, *[a for a, _ in moving], *fixed)


def after_attention(pick, mine, far, rows, exit_row, gain, shift, b_o_rows, a_up_rows):
    width = rows.shape[1]
    total = mine.astype(f32) + far.astype(f32)
    down_o = factor * jnp.where(pick, total[:, width:], 0.0).astype(bf16)
    middle = rows.astype(f32) + total[:, :width] + exit_row + dot_nn(down_o, b_o_rows)
    unit, _ = standardize(middle)
    low = (unit * gain + shift).astype(bf16)
    down_up = factor * jnp.where(pick, dot_nt(low, a_up_rows), 0.0).astype(bf16)
    return middle, jnp.concatenate([low, down_up + down_o], axis=1)


def after_hidden(pick, mine, far, middle, exit_row, b_down_rows):
    width = middle.shape[1]
    total = mine.astype(f32) + far.astype(f32)
    down = factor * jnp.where(pick, total[:, width:], 0.0).astype(bf16)
    out = middle + total[:, :width] + exit_row + dot_nn(down, b_down_rows)
    return (jnp.concatenate([out.astype(bf16), down], axis=1),)


def back_middle(pick, mine, far, middle, loss, gain, a_up_rows, b_o_rows):
    width = middle.shape[1]
    total = mine.astype(f32) + far.astype(f32)
    grad_down = (factor * jnp.where(pick, total[:, width:], 0.0)).astype(bf16)
    grad_normed = total[:, :width] + dot_nn(grad_down, a_up_rows)
    unit, inverse = standardize(middle)
    grad = loss.astype(f32) + norm_back(grad_normed * gain, unit, inverse)
    low = grad.astype(bf16)
    grad_o = (factor * jnp.where(pick, dot_nt(low, b_o_rows), 0.0)).astype(bf16)
    return grad, jnp.concatenate([low, grad_o + grad_down], axis=1)


def back_first(pick, mine, far, grad_down, rows, grad_middle, gain, a_rows):
    total = mine.astype(f32) + far.astype(f32)
    grad_normed = total + dot_nn(grad_down, a_rows)
    unit, inverse = standardize(rows.astype(f32))
    return ((grad_middle + norm_back(grad_normed * gain, unit, inverse)).astype(bf16),)


def pack_terms(tensor, two, back, attended, grad_pre, hidden, grad_dd, dd, loss, local):
    width = loss.shape[1]
    cut = local // 4

    def kernel(t_ref, two_ref, back_ref, att_ref, gp_ref, hid_ref, gdd_ref, dd_ref, loss_ref, out):
        lanes = pl.ds(pl.multiple_of(t_ref[0] * local, local), local)
        two_tail = two_ref[:, width:]
        back_tail = back_ref[:, width:]
        terms = [
            dot_tn(back_tail, att_ref[...])[PAIR : 2 * PAIR],
            dot_tn(two_tail, back_ref[:, lanes])[PAIR : 2 * PAIR],
            dot_tn(back_tail, two_ref[:, lanes])[:PAIR],
            dot_tn(dd_ref[...], loss_ref[:, lanes])[:PAIR],
        ]
        for n, term in enumerate(terms):
            low = term.astype(bf16)
            for g in range(4):
                out[g, n * PAIR : (n + 1) * PAIR, :] = low[:, g * cut : (g + 1) * cut]
        base = len(terms) * PAIR
        for left, right in ((two_tail, gp_ref), (gdd_ref[...], hid_ref)):
            low = dot_tn(left, right[...])[:PAIR].astype(bf16)
            tiles = low.shape[1] // (4 * cut)
            for g in range(4):
                for t in range(tiles):
                    c = (g * tiles + t) * cut
                    out[g, base + t * PAIR : base + (t + 1) * PAIR, :] = low[:, c : c + cut]
            base += tiles * PAIR

    tiles = hidden.shape[1] // local
    whole = pl.BlockSpec(memory_space=pltpu.VMEM)
    return pl.pallas_call(
        kernel,
        grid_spec=pltpu.PrefetchScalarGridSpec(
            num_scalar_prefetch=1, grid=(), in_specs=[whole] * 8, out_specs=whole
        ),
        out_shape=jax.ShapeDtypeStruct((4, (4 + 2 * tiles) * PAIR, cut), bf16),
        compiler_params=pltpu.CompilerParams(vmem_limit_bytes=40 << 20),
        name="pack_terms",
    )(tensor, two, back, attended, grad_pre, hidden, grad_dd, dd, loss)


def pack_projections(tensor, grad_down, normed_wide, grad_qkv, local):
    width = normed_wide.shape[1] - AUG
    cut = local // 4

    def kernel(t_ref, gd_ref, nw_ref, gq_ref, out):
        lanes = pl.ds(pl.multiple_of(t_ref[0] * local, local), local)
        down = dot_tn(gd_ref[...], nw_ref[:, lanes]).astype(bf16)
        up = dot_tn(nw_ref[:, width:], gq_ref[...]).astype(bf16)
        for i in range(3):
            rows = slice(i * PAIR, (i + 1) * PAIR)
            for g in range(4):
                out[g, rows, :] = down[rows, g * cut : (g + 1) * cut]
                c = i * local + g * cut
                out[g, (3 + i) * PAIR : (4 + i) * PAIR, :] = up[rows, c : c + cut]

    whole = pl.BlockSpec(memory_space=pltpu.VMEM)
    return pl.pallas_call(
        kernel,
        grid_spec=pltpu.PrefetchScalarGridSpec(
            num_scalar_prefetch=1, grid=(), in_specs=[whole] * 3, out_specs=whole
        ),
        out_shape=jax.ShapeDtypeStruct((4, 6 * PAIR, cut), bf16),
        compiler_params=pltpu.CompilerParams(vmem_limit_bytes=24 << 20),
        name="pack_projections",
    )(tensor, grad_down, normed_wide, grad_qkv)


def unpack_terms(context, owner, near, cross, tiles):
    cut = near.shape[2]
    half = cut // 2
    base = (4 + 2 * tiles) * PAIR

    def kernel(c_ref, owner_ref, near_ref, cross_ref, a_attn, b_attn, a_up, b_up, a_down, b_down):
        first = c_ref[0] == 0

        for k in range(4):
            for s in range(SLOTS):
                who = owner_ref[k * SLOTS + s]

                def value(row):
                    rows = slice(row + s * RANK, row + (s + 1) * RANK)
                    return near_ref[k, rows, :].astype(f32) + cross_ref[k, rows, :].astype(f32)

                def narrow(row):
                    v = value(row)
                    return jnp.where(first, v[:, :half], v[:, half:])

                for i in range(3):
                    a_attn[i, pl.ds(who, 1)] = narrow(base + i * PAIR)[None]
                    b_attn[i, pl.ds(who, 1)] = narrow(base + (3 + i) * PAIR)[None]
                a_attn[3, pl.ds(who, 1)] = narrow(0)[None]
                b_attn[3, pl.ds(who, 1)] = narrow(PAIR)[None]
                a_up[pl.ds(who, 1)] = narrow(2 * PAIR)[None]
                b_down[pl.ds(who, 1)] = narrow(3 * PAIR)[None]
                for n, ref in enumerate((b_up, a_down)):
                    start = (4 + n * tiles) * PAIR
                    for t in range(tiles // 2):
                        ref[pl.ds(who, 1), :, t * cut : (t + 1) * cut] = jnp.where(
                            first,
                            value(start + t * PAIR),
                            value(start + (tiles // 2 + t) * PAIR),
                        )[None]

    narrow_shape = (ADAPTERS, RANK, half)
    wide_shape = (ADAPTERS, RANK, tiles * half)
    whole = pl.BlockSpec(memory_space=pltpu.VMEM)
    shapes = [(4,) + narrow_shape, (4,) + narrow_shape, narrow_shape, wide_shape, wide_shape, narrow_shape]
    return pl.pallas_call(
        kernel,
        grid_spec=pltpu.PrefetchScalarGridSpec(
            num_scalar_prefetch=2, grid=(), in_specs=[whole] * 2, out_specs=[whole] * 6
        ),
        out_shape=[jax.ShapeDtypeStruct(shape, f32) for shape in shapes],
        compiler_params=pltpu.CompilerParams(vmem_limit_bytes=24 << 20),
        name="unpack_terms",
    )(context, owner, near, cross)


def unpack_plain(context, owner, total, tiles, ctx_size):
    cut = total.shape[2]
    place = (jnp.arange(ADAPTERS, dtype=jnp.int32)[:, None] == owner[None, :]).astype(f32)
    parts = total.reshape(4, -1, SLOTS, RANK, cut)
    placed = jnp.einsum("ag,ngrc->narc", place, jnp.transpose(parts, (1, 0, 2, 3, 4)).reshape(
        parts.shape[1], 4 * SLOTS, RANK, cut), precision=lax.Precision.HIGHEST)

    def narrow(items):
        size = items.shape[-1] // ctx_size
        return lax.dynamic_slice_in_dim(items, context * size, size, items.ndim - 1)

    def broad(items):
        joined = jnp.transpose(items, (1, 2, 0, 3)).reshape(ADAPTERS, RANK, -1)
        return narrow(joined)

    base = 4 + 2 * tiles
    return (
        narrow(jnp.concatenate([placed[base : base + 3], placed[:1]])),
        narrow(jnp.concatenate([placed[base + 3 : base + 6], placed[1:2]])),
        narrow(placed[2]),
        broad(placed[4 : 4 + tiles]),
        broad(placed[4 + tiles : 4 + 2 * tiles]),
        narrow(placed[3]),
    )


def gate(value, *waits):
    if not waits:
        return value
    return lax.optimization_barrier((value,) + waits)[0]


def make_body(ctx_size):
    pair_ctx = ctx_size == 2

    def body(
        inputs,
        loss_sensitivity,
        parent_block,
        adapter_of,
        w_qkv,
        bias_qv,
        w_o,
        exit_offsets,
        ln_gain,
        ln_bias,
        w_in,
        hidden_offset_frozen,
        w_out,
        a_attn,
        b_attn,
        a_up,
        b_up,
        a_down,
        b_down,
    ):
        group = lax.axis_index("fsdp")
        context = lax.axis_index("ctx")
        tensor = lax.axis_index("tp")
        core = tensor % 2
        tokens, width = inputs.shape
        half = tokens // 2
        local = w_qkv.shape[2]
        shard = w_qkv.shape[1]
        hidden_local = w_in.shape[1]
        heads = local // HD
        blocks = tokens // BLOCK
        scale = HD ** (-0.5)
        wide = width + AUG

        def on(value, axis, pairs):
            return lax.ppermute(value, axis, pairs)

        def own_rows(matrix):
            return lax.dynamic_slice_in_dim(matrix, core * half, half, 0)

        def other_rows(matrix):
            return lax.dynamic_slice_in_dim(matrix, (1 - core) * half, half, 0)

        def natural(own, other):
            return jnp.concatenate(
                [jnp.where(core == 0, own, other), jnp.where(core == 0, other, own)], axis=0
            )

        def local_lanes(matrix):
            return lax.dynamic_slice_in_dim(matrix, tensor * local, local, matrix.ndim - 1)

        def put(buffer, piece, row, column):
            return lax.dynamic_update_slice(buffer, piece, (row, column))

        swap_y = [(0, 1), (1, 0)]
        spot = jnp.stack([group, context]).astype(jnp.int32)

        def spread_weight(own, half_axis, first_waits, last_waits):
            size = own.shape[half_axis] // 2
            both = ("fsdp", "ctx")
            inner_y = [(2, 3), (3, 2), (4, 5), (5, 4)]
            outer_y = [(0, 1), (1, 0), (6, 7), (7, 6)]
            outward = [(1, 0), (2, 3)]
            part = lax.dynamic_slice_in_dim(own, context * size, size, half_axis)
            one = on(part, "fsdp", [(0, 1), (1, 0), (2, 3), (3, 2)])
            in_far = on(part, "fsdp", [(1, 2), (2, 1)])
            one, in_far, *first = lax.optimization_barrier((one, in_far, *first_waits))
            y_one = on(one, "ctx", swap_y)
            y_in_far = on(in_far, both, inner_y)
            out_two = on(in_far, "fsdp", outward)
            in_two = on(one, "fsdp", [(1, 2), (2, 1)])
            y_one, out_two, in_two = lax.optimization_barrier((y_one, out_two, in_two))
            out_far = on(in_two, "fsdp", outward)
            y_out_two = on(out_two, both, outer_y)
            y_in_two = on(in_two, both, inner_y)
            out_far, y_out_two, *last = lax.optimization_barrier((out_far, y_out_two, *last_waits(*first)))
            y_out_far = on(out_far, both, outer_y)
            pieces = (own, one, y_one, in_two, y_in_two, out_two, y_out_two)
            pieces += (in_far, y_in_far, out_far, y_out_far)
            return pieces, last, (in_two, out_two), (out_far,)

        def gather_weight(own, chunks, waits, swap_waits=()):
            half_rows = own.shape[0] // 2
            size = half_rows // chunks
            gathered = []
            swapped = []
            for j in range(chunks):
                part = lax.dynamic_slice_in_dim(own, context * half_rows + j * size, size, 0)
                part = gate(part, *waits)
                every = lax.all_gather(part, "fsdp", axis=0, tiled=True)
                gathered.append(every)
                every = gate(every, *swap_waits)
                others = jnp.concatenate(
                    [
                        lax.dynamic_slice_in_dim(every, (group ^ i) * size, size, 0)
                        for i in range(1, 4)
                    ],
                    axis=0,
                )
                swapped.append(on(others, "ctx", swap_y))
            return gathered, swapped

        def send_tp(other_low, own_full):
            got = on(other_low, "tp", CORE_SWAP)
            mine = round_low(own_full + got.astype(f32))
            return mine, on(mine, "tp", X_SWAP)

        def sum_sent(sent, waits=()):
            mine, far = sent
            return mine.astype(f32) + gate(far, *waits).astype(f32)

        pair = lax.dynamic_slice_in_dim(adapter_of, group * SLOTS, SLOTS)

        def pick_pair(array, axis):
            return jnp.concatenate(
                [lax.dynamic_slice_in_dim(array, pair[s], 1, axis) for s in range(SLOTS)], axis
            )

        a_pair = jnp.swapaxes(pick_pair(a_attn, 1), 2, 3)
        def down_up_pad(matrix, before=0):
            return jnp.pad(matrix, ((before, AUG - before - matrix.shape[0]), (0, 0)))

        a_qkv_rows = down_up_pad(a_pair[:3].reshape(3 * PAIR, width).astype(bf16))
        a_o_rows = local_lanes(a_pair[3].reshape(PAIR, width)).astype(bf16)
        b_pair = pick_pair(b_attn, 1)
        b_qkv_rows = local_lanes(b_pair[:3]).reshape(3, PAIR, local).astype(bf16)
        b_o_rows = down_up_pad(b_pair[3].reshape(PAIR, width).astype(bf16), PAIR)
        a_up_rows = down_up_pad(
            jnp.swapaxes(pick_pair(a_up, 0), 1, 2).reshape(PAIR, width).astype(bf16)
        )
        b_up_rows = pick_pair(b_up, 0).reshape(PAIR, hidden_local).astype(bf16)
        a_down_rows = (
            jnp.swapaxes(pick_pair(a_down, 0), 1, 2).reshape(PAIR, hidden_local).astype(bf16)
        )
        b_down_rows = down_up_pad(pick_pair(b_down, 0).reshape(PAIR, width).astype(bf16))

        def bias_lanes(opened):
            count = opened.shape[1]
            block = jnp.arange(count * BLOCK, dtype=jnp.int32) // BLOCK
            hit = opened[:, :, None] & (block[None, None, :] == jnp.arange(count)[None, :, None])
            return jnp.where(jnp.any(hit, axis=1), 0.0, neg_fill).astype(f32)

        reach, slot = ancestry(parent_block[0])
        all_blocks = reach.shape[0]
        first_block = context * blocks
        far_blocks = blocks if pair_ctx else all_blocks
        reach_rows = lax.dynamic_slice_in_dim(reach, first_block, blocks, 0)
        block_ids = jnp.arange(far_blocks, dtype=jnp.int32)
        far_open = (reach_rows[:, :far_blocks] > 0.5) & (block_ids[None, :] < first_block)
        own_open = lax.dynamic_slice_in_dim(reach_rows, first_block, blocks, 1) > 0.5
        far_bias = bias_lanes(far_open)
        own_bias = bias_lanes(own_open)

        slots = lax.dynamic_slice_in_dim(slot, first_block, blocks).astype(jnp.int32)
        lane_slot = (jnp.arange(AUG, dtype=jnp.int32) // RANK) % SLOTS

        def picks(first_row, count):
            block = (jnp.arange(count, dtype=jnp.int32) + first_row) // BLOCK
            row_slot = jnp.sum(
                jnp.where(block[:, None] == jnp.arange(blocks)[None, :], slots[None, :], 0), axis=1
            )
            return (row_slot[:, None] == lane_slot[None, :]).astype(f32)

        pick_own = picks(core * half, half)

        gain_one, shift_one = ln_gain[0][None, :], ln_bias[0][None, :]
        gain_two, shift_two = ln_gain[1][None, :], ln_bias[1][None, :]

        def widen(low, tail):
            return jnp.concatenate([low, tail], axis=1)

        normed_wide = norm_wide(
            [inputs], jnp.arange(4, dtype=jnp.int32), slots, a_qkv_rows, gain_one, shift_one, tokens
        )
        q_aug = jnp.concatenate(
            [jnp.pad(b_qkv_rows[i], ((0, 0), (i * local, (2 - i) * local))) for i in range(3)]
            + [jnp.zeros((AUG - 3 * PAIR, 3 * local), bf16)],
            axis=0,
        )
        o_aug = down_up_pad(a_o_rows, PAIR).T
        in_aug = down_up_pad(b_up_rows)
        out_aug = down_up_pad(a_down_rows).T
        if pair_ctx:
            quarter = tokens // 4
            sent = lax.dynamic_slice_in_dim(inputs, tensor * quarter, quarter, 0)
            far_quarter = on(sent, "ctx", [(0, 1)])

            def last_waits(quarter_rows):
                return (
                    quarter_rows,
                    on(quarter_rows, "tp", X_SWAP),
                    on(quarter_rows, "tp", CORE_SWAP),
                    normed_wide,
                )

            far_places = jnp.stack([tensor, tensor ^ 2, tensor ^ 1, tensor ^ 3]).astype(jnp.int32)
            q_pieces, last, q_second, q_third = spread_weight(
                w_qkv, 1, (far_quarter,), last_waits
            )
            far_quarter, far_x, far_core, normed_wide = last
            far_both = on(far_x, "tp", CORE_SWAP)
            q_through = (q_pieces[5], q_pieces[7])
            o_near, o_cross = gather_weight(w_o, 1, q_second)
            in_near, in_cross = gather_weight(w_in, 2, q_third)
            q_full = assemble(
                spot, q_pieces, q_aug, wide, 3 * local, ("rows", shard, shard // 2), 3
            )
            o_full = assemble_gathered(spot, w_o, o_near, o_cross, o_aug, local, wide, "columns")
            in_full = assemble_gathered(
                spot, w_in, in_near, in_cross, in_aug, wide, hidden_local, "rows"
            )
            out_near, out_cross = gather_weight(w_out, 2, q_third)
        else:
            own_q = jnp.transpose(w_qkv, (1, 0, 2)).reshape(shard, 3 * local)
            q_full = jnp.concatenate([lax.all_gather(own_q, "fsdp", axis=0, tiled=True), q_aug], 0)
            o_full = jnp.concatenate([lax.all_gather(w_o, "fsdp", axis=1, tiled=True), o_aug], 1)
            in_full = jnp.concatenate([lax.all_gather(w_in, "fsdp", axis=0, tiled=True), in_aug], 0)
            out_full = jnp.concatenate(
                [lax.all_gather(w_out, "fsdp", axis=1, tiled=True), out_aug], 1
            )

        normed, reduced_qkv = normed_wide[:, :width], normed_wide[:, width:]
        zero_bias = jnp.zeros((local,), f32)
        q_bias = jnp.concatenate([bias_qv[0], zero_bias, bias_qv[1]])[None, :]
        qkv = (dot_nn(normed_wide, q_full) + q_bias).astype(bf16)
        if pair_ctx:
            far_wide = norm_wide(
                [far_quarter, far_x, far_core, far_both],
                far_places,
                slot[:blocks].astype(jnp.int32),
                a_qkv_rows,
                gain_one,
                shift_one,
                tokens,
            )
            far_kv = (dot_nn(far_wide, q_full[:, local:]) + q_bias[:, local:]).astype(bf16)
        else:
            far_kv = lax.all_gather(qkv[:, local:], "ctx", axis=0, tiled=True)

        attended_f, probs_far, probs_own = attend_forward(
            qkv, far_kv, far_bias, own_bias, heads, scale
        )
        attended = attended_f.astype(bf16)
        attended_own = own_rows(attended)
        attended_other = other_rows(attended)
        branch_sent = send_tp(
            dot_nn(attended_other, o_full).astype(bf16), dot_nn(attended_own, o_full)
        )
        core_id = core.astype(jnp.int32)[None]
        middle, two_own = row_call(
            after_attention,
            "after_attention",
            core_id,
            slots,
            half,
            [(branch_sent[0], False), (branch_sent[1], False), (inputs, True)],
            [exit_offsets[:1], gain_two, shift_two, b_o_rows, a_up_rows],
            [(width, f32), (wide, bf16)],
        )
        two_other = on(two_own, "tp", CORE_SWAP)
        two_wide = jnp.concatenate([two_own, two_other], axis=0)

        pre_act = dot_nn(two_wide, in_full) + hidden_offset_frozen[None, :]
        phi = 0.5 * (1.0 + lax.erf(pre_act * (2.0 ** -0.5)))
        hidden = (pre_act * phi).astype(bf16)
        slope = (
            phi + pre_act * jnp.exp(-0.5 * pre_act * pre_act) * (0.5 / jnp.pi) ** 0.5
        ).astype(bf16)

        if pair_ctx:
            out_full = assemble_gathered(
                gate(spot, hidden),
                w_out,
                out_near,
                out_cross,
                out_aug,
                hidden_local,
                wide,
                "columns",
            )

        loss_own = own_rows(loss_sensitivity)
        loss_rel = jnp.concatenate([loss_own, other_rows(loss_sensitivity)], axis=0)
        pick_rel = jnp.concatenate([pick_own, picks((1 - core) * half, half)], axis=0)
        grad_down_down = (factor * dot_nt(loss_rel, b_down_rows) * pick_rel).astype(bf16)
        loss_wide = widen(loss_rel, grad_down_down)
        grad_pre = (dot_nt(loss_wide, out_full) * slope.astype(f32)).astype(bf16)
        two_sent = send_tp(
            dot_nt(grad_pre[half:], in_full).astype(bf16), dot_nt(grad_pre[:half], in_full)
        )
        grad_middle, back_own = row_call(
            back_middle,
            "back_middle",
            core_id,
            slots,
            half,
            [
                (two_sent[0], False),
                (two_sent[1], False),
                (middle, False),
                (loss_sensitivity, True),
            ],
            [gain_two, a_up_rows, b_o_rows],
            [(width, f32), (wide, bf16)],
        )
        back_other = on(back_own, "tp", CORE_SWAP)
        grad_attended = natural(
            dot_nt(back_own, o_full).astype(bf16), dot_nt(back_other, o_full).astype(bf16)
        )

        grad_q, grad_k, grad_v, far_grad_k, far_grad_v = attend_backward(
            qkv, far_kv, grad_attended, attended_f, probs_far, probs_own, heads, scale
        )
        late_hidden = gate(hidden, two_sent[0])
        exit_sent = send_tp(
            dot_nn(late_hidden[half:], out_full).astype(bf16), dot_nn(late_hidden[:half], out_full)
        )
        if pair_ctx:
            more_k = on(far_grad_k, "ctx", [(1, 0)])
            more_v = on(far_grad_v, "ctx", [(1, 0)])
        else:
            more_k = lax.psum_scatter(far_grad_k, "ctx", scatter_dimension=0, tiled=True)
            more_v = lax.psum_scatter(far_grad_v, "ctx", scatter_dimension=0, tiled=True)
        (layer_wide,) = row_call(
            after_hidden,
            "after_hidden",
            core_id,
            slots,
            half,
            [(exit_sent[0], False), (gate(exit_sent[1], more_v), False), (middle, False)],
            [exit_offsets[1:], b_down_rows],
            [(wide, bf16)],
        )
        layer_other = on(layer_wide, "tp", CORE_SWAP)
        layer_out = natural(layer_wide[:, :width], layer_other[:, :width])
        down_down_rel = jnp.concatenate([layer_wide[:, width:], layer_other[:, width:]], axis=0)

        grad_qkv = jnp.concatenate(
            [
                grad_q,
                (grad_k.astype(f32) + more_k.astype(f32)).astype(bf16),
                (grad_v.astype(f32) + more_v.astype(f32)).astype(bf16),
            ],
            axis=1,
        )
        low_part = dot_nt(grad_qkv, q_full[width:]).astype(bf16)
        low_core = on(low_part, "tp", CORE_SWAP)
        low_pair = round_low(low_part.astype(f32) + low_core.astype(f32))
        low_far = on(low_pair, "tp", X_SWAP)
        low_sum = low_pair.astype(f32) + low_far.astype(f32)
        grad_down_qkv = (factor * low_sum * picks(0, tokens)).astype(bf16)
        grad_one_other = dot_nt(other_rows(grad_qkv), q_full[:width]).astype(bf16)
        grad_one_own = dot_nt(own_rows(grad_qkv), q_full[:width])
        one_sent = send_tp(grad_one_other, grad_one_own)
        tensor_id = tensor.astype(jnp.int32)[None]
        tiles = hidden_local // local
        packed = pack_terms(
            gate(tensor_id, more_v),
            two_wide,
            jnp.concatenate([back_own, back_other], axis=0),
            jnp.concatenate([attended_own, attended_other], axis=0),
            grad_pre,
            hidden,
            grad_down_down,
            down_down_rel,
            loss_rel,
            local,
        )
        packed_qkv = pack_projections(
            gate(tensor_id, one_sent[0]), grad_down_qkv, normed_wide, grad_qkv, local
        )
        received = []
        for k in range(4):
            piece = jnp.concatenate(
                [
                    lax.dynamic_index_in_dim(packed, group ^ k, 0, keepdims=False),
                    lax.dynamic_index_in_dim(packed_qkv, group ^ k, 0, keepdims=False),
                ],
                axis=0,
            )
            received.append(on(piece, "fsdp", [(i, i ^ k) for i in range(4)]) if k else piece)
        near = jnp.stack(received)
        holder = jnp.stack([group ^ k for k in range(4)])
        owner = adapter_of.reshape(4, SLOTS)[holder].reshape(4 * SLOTS)
        if pair_ctx:
            cross = on(near, "ctx", swap_y)
            adapter_grads = unpack_terms(
                context.astype(jnp.int32)[None], owner, near, cross, tiles
            )
        else:
            adapter_grads = unpack_plain(
                context, owner, lax.psum(near.astype(f32), "ctx"), tiles, ctx_size
            )
        (grad_own,) = row_call(
            back_first,
            "back_first",
            core_id,
            slots,
            half,
            [
                (one_sent[0], False),
                (gate(one_sent[1], adapter_grads[0]), False),
                (grad_down_qkv, True),
                (inputs, True),
                (grad_middle, False),
            ],
            [gain_one, a_qkv_rows],
            [(width, bf16)],
        )
        grad_other = on(grad_own, "tp", CORE_SWAP)
        grad_inputs = natural(grad_own, grad_other)

        out_a_attn, out_b_attn, out_a_up, out_b_up, out_a_down, out_b_down = adapter_grads
        return (
            layer_out,
            grad_inputs,
            jnp.swapaxes(out_a_attn, 2, 3),
            out_b_attn,
            jnp.swapaxes(out_a_up, 1, 2),
            out_b_up,
            jnp.swapaxes(out_a_down, 1, 2),
            out_b_down,
        )

    return body


def solution(mesh):
    in_specs = (
        P(("fsdp", "ctx"), None),
        P(("fsdp", "ctx"), None),
        P("fsdp", None),
        P(),
        P(None, "fsdp", "tp"),
        P(None, "tp"),
        P("tp", "fsdp"),
        P(),
        P(),
        P(),
        P("fsdp", "tp"),
        P("tp"),
        P("tp", "fsdp"),
        P(),
        P(),
        P(),
        P(None, None, "tp"),
        P(None, "tp", None),
        P(),
    )
    out_specs = (
        P(("fsdp", "ctx"), None),
        P(("fsdp", "ctx"), None),
        P(None, None, ("tp", "fsdp", "ctx"), None),
        P(None, None, None, ("tp", "fsdp", "ctx")),
        P(None, ("tp", "fsdp", "ctx"), None),
        P(None, None, ("tp", "fsdp", "ctx")),
        P(None, ("tp", "fsdp", "ctx"), None),
        P(None, None, ("tp", "fsdp", "ctx")),
    )
    return jax.shard_map(
        make_body(mesh.shape["ctx"]),
        mesh=mesh,
        in_specs=in_specs,
        out_specs=out_specs,
        check_vma=False,
    )
```

```python
import jax
import jax.numpy as jnp
from jax import lax
from jax.experimental import pallas as pl
from jax.experimental.pallas import tpu as pltpu
from jax.sharding import PartitionSpec as P

HD = 128
RANK = 16
ADAPTERS = 8
SLOTS = 2
PAIR = SLOTS * RANK
BLOCK = 256
AUG = 128
ROW_CHUNK = 128
HINT = pl.CostEstimate(flops=1, transcendentals=0, bytes_accessed=1)

layer_eps = 1e-05
factor = 0.5
neg_fill = -1e30
bf16 = jnp.bfloat16
f32 = jnp.float32

CORE_SWAP = [(0, 1), (1, 0), (2, 3), (3, 2)]
SWAP_Y = [(0, 1), (1, 0)]
X_SWAP = [(0, 2), (2, 0), (1, 3), (3, 1)]


def dot_nn(a, b):
    return lax.dot_general(a, b, (((1,), (0,)), ((), ())), preferred_element_type=f32)


def dot_nt(a, b):
    return lax.dot_general(a, b, (((1,), (1,)), ((), ())), preferred_element_type=f32)


def dot_tn(a, b):
    return lax.dot_general(a, b, (((0,), (0,)), ((), ())), preferred_element_type=f32)


def round_low(v):
    return lax.reduce_precision(v, 8, 7).astype(bf16)


def standardize(rows):
    centre = rows - jnp.mean(rows, axis=-1, keepdims=True)
    spread = jnp.mean(centre * centre, axis=-1, keepdims=True)
    inverse = lax.rsqrt(spread + layer_eps)
    return centre * inverse, inverse


def norm_back(grad_scaled, unit, inverse):
    first = jnp.mean(grad_scaled, axis=-1, keepdims=True)
    second = jnp.mean(grad_scaled * unit, axis=-1, keepdims=True)
    return inverse * (grad_scaled - first - unit * second)


def ancestry(parents):
    total = parents.shape[0]
    position = jnp.arange(total, dtype=jnp.int32)
    reach = (
        (parents[:, None] == position[None, :]) | (position[:, None] == position[None, :])
    ).astype(f32)
    span = 1
    while span < total:
        reach = jnp.minimum(jnp.sum(reach[:, :, None] * reach[None, :, :], axis=1), 1.0)
        span *= 2
    roots = (parents < 0).astype(f32)
    order = jnp.sum(jnp.where(position[None, :] <= position[:, None], roots[None, :], 0.0), axis=1)
    slot = jnp.sum(reach * (roots * (order - 1.0))[None, :], axis=1)
    return reach, slot


def attend_forward(qkv, far, far_base, far_bias, own_bias, heads, scale):
    tokens = qkv.shape[0]
    far_rows = far.shape[0]
    blocks = tokens // BLOCK

    def kernel(q_ref, k_ref, v_ref, fk_ref, fv_ref, fb_ref, ob_ref, o_ref, low_ref, pf_ref, po_ref):
        far_k = fk_ref[...]
        far_v = fv_ref[...]
        for b in range(blocks):
            rows = slice(b * BLOCK, (b + 1) * BLOCK)
            width = (b + 1) * BLOCK
            q = q_ref[rows, :]
            s_far = dot_nt(q, far_k) * scale + fb_ref[b : b + 1, :]
            s_own = dot_nt(q, k_ref[:width, :]) * scale + ob_ref[b : b + 1, :width]
            q_pos = lax.broadcasted_iota(jnp.int32, (BLOCK, width), 0) + b * BLOCK
            k_pos = lax.broadcasted_iota(jnp.int32, (BLOCK, width), 1)
            s_own = jnp.where(k_pos <= q_pos, s_own, neg_fill)
            top = jnp.maximum(
                jnp.max(s_far, axis=1, keepdims=True), jnp.max(s_own, axis=1, keepdims=True)
            )
            p_far = jnp.exp(s_far - top)
            p_own = jnp.exp(s_own - top)
            total = jnp.sum(p_far, axis=1, keepdims=True) + jnp.sum(p_own, axis=1, keepdims=True)
            inverse = 1.0 / total
            p_far = (p_far * inverse).astype(bf16)
            p_own = (p_own * inverse).astype(bf16)
            pf_ref[0, rows, :] = p_far
            po_ref[0, rows, :width] = p_own
            mixed = dot_nn(p_far, far_v) + dot_nn(p_own, v_ref[:width, :])
            o_ref[rows, :] = mixed
            low_ref[rows, :] = mixed.astype(bf16)

    return pl.pallas_call(
        kernel,
        grid=(heads,),
        in_specs=[
            pl.BlockSpec((tokens, HD), lambda h: (0, h)),
            pl.BlockSpec((tokens, HD), lambda h: (0, heads + h)),
            pl.BlockSpec((tokens, HD), lambda h: (0, 2 * heads + h)),
            pl.BlockSpec((far_rows, HD), lambda h: (0, far_base + h)),
            pl.BlockSpec((far_rows, HD), lambda h: (0, far_base + heads + h)),
            pl.BlockSpec((blocks, far_rows), lambda h: (0, 0)),
            pl.BlockSpec((blocks, tokens), lambda h: (0, 0)),
        ],
        out_specs=[
            pl.BlockSpec((tokens, HD), lambda h: (0, h)),
            pl.BlockSpec((tokens, HD), lambda h: (0, h)),
            pl.BlockSpec((1, tokens, far_rows), lambda h: (h, 0, 0)),
            pl.BlockSpec((1, tokens, tokens), lambda h: (h, 0, 0)),
        ],
        out_shape=[
            jax.ShapeDtypeStruct((tokens, heads * HD), f32),
            jax.ShapeDtypeStruct((tokens, heads * HD), bf16),
            jax.ShapeDtypeStruct((heads, tokens, far_rows), bf16),
            jax.ShapeDtypeStruct((heads, tokens, tokens), bf16),
        ],
        compiler_params=pltpu.CompilerParams(vmem_limit_bytes=56 << 20),
        cost_estimate=HINT,
        name="attend_forward",
    )(qkv, qkv, qkv, far, far, far_bias, own_bias)


def attend_backward(qkv, far, far_base, grad_attended, attended, probs_far, probs_own, heads, scale):
    tokens = qkv.shape[0]
    far_rows = far.shape[0]
    blocks = tokens // BLOCK

    def kernel(
        q_ref, k_ref, v_ref, fk_ref, fv_ref, g_ref, o_ref, pf_ref, po_ref,
        dq_ref, dk_ref, dv_ref, dfk_ref, dfv_ref,
        dk_acc, dv_acc, dfk_acc, dfv_acc,
    ):
        far_k = fk_ref[...]
        far_v = fv_ref[...]
        for b in reversed(range(blocks)):
            first = b == blocks - 1
            rows = slice(b * BLOCK, (b + 1) * BLOCK)
            width = (b + 1) * BLOCK
            q = q_ref[rows, :]
            g = g_ref[rows, :]
            row_dot = jnp.sum(g.astype(f32) * o_ref[rows, :], axis=1, keepdims=True)
            p_far = pf_ref[0, rows, :]
            p_own = po_ref[0, rows, :width]
            d_far = (p_far.astype(f32) * (dot_nt(g, far_v) - row_dot)).astype(bf16)
            d_own = (p_own.astype(f32) * (dot_nt(g, v_ref[:width, :]) - row_dot)).astype(bf16)
            dq_ref[rows, :] = (
                (dot_nn(d_far, far_k) + dot_nn(d_own, k_ref[:width, :])) * scale
            ).astype(bf16)
            if first:
                dfk_acc[...] = dot_tn(d_far, q)
                dfv_acc[...] = dot_tn(p_far, g)
                dk_acc[...] = dot_tn(d_own, q)
                dv_acc[...] = dot_tn(p_own, g)
            else:
                dfk_acc[...] += dot_tn(d_far, q)
                dfv_acc[...] += dot_tn(p_far, g)
                dk_acc[:width, :] += dot_tn(d_own, q)
                dv_acc[:width, :] += dot_tn(p_own, g)
        dk_ref[...] = (dk_acc[...] * scale).astype(bf16)
        dv_ref[...] = dv_acc[...].astype(bf16)
        dfk_ref[...] = (dfk_acc[...] * scale).astype(bf16)
        dfv_ref[...] = dfv_acc[...].astype(bf16)

    head_spec = pl.BlockSpec((tokens, HD), lambda h: (0, h))
    far_spec = pl.BlockSpec((far_rows, HD), lambda h: (0, h))
    own_shape = jax.ShapeDtypeStruct((tokens, heads * HD), bf16)
    far_shape = jax.ShapeDtypeStruct((far_rows, heads * HD), bf16)
    return pl.pallas_call(
        kernel,
        grid=(heads,),
        in_specs=[
            head_spec,
            pl.BlockSpec((tokens, HD), lambda h: (0, heads + h)),
            pl.BlockSpec((tokens, HD), lambda h: (0, 2 * heads + h)),
            pl.BlockSpec((far_rows, HD), lambda h: (0, far_base + h)),
            pl.BlockSpec((far_rows, HD), lambda h: (0, far_base + heads + h)),
            head_spec,
            head_spec,
            pl.BlockSpec((1, tokens, far_rows), lambda h: (h, 0, 0)),
            pl.BlockSpec((1, tokens, tokens), lambda h: (h, 0, 0)),
        ],
        out_specs=[head_spec, head_spec, head_spec, far_spec, far_spec],
        out_shape=[own_shape, own_shape, own_shape, far_shape, far_shape],
        scratch_shapes=[
            pltpu.VMEM((tokens, HD), f32),
            pltpu.VMEM((tokens, HD), f32),
            pltpu.VMEM((far_rows, HD), f32),
            pltpu.VMEM((far_rows, HD), f32),
        ],
        compiler_params=pltpu.CompilerParams(vmem_limit_bytes=56 << 20),
        cost_estimate=HINT,
        name="attend_backward",
    )(qkv, qkv, qkv, far, far, grad_attended, attended, probs_far, probs_own)


def assemble(spot, pieces, tail, rows, columns, step, parts):
    direction, shard, half_rows = step
    count = max(parts, 1)
    part_columns = columns // count if parts else columns
    tail_rows, tail_columns = tail.shape

    def kernel(spot_ref, *refs):
        own, one, y_one, two, y_two, three, y_three, tail_ref, out, sem = refs
        group = spot_ref[0]
        context = spot_ref[1]
        inner = (group == 1) | (group == 2)

        def moves(piece, source, which, first):
            made = []
            for i in range(count):
                src = piece.at[i] if parts else piece
                n, m = src.shape
                if direction == "rows":
                    row = pl.multiple_of(source * shard + which * half_rows, half_rows)
                    dst = out.at[pl.ds(row, n), pl.ds(i * part_columns, m)]
                else:
                    row = pl.multiple_of(which * half_rows, half_rows)
                    col = pl.multiple_of(source * shard, shard)
                    dst = out.at[pl.ds(row, n), pl.ds(col, m)]
                made.append(pltpu.make_async_copy(src, dst, sem.at[first + i]))
            return made

        fixed = moves(own, group, 0, 0)
        fixed += moves(one, group ^ 1, context, count)
        fixed += moves(y_one, group ^ 1, 1 - context, 2 * count)
        second = jnp.where(inner, group ^ 3, group ^ 2)
        third = jnp.where(inner, group ^ 2, group ^ 3)
        fixed += moves(two, second, context, 3 * count)
        fixed += moves(y_two, second, 1 - context, 4 * count)
        fixed += moves(three, third, context, 5 * count)
        fixed += moves(y_three, third, 1 - context, 6 * count)
        row0 = rows - tail_rows if direction == "rows" else 0
        col0 = 0 if direction == "rows" else columns - tail_columns
        fixed.append(
            pltpu.make_async_copy(
                tail_ref,
                out.at[pl.ds(row0, tail_rows), pl.ds(col0, tail_columns)],
                sem.at[7 * count],
            )
        )
        for move in fixed:
            move.start()

        for move in fixed:
            move.wait()

    return pl.pallas_call(
        kernel,
        grid_spec=pltpu.PrefetchScalarGridSpec(
            num_scalar_prefetch=1,
            grid=(),
            in_specs=[pl.BlockSpec(memory_space=pl.ANY)] * 8,
            out_specs=pl.BlockSpec(memory_space=pltpu.VMEM),
            scratch_shapes=[pltpu.SemaphoreType.DMA((7 * count + 1,))],
        ),
        out_shape=jax.ShapeDtypeStruct((rows, columns), bf16),
        compiler_params=pltpu.CompilerParams(vmem_limit_bytes=24 << 20),
        cost_estimate=HINT,
        name="assemble",
    )(spot, *pieces, tail)


def norm_wide(pieces, places, slots, down_rows, gain, shift, tokens):
    width = gain.shape[1]
    blocks = tokens // BLOCK
    count = len(pieces)
    quarter = tokens // 4
    steps = 4 // count

    def kernel(place_ref, slot_ref, *refs):
        down_ref, gain_ref, shift_ref, out_ref = refs[count:]
        for i in range(4):
            x_ref = refs[i // steps]
            first = (i % steps) * quarter
            rows = x_ref[first : first + quarter, :].astype(f32)
            start = pl.multiple_of(place_ref[i] * quarter, quarter)
            unit, _ = standardize(rows)
            low = (unit * gain_ref[...] + shift_ref[...]).astype(bf16)
            block = (lax.broadcasted_iota(jnp.int32, (quarter, AUG), 0) + start) // BLOCK
            lane_slot = (lax.broadcasted_iota(jnp.int32, (quarter, AUG), 1) // RANK) % SLOTS
            slot = jnp.zeros((quarter, AUG), jnp.int32)
            for b in range(blocks):
                slot = jnp.where(block == b, slot_ref[b], slot)
            down = jnp.where(slot == lane_slot, dot_nt(low, down_ref[...]), 0.0)
            out_ref[pl.ds(start, quarter), :width] = low
            out_ref[pl.ds(start, quarter), width:] = factor * down.astype(bf16)

    whole = pl.BlockSpec(memory_space=pltpu.VMEM)
    return pl.pallas_call(
        kernel,
        grid_spec=pltpu.PrefetchScalarGridSpec(
            num_scalar_prefetch=2,
            grid=(),
            in_specs=[whole] * (count + 3),
            out_specs=whole,
        ),
        out_shape=jax.ShapeDtypeStruct((tokens, width + AUG), bf16),
        compiler_params=pltpu.CompilerParams(vmem_limit_bytes=32 << 20),
        cost_estimate=HINT,
        name="norm_wide",
    )(places, slots, *pieces, down_rows, gain, shift)


def own_pick(first_row, count, slot_ref, blocks):
    block = (lax.broadcasted_iota(jnp.int32, (count, AUG), 0) + first_row) // BLOCK
    lane_slot = (lax.broadcasted_iota(jnp.int32, (count, AUG), 1) // RANK) % SLOTS
    slot = jnp.zeros((count, AUG), jnp.int32)
    for b in range(blocks):
        slot = jnp.where(block == b, slot_ref[b], slot)
    return slot == lane_slot


def row_call(body, name, core, slots, rows, moving, fixed, outs):
    chunk = ROW_CHUNK
    steps = rows // chunk
    blocks = slots.shape[0]
    n_in = len(moving) + len(fixed)

    def kernel(core_ref, slot_ref, *refs):
        first = core_ref[0] * rows + pl.program_id(0) * chunk
        pick = own_pick(first, chunk, slot_ref, blocks)
        results = body(pick, *[r[...] for r in refs[:n_in]])
        for ref, value in zip(refs[n_in:], results):
            ref[...] = value

    specs = []
    for array, offset in moving:
        if offset:
            specs.append(
                pl.BlockSpec((chunk, array.shape[1]), lambda i, c, s: (c[0] * steps + i, 0))
            )
        else:
            specs.append(pl.BlockSpec((chunk, array.shape[1]), lambda i, c, s: (i, 0)))
    for array in fixed:
        specs.append(pl.BlockSpec(array.shape, lambda i, c, s: (0, 0)))
    return pl.pallas_call(
        kernel,
        grid_spec=pltpu.PrefetchScalarGridSpec(
            num_scalar_prefetch=2,
            grid=(steps,),
            in_specs=specs,
            out_specs=[pl.BlockSpec((chunk, c), lambda i, c_, s: (i, 0)) for c, _ in outs],
        ),
        out_shape=[jax.ShapeDtypeStruct((rows, c), d) for c, d in outs],
        compiler_params=pltpu.CompilerParams(vmem_limit_bytes=40 << 20),
        cost_estimate=HINT,
        name=name,
    )(core, slots, *[a for a, _ in moving], *fixed)


def after_attention(pick, mine, far, rows, exit_row, gain, shift, b_o_rows, a_up_rows):
    width = rows.shape[1]
    total = mine.astype(f32) + far.astype(f32)
    down_o = factor * jnp.where(pick, total[:, width:], 0.0).astype(bf16)
    middle = rows.astype(f32) + total[:, :width] + exit_row + dot_nn(down_o, b_o_rows)
    unit, _ = standardize(middle)
    low = (unit * gain + shift).astype(bf16)
    down_up = factor * jnp.where(pick, dot_nt(low, a_up_rows), 0.0).astype(bf16)
    return middle, jnp.concatenate([low, down_up + down_o], axis=1)


def after_hidden(pick, mine, far, middle, exit_row, b_down_rows):
    width = middle.shape[1]
    total = mine.astype(f32) + far.astype(f32)
    down = factor * jnp.where(pick, total[:, width:], 0.0).astype(bf16)
    out = middle + total[:, :width] + exit_row + dot_nn(down, b_down_rows)
    return (jnp.concatenate([out.astype(bf16), down], axis=1),)


def back_middle(pick, mine, far, middle, loss, gain, a_up_rows, b_o_rows):
    width = middle.shape[1]
    total = mine.astype(f32) + far.astype(f32)
    grad_down = (factor * jnp.where(pick, total[:, width:], 0.0)).astype(bf16)
    grad_normed = total[:, :width] + dot_nn(grad_down, a_up_rows)
    unit, inverse = standardize(middle)
    grad = loss.astype(f32) + norm_back(grad_normed * gain, unit, inverse)
    low = grad.astype(bf16)
    grad_o = (factor * jnp.where(pick, dot_nt(low, b_o_rows), 0.0)).astype(bf16)
    return grad, jnp.concatenate([low, grad_o + grad_down], axis=1)


def back_first(pick, mine, far, grad_down, rows, grad_middle, gain, a_rows):
    total = mine.astype(f32) + far.astype(f32)
    grad_normed = total + dot_nn(grad_down, a_rows)
    unit, inverse = standardize(rows.astype(f32))
    return ((grad_middle + norm_back(grad_normed * gain, unit, inverse)).astype(bf16),)


def pack_terms(where, two, back, attended, grad_pre, hidden, grad_dd, dd, loss, local):
    width = loss.shape[1]
    half = loss.shape[0] // 2
    cut = local // 4

    def kernel(
        t_ref, two_a, two_b, back_a, back_b, att_ref, gp_ref, hid_ref, gdd_ref, dd_a, dd_b, loss_ref, out
    ):
        lanes = pl.ds(pl.multiple_of(t_ref[0] * local, local), local)
        mine = pl.ds(pl.multiple_of(t_ref[1] * half, half), half)
        theirs = pl.ds(pl.multiple_of((1 - t_ref[1]) * half, half), half)
        halves = ((two_a, back_a, dd_a, mine), (two_b, back_b, dd_b, theirs))

        def both(make):
            return make(*halves[0]) + make(*halves[1])

        terms = [
            both(lambda t, b, d, r: dot_tn(b[:, width:], att_ref[r, :]))[PAIR : 2 * PAIR],
            both(lambda t, b, d, r: dot_tn(t[:, width:], b[:, lanes]))[PAIR : 2 * PAIR],
            both(lambda t, b, d, r: dot_tn(b[:, width:], t[:, lanes]))[:PAIR],
            both(lambda t, b, d, r: dot_tn(d[...], loss_ref[r, lanes]))[:PAIR],
        ]
        for n, term in enumerate(terms):
            low = term.astype(bf16)
            for g in range(4):
                out[g, n * PAIR : (n + 1) * PAIR, :] = low[:, g * cut : (g + 1) * cut]
        base = len(terms) * PAIR
        wide_terms = (
            dot_tn(two_a[:, width:], gp_ref[:half, :]) + dot_tn(two_b[:, width:], gp_ref[half:, :]),
            dot_tn(gdd_ref[...], hid_ref[...]),
        )
        for term in wide_terms:
            low = term[:PAIR].astype(bf16)
            tiles = low.shape[1] // (4 * cut)
            for g in range(4):
                for t in range(tiles):
                    c = (g * tiles + t) * cut
                    out[g, base + t * PAIR : base + (t + 1) * PAIR, :] = low[:, c : c + cut]
            base += tiles * PAIR

    tiles = hidden.shape[1] // local
    whole = pl.BlockSpec(memory_space=pltpu.VMEM)
    return pl.pallas_call(
        kernel,
        grid_spec=pltpu.PrefetchScalarGridSpec(
            num_scalar_prefetch=1, grid=(), in_specs=[whole] * 11, out_specs=whole
        ),
        out_shape=jax.ShapeDtypeStruct((4, (4 + 2 * tiles) * PAIR, cut), bf16),
        compiler_params=pltpu.CompilerParams(vmem_limit_bytes=40 << 20),
        cost_estimate=HINT,
        name="pack_terms",
    )(where, *two, *back, attended, grad_pre, hidden, grad_dd, *dd, loss)


def pack_projections(tensor, grad_down, normed_wide, grad_qkv, local):
    width = normed_wide.shape[1] - AUG
    cut = local // 4

    def kernel(t_ref, gd_ref, nw_ref, gq_ref, out):
        lanes = pl.ds(pl.multiple_of(t_ref[0] * local, local), local)
        down = dot_tn(gd_ref[...], nw_ref[:, lanes]).astype(bf16)
        up = dot_tn(nw_ref[:, width:], gq_ref[...]).astype(bf16)
        for i in range(3):
            rows = slice(i * PAIR, (i + 1) * PAIR)
            for g in range(4):
                out[g, rows, :] = down[rows, g * cut : (g + 1) * cut]
                c = i * local + g * cut
                out[g, (3 + i) * PAIR : (4 + i) * PAIR, :] = up[rows, c : c + cut]

    whole = pl.BlockSpec(memory_space=pltpu.VMEM)
    return pl.pallas_call(
        kernel,
        grid_spec=pltpu.PrefetchScalarGridSpec(
            num_scalar_prefetch=1, grid=(), in_specs=[whole] * 3, out_specs=whole
        ),
        out_shape=jax.ShapeDtypeStruct((4, 6 * PAIR, cut), bf16),
        compiler_params=pltpu.CompilerParams(vmem_limit_bytes=24 << 20),
        cost_estimate=HINT,
        name="pack_projections",
    )(tensor, grad_down, normed_wide, grad_qkv)


def unpack_terms(context, owner, near, cross, tiles):
    cut = near.shape[2]
    half = cut // 2
    base = (4 + 2 * tiles) * PAIR

    def kernel(c_ref, owner_ref, near_ref, cross_ref, a_attn, b_attn, a_up, b_up, a_down, b_down):
        first = c_ref[0] == 0

        for k in range(4):
            for s in range(SLOTS):
                who = owner_ref[k * SLOTS + s]

                def value(row):
                    rows = slice(row + s * RANK, row + (s + 1) * RANK)
                    return near_ref[k, rows, :].astype(f32) + cross_ref[k, rows, :].astype(f32)

                def narrow(row):
                    v = value(row)
                    return jnp.where(first, v[:, :half], v[:, half:])

                for i in range(3):
                    a_attn[i, pl.ds(who, 1)] = narrow(base + i * PAIR)[None]
                    b_attn[i, pl.ds(who, 1)] = narrow(base + (3 + i) * PAIR)[None]
                a_attn[3, pl.ds(who, 1)] = narrow(0)[None]
                b_attn[3, pl.ds(who, 1)] = narrow(PAIR)[None]
                a_up[pl.ds(who, 1)] = narrow(2 * PAIR)[None]
                b_down[pl.ds(who, 1)] = narrow(3 * PAIR)[None]
                for n, ref in enumerate((b_up, a_down)):
                    start = (4 + n * tiles) * PAIR
                    for t in range(tiles // 2):
                        ref[pl.ds(who, 1), :, t * cut : (t + 1) * cut] = jnp.where(
                            first,
                            value(start + t * PAIR),
                            value(start + (tiles // 2 + t) * PAIR),
                        )[None]

    narrow_shape = (ADAPTERS, RANK, half)
    wide_shape = (ADAPTERS, RANK, tiles * half)
    whole = pl.BlockSpec(memory_space=pltpu.VMEM)
    shapes = [(4,) + narrow_shape, (4,) + narrow_shape, narrow_shape, wide_shape, wide_shape, narrow_shape]
    return pl.pallas_call(
        kernel,
        grid_spec=pltpu.PrefetchScalarGridSpec(
            num_scalar_prefetch=2, grid=(), in_specs=[whole] * 2, out_specs=[whole] * 6
        ),
        out_shape=[jax.ShapeDtypeStruct(shape, f32) for shape in shapes],
        compiler_params=pltpu.CompilerParams(vmem_limit_bytes=24 << 20),
        cost_estimate=HINT,
        name="unpack_terms",
    )(context, owner, near, cross)


def unpack_plain(context, owner, total, tiles, ctx_size):
    cut = total.shape[2]
    place = (jnp.arange(ADAPTERS, dtype=jnp.int32)[:, None] == owner[None, :]).astype(f32)
    parts = total.reshape(4, -1, SLOTS, RANK, cut)
    placed = jnp.einsum("ag,ngrc->narc", place, jnp.transpose(parts, (1, 0, 2, 3, 4)).reshape(
        parts.shape[1], 4 * SLOTS, RANK, cut), precision=lax.Precision.HIGHEST)

    def narrow(items):
        size = items.shape[-1] // ctx_size
        return lax.dynamic_slice_in_dim(items, context * size, size, items.ndim - 1)

    def broad(items):
        joined = jnp.transpose(items, (1, 2, 0, 3)).reshape(ADAPTERS, RANK, -1)
        return narrow(joined)

    base = 4 + 2 * tiles
    return (
        narrow(jnp.concatenate([placed[base : base + 3], placed[:1]])),
        narrow(jnp.concatenate([placed[base + 3 : base + 6], placed[1:2]])),
        narrow(placed[2]),
        broad(placed[4 : 4 + tiles]),
        broad(placed[4 + tiles : 4 + 2 * tiles]),
        narrow(placed[3]),
    )


def project(own, far, weight, bias, local):
    tokens, wide = own.shape
    blocks = 3 + (2 if far is not None else 0)

    def kernel(*refs):
        bias_ref, w_ref, out_ref = refs[-3:]

        def write(x_ref):
            out_ref[...] = (dot_nn(x_ref[...], w_ref[...]) + bias_ref[...]).astype(bf16)

        if far is None:
            write(refs[0])
        else:
            pl.when(pl.program_id(0) < 3)(lambda: write(refs[0]))
            pl.when(pl.program_id(0) >= 3)(lambda: write(refs[1]))

    def column(n):
        return jnp.where(n < 3, n, n - 2)

    rows = [own] if far is None else [own, far]
    return pl.pallas_call(
        kernel,
        grid=(blocks,),
        in_specs=[pl.BlockSpec((tokens, wide), lambda n: (0, 0))] * len(rows)
        + [
            pl.BlockSpec((1, local), lambda n: (0, column(n))),
            pl.BlockSpec((wide, local), lambda n: (0, column(n))),
        ],
        out_specs=pl.BlockSpec((tokens, local), lambda n: (0, n)),
        out_shape=jax.ShapeDtypeStruct((tokens, blocks * local), bf16),
        compiler_params=pltpu.CompilerParams(vmem_limit_bytes=40 << 20),
        cost_estimate=HINT,
        name="project",
    )(*rows, bias, weight)


def expand(own, other, weight, bias):
    size, wide = own.shape
    hidden = weight.shape[1]
    cut = 512
    part = 128

    def kernel(own_ref, other_ref, w_ref, b_ref, h_ref, s_ref):
        for i, x_ref in enumerate((own_ref, other_ref)):
            for r in range(0, size, part):
                pre = dot_nn(x_ref[r : r + part, :], w_ref[...]) + b_ref[...]
                phi = 0.5 * (1.0 + lax.erf(pre * (2.0**-0.5)))
                bell = jnp.exp(-0.5 * pre * pre) * (0.5 / jnp.pi) ** 0.5
                to = slice(i * size + r, i * size + r + part)
                h_ref[to, :] = (pre * phi).astype(bf16)
                s_ref[to, :] = (phi + pre * bell).astype(bf16)

    block = pl.BlockSpec((2 * size, cut), lambda n: (0, n))
    shape = jax.ShapeDtypeStruct((2 * size, hidden), bf16)
    return pl.pallas_call(
        kernel,
        grid=(hidden // cut,),
        in_specs=[
            pl.BlockSpec((size, wide), lambda n: (0, 0)),
            pl.BlockSpec((size, wide), lambda n: (0, 0)),
            pl.BlockSpec((wide, cut), lambda n: (0, n)),
            pl.BlockSpec((1, cut), lambda n: (0, n)),
        ],
        out_specs=[block, block],
        out_shape=[shape, shape],
        compiler_params=pltpu.CompilerParams(vmem_limit_bytes=40 << 20),
        cost_estimate=HINT,
        name="expand",
    )(own, other, weight, bias)


def back_hidden(loss, weight, slope):
    tokens, wide = loss.shape
    hidden = weight.shape[0]
    cut = 512

    def kernel(x_ref, w_ref, s_ref, out_ref):
        grad = dot_nt(x_ref[...], w_ref[...])
        out_ref[...] = (grad * s_ref[...].astype(f32)).astype(bf16)

    block = pl.BlockSpec((tokens, cut), lambda n: (0, n))
    return pl.pallas_call(
        kernel,
        grid=(hidden // cut,),
        in_specs=[
            pl.BlockSpec((tokens, wide), lambda n: (0, 0)),
            pl.BlockSpec((cut, wide), lambda n: (n, 0)),
            block,
        ],
        out_specs=block,
        out_shape=jax.ShapeDtypeStruct((tokens, hidden), bf16),
        compiler_params=pltpu.CompilerParams(vmem_limit_bytes=40 << 20),
        cost_estimate=HINT,
        name="back_hidden",
    )(loss, weight, slope)


class Ring:
    def __init__(self, own, half_axis, context, inner):
        size = own.shape[half_axis] // 2
        self.own = own
        self.inner = inner
        self.part = lax.dynamic_slice_in_dim(own, context * size, size, half_axis)

    def first(self, *waits):
        part = gate(self.part, *waits)
        self.one = lax.ppermute(part, "fsdp", [(0, 1), (1, 0), (2, 3), (3, 2)])
        self.across = lax.ppermute(part, "fsdp", [(1, 2), (2, 1)])

    def second(self, *waits):
        self.one, across, *_ = lax.optimization_barrier((self.one, self.across, *waits))
        self.y_one = lax.ppermute(self.one, "ctx", SWAP_Y)
        outward = lax.ppermute(across, "fsdp", [(1, 0), (2, 3)])
        self.back = lax.ppermute(self.one, "fsdp", [(1, 2), (2, 1)])
        self.two = jnp.where(self.inner, across, outward)

    def third(self, *waits):
        self.two, back, self.y_one, *_ = lax.optimization_barrier(
            (self.two, self.back, self.y_one, *waits)
        )
        self.y_two = lax.ppermute(self.two, "ctx", SWAP_Y)
        outward = lax.ppermute(back, "fsdp", [(1, 0), (2, 3)])
        self.three = jnp.where(self.inner, back, outward)

    def fourth(self, *waits):
        self.three, self.y_two, *_ = lax.optimization_barrier((self.three, self.y_two, *waits))
        self.y_three = lax.ppermute(self.three, "ctx", SWAP_Y)

    def pieces(self):
        return (
            self.own,
            self.one,
            self.y_one,
            self.two,
            self.y_two,
            self.three,
            self.y_three,
        )


def matmul(rows, half, weight, cut, dtype, flipped, count=None):
    summed = rows.shape[1]
    steps = summed // cut
    wide = count or (weight.shape[0] if flipped else weight.shape[1])
    size = rows.shape[0] // 2 if half is not None else rows.shape[0]

    def kernel(half_ref, x_ref, w_ref, out_ref, *acc):
        part = dot_nt(x_ref[...], w_ref[...]) if flipped else dot_nn(x_ref[...], w_ref[...])
        if steps == 1:
            out_ref[...] = part.astype(dtype)
            return
        step = pl.program_id(0)

        @pl.when(step == 0)
        def _():
            acc[0][...] = part

        @pl.when((step > 0) & (step < steps - 1))
        def _():
            acc[0][...] += part

        @pl.when(step == steps - 1)
        def _():
            out_ref[...] = (acc[0][...] + part).astype(dtype)

    if flipped:
        w_spec = pl.BlockSpec((wide, cut), lambda k, h: (0, k))
    else:
        w_spec = pl.BlockSpec((cut, wide), lambda k, h: (k, 0))
    return pl.pallas_call(
        kernel,
        grid_spec=pltpu.PrefetchScalarGridSpec(
            num_scalar_prefetch=1,
            grid=(steps,),
            in_specs=[pl.BlockSpec((size, cut), lambda k, h: (h[0], k)), w_spec],
            out_specs=pl.BlockSpec((size, wide), lambda k, h: (0, 0)),
            scratch_shapes=[pltpu.VMEM((size, wide), f32)] if steps > 1 else [],
        ),
        out_shape=jax.ShapeDtypeStruct((size, wide), dtype),
        compiler_params=pltpu.CompilerParams(vmem_limit_bytes=48 << 20),
        cost_estimate=HINT,
        name="matmul",
    )(jnp.zeros((1,), jnp.int32) if half is None else half, rows, weight)


def back_attend(core, own, other, weight):
    size = own.shape[0]
    local = weight.shape[0]

    def kernel(core_ref, own_ref, other_ref, w_ref, out_ref):
        w = w_ref[...]
        mine = pl.multiple_of(core_ref[0] * size, size)
        theirs = pl.multiple_of((1 - core_ref[0]) * size, size)
        out_ref[pl.ds(mine, size), :] = dot_nt(own_ref[...], w).astype(bf16)
        out_ref[pl.ds(theirs, size), :] = dot_nt(other_ref[...], w).astype(bf16)

    whole = pl.BlockSpec(memory_space=pltpu.VMEM)
    return pl.pallas_call(
        kernel,
        grid_spec=pltpu.PrefetchScalarGridSpec(
            num_scalar_prefetch=1, grid=(), in_specs=[whole] * 3, out_specs=whole
        ),
        out_shape=jax.ShapeDtypeStruct((2 * size, local), bf16),
        compiler_params=pltpu.CompilerParams(vmem_limit_bytes=32 << 20),
        cost_estimate=HINT,
        name="back_attend",
    )(core, own, other, weight)


def gate(value, *waits):
    if not waits:
        return value
    return lax.optimization_barrier((value,) + waits)[0]


def make_body(ctx_size):
    pair_ctx = ctx_size == 2

    def body(
        inputs,
        loss_sensitivity,
        parent_block,
        adapter_of,
        w_qkv,
        bias_qv,
        w_o,
        exit_offsets,
        ln_gain,
        ln_bias,
        w_in,
        hidden_offset_frozen,
        w_out,
        a_attn,
        b_attn,
        a_up,
        b_up,
        a_down,
        b_down,
    ):
        group = lax.axis_index("fsdp")
        context = lax.axis_index("ctx")
        tensor = lax.axis_index("tp")
        core = tensor % 2
        tokens, width = inputs.shape
        half = tokens // 2
        local = w_qkv.shape[2]
        shard = w_qkv.shape[1]
        hidden_local = w_in.shape[1]
        heads = local // HD
        blocks = tokens // BLOCK
        scale = HD ** (-0.5)
        wide = width + AUG

        def on(value, axis, pairs):
            return lax.ppermute(value, axis, pairs)

        def own_rows(matrix):
            return lax.dynamic_slice_in_dim(matrix, core * half, half, 0)

        def other_rows(matrix):
            return lax.dynamic_slice_in_dim(matrix, (1 - core) * half, half, 0)

        def natural(own, other):
            return jnp.concatenate(
                [jnp.where(core == 0, own, other), jnp.where(core == 0, other, own)], axis=0
            )

        def local_lanes(matrix):
            return lax.dynamic_slice_in_dim(matrix, tensor * local, local, matrix.ndim - 1)

        def put(buffer, piece, row, column):
            return lax.dynamic_update_slice(buffer, piece, (row, column))

        swap_y = [(0, 1), (1, 0)]
        spot = jnp.stack([group, context]).astype(jnp.int32)

        def send_tp(other_low, own_low):
            got = on(other_low, "tp", CORE_SWAP)
            mine = round_low(own_low.astype(f32) + got.astype(f32))
            return mine, on(mine, "tp", X_SWAP)

        def sum_sent(sent, waits=()):
            mine, far = sent
            return mine.astype(f32) + gate(far, *waits).astype(f32)

        pair = lax.dynamic_slice_in_dim(adapter_of, group * SLOTS, SLOTS)

        def pick_pair(array, axis):
            return jnp.concatenate(
                [lax.dynamic_slice_in_dim(array, pair[s], 1, axis) for s in range(SLOTS)], axis
            )

        a_pair = jnp.swapaxes(pick_pair(a_attn, 1), 2, 3)
        def down_up_pad(matrix, before=0):
            return jnp.pad(matrix, ((before, AUG - before - matrix.shape[0]), (0, 0)))

        a_qkv_rows = down_up_pad(a_pair[:3].reshape(3 * PAIR, width).astype(bf16))
        a_o_rows = local_lanes(a_pair[3].reshape(PAIR, width)).astype(bf16)
        b_pair = pick_pair(b_attn, 1)
        b_qkv_rows = local_lanes(b_pair[:3]).reshape(3, PAIR, local).astype(bf16)
        b_o_rows = down_up_pad(b_pair[3].reshape(PAIR, width).astype(bf16), PAIR)
        a_up_rows = down_up_pad(
            jnp.swapaxes(pick_pair(a_up, 0), 1, 2).reshape(PAIR, width).astype(bf16)
        )
        b_up_rows = pick_pair(b_up, 0).reshape(PAIR, hidden_local).astype(bf16)
        a_down_rows = (
            jnp.swapaxes(pick_pair(a_down, 0), 1, 2).reshape(PAIR, hidden_local).astype(bf16)
        )
        b_down_rows = down_up_pad(pick_pair(b_down, 0).reshape(PAIR, width).astype(bf16))

        def bias_lanes(opened):
            count = opened.shape[1]
            block = jnp.arange(count * BLOCK, dtype=jnp.int32) // BLOCK
            hit = opened[:, :, None] & (block[None, None, :] == jnp.arange(count)[None, :, None])
            return jnp.where(jnp.any(hit, axis=1), 0.0, neg_fill).astype(f32)

        reach, slot = ancestry(parent_block[0])
        all_blocks = reach.shape[0]
        first_block = context * blocks
        far_blocks = blocks if pair_ctx else all_blocks
        reach_rows = lax.dynamic_slice_in_dim(reach, first_block, blocks, 0)
        block_ids = jnp.arange(far_blocks, dtype=jnp.int32)
        far_open = (reach_rows[:, :far_blocks] > 0.5) & (block_ids[None, :] < first_block)
        own_open = lax.dynamic_slice_in_dim(reach_rows, first_block, blocks, 1) > 0.5
        far_bias = bias_lanes(far_open)
        own_bias = bias_lanes(own_open)

        slots = lax.dynamic_slice_in_dim(slot, first_block, blocks).astype(jnp.int32)
        lane_slot = (jnp.arange(AUG, dtype=jnp.int32) // RANK) % SLOTS

        def picks(first_row, count):
            block = (jnp.arange(count, dtype=jnp.int32) + first_row) // BLOCK
            row_slot = jnp.sum(
                jnp.where(block[:, None] == jnp.arange(blocks)[None, :], slots[None, :], 0), axis=1
            )
            return (row_slot[:, None] == lane_slot[None, :]).astype(f32)

        pick_own = picks(core * half, half)

        gain_one, shift_one = ln_gain[0][None, :], ln_bias[0][None, :]
        gain_two, shift_two = ln_gain[1][None, :], ln_bias[1][None, :]

        def widen(low, tail):
            return jnp.concatenate([low, tail], axis=1)

        normed_wide = norm_wide(
            [inputs], jnp.arange(4, dtype=jnp.int32), slots, a_qkv_rows, gain_one, shift_one, tokens
        )
        q_aug = jnp.concatenate(
            [jnp.pad(b_qkv_rows[i], ((0, 0), (i * local, (2 - i) * local))) for i in range(3)]
            + [jnp.zeros((AUG - 3 * PAIR, 3 * local), bf16)],
            axis=0,
        )
        o_aug = down_up_pad(a_o_rows, PAIR).T
        in_aug = down_up_pad(b_up_rows)
        out_aug = down_up_pad(a_down_rows).T
        if pair_ctx:
            quarter = tokens // 4
            sent = lax.dynamic_slice_in_dim(inputs, tensor * quarter, quarter, 0)
            far_quarter = on(sent, "ctx", [(0, 1)])

            far_places = jnp.stack([tensor, tensor ^ 2, tensor ^ 1, tensor ^ 3]).astype(jnp.int32)
            inner = (group == 1) | (group == 2)
            q_ring = Ring(w_qkv, 1, context, inner)
            o_ring = Ring(w_o, 0, context, inner)
            in_ring = Ring(w_in, 0, context, inner)
            out_ring = Ring(w_out, 0, context, inner)
            q_ring.first()
            q_ring.second()
            q_ring.third(far_quarter)
            far_quarter, _ = lax.optimization_barrier((far_quarter, q_ring.two))
            far_x = on(far_quarter, "tp", X_SWAP)
            far_core = on(far_quarter, "tp", CORE_SWAP)
            o_ring.first(q_ring.two)
            far_x, far_core, normed_wide, _ = lax.optimization_barrier(
                (far_x, far_core, normed_wide, q_ring.three)
            )
            q_ring.fourth(normed_wide, o_ring.one, o_ring.across)
            far_both = on(far_x, "tp", CORE_SWAP)
            o_ring.second(q_ring.three)
            in_ring.first(o_ring.two, o_ring.back)
            far_wide = norm_wide(
                [far_quarter, far_x, far_core, far_both],
                far_places,
                slot[:blocks].astype(jnp.int32),
                a_qkv_rows,
                gain_one,
                shift_one,
                tokens,
            )
            o_ring.third(far_wide, q_ring.y_three)
            q_full = assemble(
                gate(spot, o_ring.two, far_wide),
                q_ring.pieces(),
                q_aug,
                wide,
                3 * local,
                ("rows", shard, shard // 2),
                3,
            )
        else:
            own_q = jnp.transpose(w_qkv, (1, 0, 2)).reshape(shard, 3 * local)
            q_full = jnp.concatenate([lax.all_gather(own_q, "fsdp", axis=0, tiled=True), q_aug], 0)
            o_full = jnp.concatenate([lax.all_gather(w_o, "fsdp", axis=1, tiled=True), o_aug], 1)
            in_full = jnp.concatenate([lax.all_gather(w_in, "fsdp", axis=0, tiled=True), in_aug], 0)
            out_full = jnp.concatenate(
                [lax.all_gather(w_out, "fsdp", axis=1, tiled=True), out_aug], 1
            )

        normed, reduced_qkv = normed_wide[:, :width], normed_wide[:, width:]
        zero_bias = jnp.zeros((local,), f32)
        q_bias = jnp.concatenate([bias_qv[0], zero_bias, bias_qv[1]])[None, :]
        if pair_ctx:
            qkv = project(normed_wide, far_wide, q_full, q_bias, local)
            far_kv = qkv
            far_base = 3 * heads
            qkv, _, _, _ = lax.optimization_barrier(
                (qkv, in_ring.one, in_ring.across, o_ring.three)
            )
            in_ring.second(qkv)
            o_ring.fourth(qkv)
            far_kv = qkv
        else:
            qkv = project(normed_wide, None, q_full, q_bias, local)
            far_kv = lax.all_gather(qkv[:, local:], "ctx", axis=0, tiled=True)
            far_base = 0

        attended_f, attended, probs_far, probs_own = attend_forward(
            qkv, far_kv, far_base, far_bias, own_bias, heads, scale
        )
        if pair_ctx:
            o_full = assemble(
                gate(spot, attended, in_ring.two, in_ring.back),
                o_ring.pieces(),
                o_aug,
                local,
                wide,
                ("columns", shard, local // 2),
                0,
            )
        core_id = core.astype(jnp.int32)[None]
        other_id = 1 - core_id
        branch_sent = send_tp(
            matmul(attended, other_id, o_full, local, bf16, False),
            matmul(attended, core_id, o_full, local, bf16, False),
        )
        branch_far = branch_sent[1]
        if pair_ctx:
            in_ring.third()
            in_ring.fourth()
            out_ring.first(in_ring.three)
            branch_far = gate(branch_far, in_ring.y_three, out_ring.one, out_ring.across)
        middle, two_own = row_call(
            after_attention,
            "after_attention",
            core_id,
            slots,
            half,
            [(branch_sent[0], False), (branch_far, False), (inputs, True)],
            [exit_offsets[:1], gain_two, shift_two, b_o_rows, a_up_rows],
            [(width, f32), (wide, bf16)],
        )
        two_other = on(two_own, "tp", CORE_SWAP)

        if pair_ctx:
            out_ring.second(in_ring.y_three)
            in_full = assemble(
                gate(spot, out_ring.two, out_ring.back),
                in_ring.pieces(),
                in_aug,
                wide,
                hidden_local,
                ("rows", shard, shard // 2),
                0,
            )
        hidden, slope = expand(two_own, two_other, in_full, hidden_offset_frozen[None, :])
        if pair_ctx:
            out_ring.third()
            out_ring.fourth()
            out_full = assemble(
                gate(spot, hidden),
                out_ring.pieces(),
                out_aug,
                hidden_local,
                wide,
                ("columns", shard, hidden_local // 2),
                0,
            )

        loss_own = own_rows(loss_sensitivity)
        loss_rel = jnp.concatenate([loss_own, other_rows(loss_sensitivity)], axis=0)
        pick_rel = jnp.concatenate([pick_own, picks((1 - core) * half, half)], axis=0)
        grad_down_down = (factor * dot_nt(loss_rel, b_down_rows) * pick_rel).astype(bf16)
        loss_wide = widen(loss_rel, grad_down_down)
        grad_pre = back_hidden(loss_wide, out_full, slope)
        first_id = jnp.zeros((1,), jnp.int32)
        second_id = first_id + 1
        ff_cut = hidden_local // 2
        two_sent = send_tp(
            matmul(grad_pre, second_id, in_full, ff_cut, bf16, True),
            matmul(grad_pre, first_id, in_full, ff_cut, bf16, True),
        )
        late_hidden = gate(hidden, two_sent[0])
        exit_sent = send_tp(
            matmul(late_hidden, second_id, out_full, ff_cut, bf16, False),
            matmul(late_hidden, first_id, out_full, ff_cut, bf16, False),
        )
        grad_middle, back_own = row_call(
            back_middle,
            "back_middle",
            core_id,
            slots,
            half,
            [
                (two_sent[0], False),
                (gate(two_sent[1], exit_sent[0]), False),
                (middle, False),
                (loss_sensitivity, True),
            ],
            [gain_two, a_up_rows, b_o_rows],
            [(width, f32), (wide, bf16)],
        )
        back_other = on(back_own, "tp", CORE_SWAP)
        grad_attended = back_attend(core_id, back_own, back_other, o_full)

        grad_q, grad_k, grad_v, far_grad_k, far_grad_v = attend_backward(
            qkv, far_kv, far_base, grad_attended, attended_f, probs_far, probs_own, heads, scale
        )
        if pair_ctx:
            more_k = on(far_grad_k, "ctx", [(1, 0)])
            more_v = on(far_grad_v, "ctx", [(1, 0)])
        else:
            more_k = lax.psum_scatter(far_grad_k, "ctx", scatter_dimension=0, tiled=True)
            more_v = lax.psum_scatter(far_grad_v, "ctx", scatter_dimension=0, tiled=True)
        (layer_wide,) = row_call(
            after_hidden,
            "after_hidden",
            core_id,
            slots,
            half,
            [(exit_sent[0], False), (gate(exit_sent[1], more_v), False), (middle, False)],
            [exit_offsets[1:], b_down_rows],
            [(wide, bf16)],
        )
        layer_other = on(layer_wide, "tp", CORE_SWAP)
        layer_out = natural(layer_wide[:, :width], layer_other[:, :width])
        where = jnp.stack([tensor, core]).astype(jnp.int32)
        tiles = hidden_local // local
        packed = pack_terms(
            where,
            (two_own, two_other),
            (back_own, back_other),
            attended,
            grad_pre,
            hidden,
            grad_down_down,
            (layer_wide[:, width:], layer_other[:, width:]),
            loss_sensitivity,
            local,
        )
        more_k = gate(more_k, packed, layer_out)
        grad_qkv = jnp.concatenate(
            [
                grad_q,
                (grad_k.astype(f32) + more_k.astype(f32)).astype(bf16),
                (grad_v.astype(f32) + more_v.astype(f32)).astype(bf16),
            ],
            axis=1,
        )
        low_part = dot_nt(grad_qkv, q_full[width:]).astype(bf16)
        low_core = on(low_part, "tp", CORE_SWAP)
        low_pair = round_low(low_part.astype(f32) + low_core.astype(f32))
        low_far = on(low_pair, "tp", X_SWAP)
        low_sum = low_pair.astype(f32) + low_far.astype(f32)
        grad_down_qkv = (factor * low_sum * picks(0, tokens)).astype(bf16)
        qkv_cut = 3 * local // 2
        one_sent = send_tp(
            matmul(grad_qkv, other_id, q_full, qkv_cut, bf16, True, width),
            matmul(grad_qkv, core_id, q_full, qkv_cut, bf16, True, width),
        )
        tensor_id = tensor.astype(jnp.int32)[None]
        packed_qkv = pack_projections(
            gate(tensor_id, one_sent[0]), grad_down_qkv, normed_wide, grad_qkv, local
        )
        received = []
        for k in range(4):
            piece = jnp.concatenate(
                [
                    lax.dynamic_index_in_dim(packed, group ^ k, 0, keepdims=False),
                    lax.dynamic_index_in_dim(packed_qkv, group ^ k, 0, keepdims=False),
                ],
                axis=0,
            )
            received.append(on(piece, "fsdp", [(i, i ^ k) for i in range(4)]) if k else piece)
        near = jnp.stack(received)
        holder = jnp.stack([group ^ k for k in range(4)])
        owner = adapter_of.reshape(4, SLOTS)[holder].reshape(4 * SLOTS)
        if pair_ctx:
            cross = on(near, "ctx", swap_y)
            adapter_grads = unpack_terms(
                context.astype(jnp.int32)[None], owner, near, cross, tiles
            )
        else:
            adapter_grads = unpack_plain(
                context, owner, lax.psum(near.astype(f32), "ctx"), tiles, ctx_size
            )
        (grad_own,) = row_call(
            back_first,
            "back_first",
            core_id,
            slots,
            half,
            [
                (one_sent[0], False),
                (gate(one_sent[1], adapter_grads[0]), False),
                (grad_down_qkv, True),
                (inputs, True),
                (grad_middle, False),
            ],
            [gain_one, a_qkv_rows],
            [(width, bf16)],
        )
        grad_other = on(grad_own, "tp", CORE_SWAP)
        grad_inputs = natural(grad_own, grad_other)

        out_a_attn, out_b_attn, out_a_up, out_b_up, out_a_down, out_b_down = adapter_grads
        return (
            layer_out,
            grad_inputs,
            jnp.swapaxes(out_a_attn, 2, 3),
            out_b_attn,
            jnp.swapaxes(out_a_up, 1, 2),
            out_b_up,
            jnp.swapaxes(out_a_down, 1, 2),
            out_b_down,
        )

    return body


def solution(mesh):
    in_specs = (
        P(("fsdp", "ctx"), None),
        P(("fsdp", "ctx"), None),
        P("fsdp", None),
        P(),
        P(None, "fsdp", "tp"),
        P(None, "tp"),
        P("tp", "fsdp"),
        P(),
        P(),
        P(),
        P("fsdp", "tp"),
        P("tp"),
        P("tp", "fsdp"),
        P(),
        P(),
        P(),
        P(None, None, "tp"),
        P(None, "tp", None),
        P(),
    )
    out_specs = (
        P(("fsdp", "ctx"), None),
        P(("fsdp", "ctx"), None),
        P(None, None, ("tp", "fsdp", "ctx"), None),
        P(None, None, None, ("tp", "fsdp", "ctx")),
        P(None, ("tp", "fsdp", "ctx"), None),
        P(None, None, ("tp", "fsdp", "ctx")),
        P(None, ("tp", "fsdp", "ctx"), None),
        P(None, None, ("tp", "fsdp", "ctx")),
    )
    return jax.shard_map(
        make_body(mesh.shape["ctx"]),
        mesh=mesh,
        in_specs=in_specs,
        out_specs=out_specs,
        check_vma=False,
    )
```

```python
import jax
import jax.numpy as jnp
from jax import lax
from jax.experimental import pallas as pl
from jax.experimental.pallas import tpu as pltpu
from jax.sharding import PartitionSpec as P

HD = 128
RANK = 16
ADAPTERS = 8
SLOTS = 2
PAIR = SLOTS * RANK
BLOCK = 256
AUG = 128
ROW_CHUNK = 128
HINT = pl.CostEstimate(flops=1, transcendentals=0, bytes_accessed=1)

layer_eps = 1e-05
factor = 0.5
neg_fill = -1e30
bf16 = jnp.bfloat16
f32 = jnp.float32

CORE_SWAP = [(0, 1), (1, 0), (2, 3), (3, 2)]
SWAP_Y = [(0, 1), (1, 0)]
X_SWAP = [(0, 2), (2, 0), (1, 3), (3, 1)]


def dot_nn(a, b):
    return lax.dot_general(a, b, (((1,), (0,)), ((), ())), preferred_element_type=f32)


def dot_nt(a, b):
    return lax.dot_general(a, b, (((1,), (1,)), ((), ())), preferred_element_type=f32)


def dot_tn(a, b):
    return lax.dot_general(a, b, (((0,), (0,)), ((), ())), preferred_element_type=f32)


def round_low(v):
    return lax.reduce_precision(v, 8, 7).astype(bf16)


def standardize(rows):
    centre = rows - jnp.mean(rows, axis=-1, keepdims=True)
    spread = jnp.mean(centre * centre, axis=-1, keepdims=True)
    inverse = lax.rsqrt(spread + layer_eps)
    return centre * inverse, inverse


def norm_back(grad_scaled, unit, inverse):
    first = jnp.mean(grad_scaled, axis=-1, keepdims=True)
    second = jnp.mean(grad_scaled * unit, axis=-1, keepdims=True)
    return inverse * (grad_scaled - first - unit * second)


def ancestry(parents):
    total = parents.shape[0]
    position = jnp.arange(total, dtype=jnp.int32)
    reach = (
        (parents[:, None] == position[None, :]) | (position[:, None] == position[None, :])
    ).astype(f32)
    span = 1
    while span < total:
        reach = jnp.minimum(jnp.sum(reach[:, :, None] * reach[None, :, :], axis=1), 1.0)
        span *= 2
    roots = (parents < 0).astype(f32)
    order = jnp.sum(jnp.where(position[None, :] <= position[:, None], roots[None, :], 0.0), axis=1)
    slot = jnp.sum(reach * (roots * (order - 1.0))[None, :], axis=1)
    return reach, slot


def attend_forward(qkv, far, far_base, far_bias, own_bias, heads, scale):
    tokens = qkv.shape[0]
    far_rows = far.shape[0]
    blocks = tokens // BLOCK

    def kernel(q_ref, k_ref, v_ref, fk_ref, fv_ref, fb_ref, ob_ref, o_ref, low_ref, pf_ref, po_ref):
        far_k = fk_ref[...]
        far_v = fv_ref[...]
        for b in range(blocks):
            rows = slice(b * BLOCK, (b + 1) * BLOCK)
            width = (b + 1) * BLOCK
            q = q_ref[rows, :]
            s_far = dot_nt(q, far_k) * scale + fb_ref[b : b + 1, :]
            s_own = dot_nt(q, k_ref[:width, :]) * scale + ob_ref[b : b + 1, :width]
            q_pos = lax.broadcasted_iota(jnp.int32, (BLOCK, width), 0) + b * BLOCK
            k_pos = lax.broadcasted_iota(jnp.int32, (BLOCK, width), 1)
            s_own = jnp.where(k_pos <= q_pos, s_own, neg_fill)
            top = jnp.maximum(
                jnp.max(s_far, axis=1, keepdims=True), jnp.max(s_own, axis=1, keepdims=True)
            )
            p_far = jnp.exp(s_far - top)
            p_own = jnp.exp(s_own - top)
            total = jnp.sum(p_far, axis=1, keepdims=True) + jnp.sum(p_own, axis=1, keepdims=True)
            inverse = 1.0 / total
            p_far = (p_far * inverse).astype(bf16)
            p_own = (p_own * inverse).astype(bf16)
            pf_ref[0, rows, :] = p_far
            po_ref[0, rows, :width] = p_own
            mixed = dot_nn(p_far, far_v) + dot_nn(p_own, v_ref[:width, :])
            o_ref[rows, :] = mixed
            low_ref[rows, :] = mixed.astype(bf16)

    return pl.pallas_call(
        kernel,
        grid=(heads,),
        in_specs=[
            pl.BlockSpec((tokens, HD), lambda h: (0, h)),
            pl.BlockSpec((tokens, HD), lambda h: (0, heads + h)),
            pl.BlockSpec((tokens, HD), lambda h: (0, 2 * heads + h)),
            pl.BlockSpec((far_rows, HD), lambda h: (0, far_base + h)),
            pl.BlockSpec((far_rows, HD), lambda h: (0, far_base + heads + h)),
            pl.BlockSpec((blocks, far_rows), lambda h: (0, 0)),
            pl.BlockSpec((blocks, tokens), lambda h: (0, 0)),
        ],
        out_specs=[
            pl.BlockSpec((tokens, HD), lambda h: (0, h)),
            pl.BlockSpec((tokens, HD), lambda h: (0, h)),
            pl.BlockSpec((1, tokens, far_rows), lambda h: (h, 0, 0)),
            pl.BlockSpec((1, tokens, tokens), lambda h: (h, 0, 0)),
        ],
        out_shape=[
            jax.ShapeDtypeStruct((tokens, heads * HD), f32),
            jax.ShapeDtypeStruct((tokens, heads * HD), bf16),
            jax.ShapeDtypeStruct((heads, tokens, far_rows), bf16),
            jax.ShapeDtypeStruct((heads, tokens, tokens), bf16),
        ],
        compiler_params=pltpu.CompilerParams(vmem_limit_bytes=(14 if far_rows == tokens else 56) << 20),
        cost_estimate=HINT,
        name="attend_forward",
    )(qkv, qkv, qkv, far, far, far_bias, own_bias)


def attend_backward(qkv, far, far_base, grad_attended, attended, probs_far, probs_own, heads, scale):
    tokens = qkv.shape[0]
    far_rows = far.shape[0]
    blocks = tokens // BLOCK

    def kernel(
        q_ref, k_ref, v_ref, fk_ref, fv_ref, g_ref, o_ref, pf_ref, po_ref,
        dq_ref, dk_ref, dv_ref, far_ref,
        dk_acc, dv_acc, dfk_acc, dfv_acc,
    ):
        far_k = fk_ref[...]
        far_v = fv_ref[...]
        for b in reversed(range(blocks)):
            first = b == blocks - 1
            rows = slice(b * BLOCK, (b + 1) * BLOCK)
            width = (b + 1) * BLOCK
            q = q_ref[rows, :]
            g = g_ref[rows, :]
            row_dot = jnp.sum(g.astype(f32) * o_ref[rows, :], axis=1, keepdims=True)
            p_far = pf_ref[0, rows, :]
            p_own = po_ref[0, rows, :width]
            d_far = (p_far.astype(f32) * (dot_nt(g, far_v) - row_dot)).astype(bf16)
            d_own = (p_own.astype(f32) * (dot_nt(g, v_ref[:width, :]) - row_dot)).astype(bf16)
            dq_ref[rows, :] = (
                (dot_nn(d_far, far_k) + dot_nn(d_own, k_ref[:width, :])) * scale
            ).astype(bf16)
            if first:
                dfk_acc[...] = dot_tn(d_far, q)
                dfv_acc[...] = dot_tn(p_far, g)
                dk_acc[...] = dot_tn(d_own, q)
                dv_acc[...] = dot_tn(p_own, g)
            else:
                dfk_acc[...] += dot_tn(d_far, q)
                dfv_acc[...] += dot_tn(p_far, g)
                dk_acc[:width, :] += dot_tn(d_own, q)
                dv_acc[:width, :] += dot_tn(p_own, g)
        dk_ref[...] = (dk_acc[...] * scale).astype(bf16)
        dv_ref[...] = dv_acc[...].astype(bf16)
        far_ref[0] = (dfk_acc[...] * scale).astype(bf16)
        far_ref[1] = dfv_acc[...].astype(bf16)

    head_spec = pl.BlockSpec((tokens, HD), lambda h: (0, h))
    far_spec = pl.BlockSpec((2, far_rows, HD), lambda h: (0, 0, h))
    own_shape = jax.ShapeDtypeStruct((tokens, heads * HD), bf16)
    far_shape = jax.ShapeDtypeStruct((2, far_rows, heads * HD), bf16)
    return pl.pallas_call(
        kernel,
        grid=(heads,),
        in_specs=[
            head_spec,
            pl.BlockSpec((tokens, HD), lambda h: (0, heads + h)),
            pl.BlockSpec((tokens, HD), lambda h: (0, 2 * heads + h)),
            pl.BlockSpec((far_rows, HD), lambda h: (0, far_base + h)),
            pl.BlockSpec((far_rows, HD), lambda h: (0, far_base + heads + h)),
            head_spec,
            head_spec,
            pl.BlockSpec((1, tokens, far_rows), lambda h: (h, 0, 0)),
            pl.BlockSpec((1, tokens, tokens), lambda h: (h, 0, 0)),
        ],
        out_specs=[head_spec, head_spec, head_spec, far_spec],
        out_shape=[own_shape, own_shape, own_shape, far_shape],
        scratch_shapes=[
            pltpu.VMEM((tokens, HD), f32),
            pltpu.VMEM((tokens, HD), f32),
            pltpu.VMEM((far_rows, HD), f32),
            pltpu.VMEM((far_rows, HD), f32),
        ],
        compiler_params=pltpu.CompilerParams(vmem_limit_bytes=(16 if far_rows == tokens else 56) << 20),
        cost_estimate=HINT,
        name="attend_backward",
    )(qkv, qkv, qkv, far, far, grad_attended, attended, probs_far, probs_own)


def assemble(spot, pieces, tail, rows, columns, step, parts, straight=False):
    direction, shard, half_rows = step
    count = max(parts, 1)
    part_columns = columns // count if parts else columns
    tail_rows, tail_columns = tail.shape

    def kernel(spot_ref, *refs):
        own, one, y_one, two, y_two, three, y_three, tail_ref, out, sem = refs
        group = spot_ref[0]
        context = spot_ref[1]
        inner = (group == 1) | (group == 2)

        def moves(piece, source, which, first):
            made = []
            for i in range(count):
                src = piece.at[i] if parts else piece
                n, m = src.shape
                if direction == "rows":
                    row = pl.multiple_of(source * shard + which * half_rows, half_rows)
                    dst = out.at[pl.ds(row, n), pl.ds(i * part_columns, m)]
                else:
                    row = pl.multiple_of(which * half_rows, half_rows)
                    col = pl.multiple_of(source * shard, shard)
                    dst = out.at[pl.ds(row, n), pl.ds(col, m)]
                made.append(pltpu.make_async_copy(src, dst, sem.at[first + i]))
            return made

        fixed = moves(own, group, 0, 0)
        fixed += moves(one, group ^ 1, context, count)
        fixed += moves(y_one, group ^ 1, 1 - context, 2 * count)
        second = group ^ 2 if straight else jnp.where(inner, group ^ 3, group ^ 2)
        third = group ^ 3 if straight else jnp.where(inner, group ^ 2, group ^ 3)
        fixed += moves(two, second, context, 3 * count)
        fixed += moves(y_two, second, 1 - context, 4 * count)
        fixed += moves(three, third, context, 5 * count)
        fixed += moves(y_three, third, 1 - context, 6 * count)
        row0 = rows - tail_rows if direction == "rows" else 0
        col0 = 0 if direction == "rows" else columns - tail_columns
        fixed.append(
            pltpu.make_async_copy(
                tail_ref,
                out.at[pl.ds(row0, tail_rows), pl.ds(col0, tail_columns)],
                sem.at[7 * count],
            )
        )
        for move in fixed:
            move.start()

        for move in fixed:
            move.wait()

    return pl.pallas_call(
        kernel,
        grid_spec=pltpu.PrefetchScalarGridSpec(
            num_scalar_prefetch=1,
            grid=(),
            in_specs=[pl.BlockSpec(memory_space=pltpu.HBM)] * 8,
            out_specs=pl.BlockSpec(memory_space=pltpu.VMEM),
            scratch_shapes=[pltpu.SemaphoreType.DMA((7 * count + 1,))],
        ),
        out_shape=jax.ShapeDtypeStruct((rows, columns), bf16),
        compiler_params=pltpu.CompilerParams(vmem_limit_bytes=4 << 20),
        cost_estimate=HINT,
        name="assemble",
    )(spot, *pieces, tail)


def norm_wide(pieces, places, slots, down_rows, gain, shift, tokens):
    width = gain.shape[1]
    blocks = tokens // BLOCK
    count = len(pieces)
    quarter = tokens // 4
    steps = 4 // count

    def kernel(place_ref, slot_ref, *refs):
        down_ref, gain_ref, shift_ref, out_ref = refs[count:]
        for i in range(4):
            x_ref = refs[i // steps]
            first = (i % steps) * quarter
            rows = x_ref[first : first + quarter, :].astype(f32)
            start = pl.multiple_of(place_ref[i] * quarter, quarter)
            unit, _ = standardize(rows)
            low = (unit * gain_ref[...] + shift_ref[...]).astype(bf16)
            block = (lax.broadcasted_iota(jnp.int32, (quarter, AUG), 0) + start) // BLOCK
            lane_slot = (lax.broadcasted_iota(jnp.int32, (quarter, AUG), 1) // RANK) % SLOTS
            slot = jnp.zeros((quarter, AUG), jnp.int32)
            for b in range(blocks):
                slot = jnp.where(block == b, slot_ref[b], slot)
            down = jnp.where(slot == lane_slot, dot_nt(low, down_ref[...]), 0.0)
            out_ref[pl.ds(start, quarter), :width] = low
            out_ref[pl.ds(start, quarter), width:] = factor * down.astype(bf16)

    whole = pl.BlockSpec(memory_space=pltpu.VMEM)
    return pl.pallas_call(
        kernel,
        grid_spec=pltpu.PrefetchScalarGridSpec(
            num_scalar_prefetch=2,
            grid=(),
            in_specs=[whole] * (count + 3),
            out_specs=whole,
        ),
        out_shape=jax.ShapeDtypeStruct((tokens, width + AUG), bf16),
        compiler_params=pltpu.CompilerParams(vmem_limit_bytes=12 << 20),
        cost_estimate=HINT,
        name="norm_wide",
    )(places, slots, *pieces, down_rows, gain, shift)


def own_pick(first_row, count, slot_ref, blocks):
    block = (lax.broadcasted_iota(jnp.int32, (count, AUG), 0) + first_row) // BLOCK
    lane_slot = (lax.broadcasted_iota(jnp.int32, (count, AUG), 1) // RANK) % SLOTS
    slot = jnp.zeros((count, AUG), jnp.int32)
    for b in range(blocks):
        slot = jnp.where(block == b, slot_ref[b], slot)
    return slot == lane_slot


def row_call(body, name, core, slots, rows, moving, fixed, outs):
    chunk = ROW_CHUNK
    steps = rows // chunk
    blocks = slots.shape[0]
    n_in = len(moving) + len(fixed)

    def kernel(core_ref, slot_ref, *refs):
        first = core_ref[0] * rows + pl.program_id(0) * chunk
        pick = own_pick(first, chunk, slot_ref, blocks)
        results = body(pick, *[r[...] for r in refs[:n_in]])
        for ref, value in zip(refs[n_in:], results):
            ref[...] = value

    specs = []
    for array, offset in moving:
        if offset:
            specs.append(
                pl.BlockSpec((chunk, array.shape[1]), lambda i, c, s: (c[0] * steps + i, 0))
            )
        else:
            specs.append(pl.BlockSpec((chunk, array.shape[1]), lambda i, c, s: (i, 0)))
    for array in fixed:
        specs.append(pl.BlockSpec(array.shape, lambda i, c, s: (0, 0)))
    return pl.pallas_call(
        kernel,
        grid_spec=pltpu.PrefetchScalarGridSpec(
            num_scalar_prefetch=2,
            grid=(steps,),
            in_specs=specs,
            out_specs=[pl.BlockSpec((chunk, c), lambda i, c_, s: (i, 0)) for c, _ in outs],
        ),
        out_shape=[jax.ShapeDtypeStruct((rows, c), d) for c, d in outs],
        compiler_params=pltpu.CompilerParams(vmem_limit_bytes=12 << 20),
        cost_estimate=HINT,
        name=name,
    )(core, slots, *[a for a, _ in moving], *fixed)


def join(mine, got):
    piece = got[0].shape[0]

    def kernel(a_ref, *refs):
        out_ref, sum_ref, sem = refs[len(got) :]
        for i, b_ref in enumerate(refs[: len(got)]):
            rows = slice(i * piece, (i + 1) * piece)
            sum_ref[rows, :] = (a_ref[rows, :].astype(f32) + b_ref[...].astype(f32)).astype(bf16)
        move = pltpu.make_async_copy(sum_ref, out_ref, sem)
        move.start()
        move.wait()

    whole = pl.BlockSpec(memory_space=pltpu.VMEM)
    return pl.pallas_call(
        kernel,
        in_specs=[whole] * (1 + len(got)),
        out_specs=pl.BlockSpec(memory_space=pltpu.HBM),
        out_shape=jax.ShapeDtypeStruct(mine.shape, bf16),
        scratch_shapes=[pltpu.VMEM(mine.shape, bf16), pltpu.SemaphoreType.DMA],
        compiler_params=pltpu.CompilerParams(vmem_limit_bytes=8 << 20),
        cost_estimate=HINT,
        name="join",
    )(mine, *got)


def back_project(grad, core, weight, width):
    tokens, summed = grad.shape
    size = tokens // 2

    def kernel(core_ref, x_ref, w_ref, other_ref, own_ref):
        part = dot_nt(x_ref[...], w_ref[...]).astype(bf16)

        @pl.when(pl.program_id(0) == 0)
        def _():
            other_ref[...] = part

        @pl.when(pl.program_id(0) == 1)
        def _():
            own_ref[...] = part

    whole = pl.BlockSpec((size, width), lambda n, c: (0, 0))
    shape = jax.ShapeDtypeStruct((size, width), bf16)
    return pl.pallas_call(
        kernel,
        grid_spec=pltpu.PrefetchScalarGridSpec(
            num_scalar_prefetch=1,
            grid=(2,),
            in_specs=[
                pl.BlockSpec((size, summed), lambda n, c: (jnp.where(n == 0, 1 - c[0], c[0]), 0)),
                pl.BlockSpec((width, summed), lambda n, c: (0, 0)),
            ],
            out_specs=[whole, whole],
        ),
        out_shape=[shape, shape],
        compiler_params=pltpu.CompilerParams(vmem_limit_bytes=26 << 20),
        cost_estimate=HINT,
        name="back_project",
    )(core, grad, weight)


def place_rows(core, own, other, width):
    size = own.shape[0]

    def kernel(core_ref, own_ref, other_ref, out_ref, sem):
        moves = []
        for n, (ref, side) in enumerate(((own_ref, core_ref[0]), (other_ref, 1 - core_ref[0]))):
            start = pl.multiple_of(side * size, size)
            moves.append(
                pltpu.make_async_copy(
                    ref.at[:, pl.ds(0, width)], out_ref.at[pl.ds(start, size), :], sem.at[n]
                )
            )
        for move in moves:
            move.start()
        for move in moves:
            move.wait()

    whole = pl.BlockSpec(memory_space=pltpu.VMEM)
    return pl.pallas_call(
        kernel,
        grid_spec=pltpu.PrefetchScalarGridSpec(
            num_scalar_prefetch=1,
            grid=(),
            in_specs=[whole] * 2,
            out_specs=pl.BlockSpec(memory_space=pltpu.HBM),
            scratch_shapes=[pltpu.SemaphoreType.DMA((2,))],
        ),
        out_shape=jax.ShapeDtypeStruct((2 * size, width), bf16),
        compiler_params=pltpu.CompilerParams(vmem_limit_bytes=8 << 20),
        cost_estimate=HINT,
        name="place_rows",
    )(core, own, other)


def after_attention(pick, mine, far, rows, exit_row, gain, shift, b_o_rows, a_up_rows):
    width = rows.shape[1]
    total = mine.astype(f32) + far.astype(f32)
    down_o = factor * jnp.where(pick, total[:, width:], 0.0).astype(bf16)
    middle = rows.astype(f32) + total[:, :width] + exit_row + dot_nn(down_o, b_o_rows)
    unit, _ = standardize(middle)
    low = (unit * gain + shift).astype(bf16)
    down_up = factor * jnp.where(pick, dot_nt(low, a_up_rows), 0.0).astype(bf16)
    return middle, jnp.concatenate([low, down_up + down_o], axis=1)


def after_hidden(pick, mine, far, middle, exit_row, b_down_rows):
    width = middle.shape[1]
    total = mine.astype(f32) + far.astype(f32)
    down = factor * jnp.where(pick, total[:, width:], 0.0).astype(bf16)
    out = middle + total[:, :width] + exit_row + dot_nn(down, b_down_rows)
    return out.astype(bf16), down


def back_middle(pick, mine, far, middle, loss, gain, a_up_rows, b_o_rows):
    width = middle.shape[1]
    total = mine.astype(f32) + far.astype(f32)
    grad_down = (factor * jnp.where(pick, total[:, width:], 0.0)).astype(bf16)
    grad_normed = total[:, :width] + dot_nn(grad_down, a_up_rows)
    unit, inverse = standardize(middle)
    grad = loss.astype(f32) + norm_back(grad_normed * gain, unit, inverse)
    low = grad.astype(bf16)
    grad_o = (factor * jnp.where(pick, dot_nt(low, b_o_rows), 0.0)).astype(bf16)
    return grad, jnp.concatenate([low, grad_o + grad_down], axis=1)


def back_first(pick, mine, far, grad_down, rows, grad_middle, gain, a_rows):
    total = mine.astype(f32) + far.astype(f32)
    grad_normed = total + dot_nn(grad_down, a_rows)
    unit, inverse = standardize(rows.astype(f32))
    return ((grad_middle + norm_back(grad_normed * gain, unit, inverse)).astype(bf16),)


def pack_terms(tensor, core, two, back, attended, grad_pre, hidden, grad_dd, local):
    width = two[0].shape[1] - AUG
    half = two[0].shape[0]
    cut = local // 4

    def kernel(t_ref, two_a, two_b, back_a, back_b, att_ref, gp_ref, hid_ref, gdd_ref, out):
        lanes = pl.ds(pl.multiple_of(t_ref[0] * local, local), local)
        mine = pl.ds(pl.multiple_of(t_ref[1] * half, half), half)
        theirs = pl.ds(pl.multiple_of((1 - t_ref[1]) * half, half), half)
        halves = ((two_a, back_a, mine), (two_b, back_b, theirs))

        def both(make):
            return make(*halves[0]) + make(*halves[1])

        terms = [
            both(lambda t, b, r: dot_tn(b[:, width:], att_ref[r, :]))[PAIR : 2 * PAIR],
            both(lambda t, b, r: dot_tn(t[:, width:], b[:, lanes]))[PAIR : 2 * PAIR],
            both(lambda t, b, r: dot_tn(b[:, width:], t[:, lanes]))[:PAIR],
        ]
        for n, term in enumerate(terms):
            low = term.astype(bf16)
            for g in range(4):
                out[g, n * PAIR : (n + 1) * PAIR, :] = low[:, g * cut : (g + 1) * cut]
        base = len(terms) * PAIR
        wide_terms = (
            dot_tn(two_a[:, width:], gp_ref[:half, :]) + dot_tn(two_b[:, width:], gp_ref[half:, :]),
            dot_tn(gdd_ref[...], hid_ref[...]),
        )
        for term in wide_terms:
            low = term[:PAIR].astype(bf16)
            tiles = low.shape[1] // (4 * cut)
            for g in range(4):
                for t in range(tiles):
                    c = (g * tiles + t) * cut
                    out[g, base + t * PAIR : base + (t + 1) * PAIR, :] = low[:, c : c + cut]
            base += tiles * PAIR

    tiles = hidden.shape[1] // local
    whole = pl.BlockSpec(memory_space=pltpu.VMEM)
    return pl.pallas_call(
        kernel,
        grid_spec=pltpu.PrefetchScalarGridSpec(
            num_scalar_prefetch=1, grid=(), in_specs=[whole] * 8, out_specs=whole
        ),
        out_shape=jax.ShapeDtypeStruct((4, (3 + 2 * tiles) * PAIR, cut), bf16),
        compiler_params=pltpu.CompilerParams(vmem_limit_bytes=24 << 20),
        cost_estimate=HINT,
        name="pack_terms",
    )(jnp.stack([tensor, core]), *two, *back, attended, grad_pre, hidden, grad_dd)


def pack_layer(tensor, core, down, loss, local):
    half = down[0].shape[0]
    cut = local // 4

    def kernel(t_ref, own_ref, other_ref, loss_ref, out, low, sem):
        lanes = pl.ds(pl.multiple_of(t_ref[0] * local, local), local)
        move = pltpu.make_async_copy(loss_ref.at[:, lanes], low, sem)
        move.start()
        move.wait()
        mine = pl.ds(pl.multiple_of(t_ref[1] * half, half), half)
        theirs = pl.ds(pl.multiple_of((1 - t_ref[1]) * half, half), half)
        term = dot_tn(own_ref[...], low[mine, :]) + dot_tn(other_ref[...], low[theirs, :])
        for g in range(4):
            out[g] = term[:PAIR, g * cut : (g + 1) * cut].astype(bf16)

    whole = pl.BlockSpec(memory_space=pltpu.VMEM)
    return pl.pallas_call(
        kernel,
        grid_spec=pltpu.PrefetchScalarGridSpec(
            num_scalar_prefetch=1,
            grid=(),
            in_specs=[whole] * 2 + [pl.BlockSpec(memory_space=pltpu.HBM)],
            out_specs=whole,
            scratch_shapes=[pltpu.VMEM((2 * half, local), bf16), pltpu.SemaphoreType.DMA],
        ),
        out_shape=jax.ShapeDtypeStruct((4, PAIR, cut), bf16),
        compiler_params=pltpu.CompilerParams(vmem_limit_bytes=4 << 20),
        cost_estimate=HINT,
        name="pack_layer",
    )(jnp.stack([tensor, core]), *down, loss)


def pack_projections(tensor, grad_down, normed_wide, grad_qkv, local):
    width = normed_wide.shape[1] - AUG
    cut = local // 4

    def kernel(t_ref, gd_ref, nw_ref, gq_ref, out):
        lanes = pl.ds(pl.multiple_of(t_ref[0] * local, local), local)
        down = dot_tn(gd_ref[...], nw_ref[:, lanes]).astype(bf16)
        up = dot_tn(nw_ref[:, width:], gq_ref[...]).astype(bf16)
        for i in range(3):
            rows = slice(i * PAIR, (i + 1) * PAIR)
            for g in range(4):
                out[g, rows, :] = down[rows, g * cut : (g + 1) * cut]
                c = i * local + g * cut
                out[g, (3 + i) * PAIR : (4 + i) * PAIR, :] = up[rows, c : c + cut]

    whole = pl.BlockSpec(memory_space=pltpu.VMEM)
    return pl.pallas_call(
        kernel,
        grid_spec=pltpu.PrefetchScalarGridSpec(
            num_scalar_prefetch=1, grid=(), in_specs=[whole] * 3, out_specs=whole
        ),
        out_shape=jax.ShapeDtypeStruct((4, 6 * PAIR, cut), bf16),
        compiler_params=pltpu.CompilerParams(vmem_limit_bytes=4 << 20),
        cost_estimate=HINT,
        name="pack_projections",
    )(tensor, grad_down, normed_wide, grad_qkv)


def unpack_terms(context, owner, near, cross, tiles):
    cut = near[0].shape[2]
    half = cut // 2

    def kernel(c_ref, owner_ref, n0, n1, c0, c1, a_attn, b_attn, a_up, b_up, a_down, b_down):
        first = c_ref[0] == 0

        for k in range(4):
            for s in range(SLOTS):
                who = owner_ref[k * SLOTS + s]

                def value(row, n_ref=n0, c_ref=c0):
                    rows = slice(row + s * RANK, row + (s + 1) * RANK)
                    return n_ref[k, rows, :].astype(f32) + c_ref[k, rows, :].astype(f32)

                def narrow(row, *refs):
                    v = value(row, *refs)
                    return jnp.where(first, v[:, :half], v[:, half:])

                for i in range(3):
                    a_attn[i, pl.ds(who, 1)] = narrow(i * PAIR, n1, c1)[None]
                    b_attn[i, pl.ds(who, 1)] = narrow((3 + i) * PAIR, n1, c1)[None]
                a_attn[3, pl.ds(who, 1)] = narrow(0)[None]
                b_attn[3, pl.ds(who, 1)] = narrow(PAIR)[None]
                a_up[pl.ds(who, 1)] = narrow(2 * PAIR)[None]
                b_down[pl.ds(who, 1)] = narrow(6 * PAIR, n1, c1)[None]
                for n, ref in enumerate((b_up, a_down)):
                    start = (3 + n * tiles) * PAIR
                    for t in range(tiles // 2):
                        ref[pl.ds(who, 1), :, t * cut : (t + 1) * cut] = jnp.where(
                            first,
                            value(start + t * PAIR),
                            value(start + (tiles // 2 + t) * PAIR),
                        )[None]

    narrow_shape = (ADAPTERS, RANK, half)
    wide_shape = (ADAPTERS, RANK, tiles * half)
    whole = pl.BlockSpec(memory_space=pltpu.VMEM)
    shapes = [(4,) + narrow_shape, (4,) + narrow_shape, narrow_shape, wide_shape, wide_shape, narrow_shape]
    return pl.pallas_call(
        kernel,
        grid_spec=pltpu.PrefetchScalarGridSpec(
            num_scalar_prefetch=2, grid=(), in_specs=[whole] * 4, out_specs=[whole] * 6
        ),
        out_shape=[jax.ShapeDtypeStruct(shape, f32) for shape in shapes],
        compiler_params=pltpu.CompilerParams(vmem_limit_bytes=4 << 20),
        cost_estimate=HINT,
        name="unpack_terms",
    )(context, owner, *near, *cross)


def unpack_plain(context, owner, total, tiles, ctx_size):
    cut = total.shape[2]
    place = (jnp.arange(ADAPTERS, dtype=jnp.int32)[:, None] == owner[None, :]).astype(f32)
    parts = total.reshape(4, -1, SLOTS, RANK, cut)
    placed = jnp.einsum("ag,ngrc->narc", place, jnp.transpose(parts, (1, 0, 2, 3, 4)).reshape(
        parts.shape[1], 4 * SLOTS, RANK, cut), precision=lax.Precision.HIGHEST)

    def narrow(items):
        size = items.shape[-1] // ctx_size
        return lax.dynamic_slice_in_dim(items, context * size, size, items.ndim - 1)

    def broad(items):
        joined = jnp.transpose(items, (1, 2, 0, 3)).reshape(ADAPTERS, RANK, -1)
        return narrow(joined)

    base = 3 + 2 * tiles
    return (
        narrow(jnp.concatenate([placed[base : base + 3], placed[:1]])),
        narrow(jnp.concatenate([placed[base + 3 : base + 6], placed[1:2]])),
        narrow(placed[2]),
        broad(placed[3 : 3 + tiles]),
        broad(placed[3 + tiles : base]),
        narrow(placed[base + 6]),
    )


def project(own, far, weight, bias, local):
    tokens, wide = own.shape
    blocks = 3 + (2 if far is not None else 0)

    def kernel(*refs):
        bias_ref, w_ref, out_ref = refs[-3:]

        def write(x_ref):
            out_ref[...] = (dot_nn(x_ref[...], w_ref[...]) + bias_ref[...]).astype(bf16)

        if far is None:
            write(refs[0])
        else:
            pl.when(pl.program_id(0) < 3)(lambda: write(refs[0]))
            pl.when(pl.program_id(0) >= 3)(lambda: write(refs[1]))

    def column(n):
        return jnp.where(n < 3, n, n - 2)

    rows = [own] if far is None else [own, far]
    return pl.pallas_call(
        kernel,
        grid=(blocks,),
        in_specs=[pl.BlockSpec((tokens, wide), lambda n: (0, 0))] * len(rows)
        + [
            pl.BlockSpec((1, local), lambda n: (0, column(n))),
            pl.BlockSpec((wide, local), lambda n: (0, column(n))),
        ],
        out_specs=pl.BlockSpec((tokens, local), lambda n: (0, n)),
        out_shape=jax.ShapeDtypeStruct((tokens, blocks * local), bf16),
        compiler_params=pltpu.CompilerParams(vmem_limit_bytes=12 << 20),
        cost_estimate=HINT,
        name="project",
    )(*rows, bias, weight)


def expand(own, other, weight, bias):
    size, wide = own.shape
    hidden = weight.shape[1]
    cut = 512
    part = 128

    def kernel(own_ref, other_ref, w_ref, b_ref, h_ref, s_ref):
        for i, x_ref in enumerate((own_ref, other_ref)):
            for r in range(0, size, part):
                pre = dot_nn(x_ref[r : r + part, :], w_ref[...]) + b_ref[...]
                phi = 0.5 * (1.0 + lax.erf(pre * (2.0**-0.5)))
                bell = jnp.exp(-0.5 * pre * pre) * (0.5 / jnp.pi) ** 0.5
                to = slice(i * size + r, i * size + r + part)
                h_ref[to, :] = (pre * phi).astype(bf16)
                s_ref[to, :] = (phi + pre * bell).astype(bf16)

    block = pl.BlockSpec((2 * size, cut), lambda n: (0, n))
    shape = jax.ShapeDtypeStruct((2 * size, hidden), bf16)
    return pl.pallas_call(
        kernel,
        grid=(hidden // cut,),
        in_specs=[
            pl.BlockSpec((size, wide), lambda n: (0, 0)),
            pl.BlockSpec((size, wide), lambda n: (0, 0)),
            pl.BlockSpec((wide, cut), lambda n: (0, n)),
            pl.BlockSpec((1, cut), lambda n: (0, n)),
        ],
        out_specs=[block, block],
        out_shape=[shape, shape],
        compiler_params=pltpu.CompilerParams(vmem_limit_bytes=14 << 20),
        cost_estimate=HINT,
        name="expand",
    )(own, other, weight, bias)


def back_hidden(loss, weight, slope):
    tokens, wide = loss.shape
    hidden = weight.shape[0]
    cut = 512

    def kernel(x_ref, w_ref, s_ref, out_ref):
        grad = dot_nt(x_ref[...], w_ref[...])
        out_ref[...] = (grad * s_ref[...].astype(f32)).astype(bf16)

    block = pl.BlockSpec((tokens, cut), lambda n: (0, n))
    return pl.pallas_call(
        kernel,
        grid=(hidden // cut,),
        in_specs=[
            pl.BlockSpec((tokens, wide), lambda n: (0, 0)),
            pl.BlockSpec((cut, wide), lambda n: (n, 0)),
            block,
        ],
        out_specs=block,
        out_shape=jax.ShapeDtypeStruct((tokens, hidden), bf16),
        compiler_params=pltpu.CompilerParams(vmem_limit_bytes=14 << 20),
        cost_estimate=HINT,
        name="back_hidden",
    )(loss, weight, slope)


class Direct:
    def __init__(self, own, half_axis, context):
        size = own.shape[half_axis] // 2
        self.own = own
        self.part = lax.dynamic_slice_in_dim(own, context * size, size, half_axis)

    def first(self, *waits):
        part = gate(self.part, *waits)
        self.near = [
            lax.ppermute(part, "fsdp", [(i, i ^ k) for i in range(4)]) for k in range(1, 4)
        ]

    def second(self, *waits):
        *self.near, _ = lax.optimization_barrier((*self.near, waits))
        self.far = [lax.ppermute(piece, "ctx", SWAP_Y) for piece in self.near]

    def pieces(self):
        return (self.own, *[p for pair in zip(self.near, self.far) for p in pair])


class Ring:
    def __init__(self, own, half_axis, context, inner):
        size = own.shape[half_axis] // 2
        self.own = own
        self.inner = inner
        self.part = lax.dynamic_slice_in_dim(own, context * size, size, half_axis)

    def first(self, *waits):
        part = gate(self.part, *waits)
        self.one = lax.ppermute(part, "fsdp", [(0, 1), (1, 0), (2, 3), (3, 2)])
        self.across = lax.ppermute(part, "fsdp", [(1, 2), (2, 1)])

    def second(self, *waits):
        self.one, self.across, *_ = lax.optimization_barrier((self.one, self.across, *waits))
        self.y_one = lax.ppermute(self.one, "ctx", SWAP_Y)
        self.outward = lax.ppermute(self.across, "fsdp", [(1, 0), (2, 3)])
        self.back = lax.ppermute(self.one, "fsdp", [(1, 2), (2, 1)])

    def third(self, *waits):
        outward, self.back, self.y_one, across, *_ = lax.optimization_barrier(
            (self.outward, self.back, self.y_one, self.across, *waits)
        )
        self.two = jnp.where(self.inner, across, outward)
        self.y_two = lax.ppermute(self.two, "ctx", SWAP_Y)
        self.last = lax.ppermute(self.back, "fsdp", [(1, 0), (2, 3)])

    def fourth(self, *waits):
        last, self.y_two, back, *_ = lax.optimization_barrier(
            (self.last, self.y_two, self.back, *waits)
        )
        self.three = jnp.where(self.inner, back, last)
        self.y_three = lax.ppermute(self.three, "ctx", SWAP_Y)

    def pieces(self):
        return (
            self.own,
            self.one,
            self.y_one,
            self.two,
            self.y_two,
            self.three,
            self.y_three,
        )


def matmul(rows, half, weight, cut, flipped, parts=1):
    summed = rows.shape[1]
    steps = summed // cut
    wide = weight.shape[0] if flipped else weight.shape[1]
    size = rows.shape[0] // 2
    piece = size // parts

    def kernel(half_ref, x_ref, w_ref, *refs):
        outs = refs[:parts]
        part = dot_nt(x_ref[...], w_ref[...]) if flipped else dot_nn(x_ref[...], w_ref[...])

        def finish(total):
            for i, out_ref in enumerate(outs):
                out_ref[...] = total[i * piece : (i + 1) * piece].astype(bf16)

        if steps == 1:
            finish(part)
            return
        acc = refs[parts]
        step = pl.program_id(0)

        @pl.when(step == 0)
        def _():
            acc[...] = part

        @pl.when((step > 0) & (step < steps - 1))
        def _():
            acc[...] += part

        @pl.when(step == steps - 1)
        def _():
            finish(acc[...] + part)

    if flipped:
        w_spec = pl.BlockSpec((wide, cut), lambda k, h: (0, k))
    else:
        w_spec = pl.BlockSpec((cut, wide), lambda k, h: (k, 0))
    return pl.pallas_call(
        kernel,
        grid_spec=pltpu.PrefetchScalarGridSpec(
            num_scalar_prefetch=1,
            grid=(steps,),
            in_specs=[pl.BlockSpec((size, cut), lambda k, h: (h[0], k)), w_spec],
            out_specs=[pl.BlockSpec((piece, wide), lambda k, h: (0, 0))] * parts,
            scratch_shapes=[pltpu.VMEM((size, wide), f32)] if steps > 1 else [],
        ),
        out_shape=[jax.ShapeDtypeStruct((piece, wide), bf16)] * parts,
        compiler_params=pltpu.CompilerParams(vmem_limit_bytes=22 << 20),
        cost_estimate=HINT,
        name="matmul",
    )(half, rows, weight)


def back_attend(core, own, other, weight):
    size = own.shape[0]
    local = weight.shape[0]

    def kernel(core_ref, own_ref, other_ref, w_ref, out_ref):
        w = w_ref[...]
        mine = pl.multiple_of(core_ref[0] * size, size)
        theirs = pl.multiple_of((1 - core_ref[0]) * size, size)
        out_ref[pl.ds(mine, size), :] = dot_nt(own_ref[...], w).astype(bf16)
        out_ref[pl.ds(theirs, size), :] = dot_nt(other_ref[...], w).astype(bf16)

    whole = pl.BlockSpec(memory_space=pltpu.VMEM)
    return pl.pallas_call(
        kernel,
        grid_spec=pltpu.PrefetchScalarGridSpec(
            num_scalar_prefetch=1, grid=(), in_specs=[whole] * 3, out_specs=whole
        ),
        out_shape=jax.ShapeDtypeStruct((2 * size, local), bf16),
        compiler_params=pltpu.CompilerParams(vmem_limit_bytes=6 << 20),
        cost_estimate=HINT,
        name="back_attend",
    )(core, own, other, weight)


def gate(value, *waits):
    if not waits:
        return value
    return lax.optimization_barrier((value,) + waits)[0]


def make_body(ctx_size):
    pair_ctx = ctx_size == 2

    def body(
        inputs,
        loss_sensitivity,
        parent_block,
        adapter_of,
        w_qkv,
        bias_qv,
        w_o,
        exit_offsets,
        ln_gain,
        ln_bias,
        w_in,
        hidden_offset_frozen,
        w_out,
        a_attn,
        b_attn,
        a_up,
        b_up,
        a_down,
        b_down,
    ):
        group = lax.axis_index("fsdp")
        context = lax.axis_index("ctx")
        tensor = lax.axis_index("tp")
        core = tensor % 2
        tokens, width = inputs.shape
        half = tokens // 2
        local = w_qkv.shape[2]
        shard = w_qkv.shape[1]
        hidden_local = w_in.shape[1]
        heads = local // HD
        blocks = tokens // BLOCK
        scale = HD ** (-0.5)
        wide = width + AUG

        def on(value, axis, pairs):
            return lax.ppermute(value, axis, pairs)

        def own_rows(matrix):
            return lax.dynamic_slice_in_dim(matrix, core * half, half, 0)

        def other_rows(matrix):
            return lax.dynamic_slice_in_dim(matrix, (1 - core) * half, half, 0)

        def natural(own, other):
            return jnp.concatenate(
                [jnp.where(core == 0, own, other), jnp.where(core == 0, other, own)], axis=0
            )

        def local_lanes(matrix):
            return lax.dynamic_slice_in_dim(matrix, tensor * local, local, matrix.ndim - 1)

        def put(buffer, piece, row, column):
            return lax.dynamic_update_slice(buffer, piece, (row, column))

        swap_y = [(0, 1), (1, 0)]
        spot = jnp.stack([group, context]).astype(jnp.int32)

        def send_tp(others, own_low, *waits):
            mine = join(own_low, [on(other, "tp", CORE_SWAP) for other in others])
            return mine, on(gate(mine, *waits), "tp", X_SWAP)

        def sum_sent(sent, waits=()):
            mine, far = sent
            return mine.astype(f32) + gate(far, *waits).astype(f32)

        pair = lax.dynamic_slice_in_dim(adapter_of, group * SLOTS, SLOTS)

        def pick_pair(array, axis):
            return jnp.concatenate(
                [lax.dynamic_slice_in_dim(array, pair[s], 1, axis) for s in range(SLOTS)], axis
            )

        a_pair = jnp.swapaxes(pick_pair(a_attn, 1), 2, 3)
        def down_up_pad(matrix, before=0):
            return jnp.pad(matrix, ((before, AUG - before - matrix.shape[0]), (0, 0)))

        a_qkv_rows = down_up_pad(a_pair[:3].reshape(3 * PAIR, width).astype(bf16))
        a_o_rows = local_lanes(a_pair[3].reshape(PAIR, width)).astype(bf16)
        b_pair = pick_pair(b_attn, 1)
        b_qkv_rows = local_lanes(b_pair[:3]).reshape(3, PAIR, local).astype(bf16)
        b_o_rows = down_up_pad(b_pair[3].reshape(PAIR, width).astype(bf16), PAIR)
        a_up_rows = down_up_pad(
            jnp.swapaxes(pick_pair(a_up, 0), 1, 2).reshape(PAIR, width).astype(bf16)
        )
        b_up_rows = pick_pair(b_up, 0).reshape(PAIR, hidden_local).astype(bf16)
        a_down_rows = (
            jnp.swapaxes(pick_pair(a_down, 0), 1, 2).reshape(PAIR, hidden_local).astype(bf16)
        )
        b_down_rows = down_up_pad(pick_pair(b_down, 0).reshape(PAIR, width).astype(bf16))

        def bias_lanes(opened):
            count = opened.shape[1]
            block = jnp.arange(count * BLOCK, dtype=jnp.int32) // BLOCK
            hit = opened[:, :, None] & (block[None, None, :] == jnp.arange(count)[None, :, None])
            return jnp.where(jnp.any(hit, axis=1), 0.0, neg_fill).astype(f32)

        reach, slot = ancestry(parent_block[0])
        all_blocks = reach.shape[0]
        first_block = context * blocks
        far_blocks = blocks if pair_ctx else all_blocks
        reach_rows = lax.dynamic_slice_in_dim(reach, first_block, blocks, 0)
        block_ids = jnp.arange(far_blocks, dtype=jnp.int32)
        far_open = (reach_rows[:, :far_blocks] > 0.5) & (block_ids[None, :] < first_block)
        own_open = lax.dynamic_slice_in_dim(reach_rows, first_block, blocks, 1) > 0.5
        far_bias = bias_lanes(far_open)
        own_bias = bias_lanes(own_open)

        slots = lax.dynamic_slice_in_dim(slot, first_block, blocks).astype(jnp.int32)
        lane_slot = (jnp.arange(AUG, dtype=jnp.int32) // RANK) % SLOTS

        def picks(first_row, count):
            block = (jnp.arange(count, dtype=jnp.int32) + first_row) // BLOCK
            row_slot = jnp.sum(
                jnp.where(block[:, None] == jnp.arange(blocks)[None, :], slots[None, :], 0), axis=1
            )
            return (row_slot[:, None] == lane_slot[None, :]).astype(f32)

        pick_own = picks(core * half, half)

        gain_one, shift_one = ln_gain[0][None, :], ln_bias[0][None, :]
        gain_two, shift_two = ln_gain[1][None, :], ln_bias[1][None, :]

        def widen(low, tail):
            return jnp.concatenate([low, tail], axis=1)

        def own_norm(places):
            return norm_wide([inputs], places, slots, a_qkv_rows, gain_one, shift_one, tokens)

        q_aug = jnp.concatenate(
            [jnp.pad(b_qkv_rows[i], ((0, 0), (i * local, (2 - i) * local))) for i in range(3)]
            + [jnp.zeros((AUG - 3 * PAIR, 3 * local), bf16)],
            axis=0,
        )
        o_aug = down_up_pad(a_o_rows, PAIR).T
        in_aug = down_up_pad(b_up_rows)
        out_aug = down_up_pad(a_down_rows).T
        if pair_ctx:
            quarter = tokens // 4
            sent = lax.dynamic_slice_in_dim(inputs, tensor * quarter, quarter, 0)
            far_quarter = on(sent, "ctx", [(0, 1)])

            far_places = jnp.stack([tensor, tensor ^ 2, tensor ^ 1, tensor ^ 3]).astype(jnp.int32)
            inner = (group == 1) | (group == 2)
            q_ring = Ring(w_qkv, 1, context, inner)
            o_ring = Direct(w_o, 0, context)
            in_ring = Ring(w_in, 0, context, inner)
            out_ring = Ring(w_out, 0, context, inner)
            q_ring.first()
            q_ring.second()
            q_ring.third(far_quarter)
            normed_wide = own_norm(gate(jnp.arange(4, dtype=jnp.int32), q_ring.y_one))
            far_quarter, _ = lax.optimization_barrier((far_quarter, q_ring.two))
            far_x = on(far_quarter, "tp", X_SWAP)
            far_core = on(far_quarter, "tp", CORE_SWAP)
            far_x, far_core, normed_wide, _ = lax.optimization_barrier(
                (far_x, far_core, normed_wide, q_ring.last)
            )
            q_ring.fourth(normed_wide)
            o_ring.first(q_ring.last)
            far_both = on(far_x, "tp", CORE_SWAP)
            far_wide = norm_wide(
                [far_quarter, far_x, far_core, far_both],
                far_places,
                slot[:blocks].astype(jnp.int32),
                a_qkv_rows,
                gain_one,
                shift_one,
                tokens,
            )
            o_ring.second(q_ring.y_three, far_wide)
            in_ring.first(*o_ring.near)
            q_full = assemble(
                gate(spot, *o_ring.near, far_wide),
                q_ring.pieces(),
                q_aug,
                wide,
                3 * local,
                ("rows", shard, shard // 2),
                3,
            )
        else:
            normed_wide = own_norm(jnp.arange(4, dtype=jnp.int32))
            own_q = jnp.transpose(w_qkv, (1, 0, 2)).reshape(shard, 3 * local)
            q_full = jnp.concatenate([lax.all_gather(own_q, "fsdp", axis=0, tiled=True), q_aug], 0)
            o_full = jnp.concatenate([lax.all_gather(w_o, "fsdp", axis=1, tiled=True), o_aug], 1)
            in_full = jnp.concatenate([lax.all_gather(w_in, "fsdp", axis=0, tiled=True), in_aug], 0)
            out_full = jnp.concatenate(
                [lax.all_gather(w_out, "fsdp", axis=1, tiled=True), out_aug], 1
            )

        normed, reduced_qkv = normed_wide[:, :width], normed_wide[:, width:]
        zero_bias = jnp.zeros((local,), f32)
        q_bias = jnp.concatenate([bias_qv[0], zero_bias, bias_qv[1]])[None, :]
        if pair_ctx:
            qkv = project(normed_wide, far_wide, q_full, q_bias, local)
            far_kv = qkv
            far_base = 3 * heads
            qkv, *_ = lax.optimization_barrier((qkv, in_ring.one, in_ring.across, *o_ring.far))
            in_ring.second(qkv)
            far_kv = qkv
        else:
            qkv = project(normed_wide, None, q_full, q_bias, local)
            far_kv = lax.all_gather(qkv[:, local:], "ctx", axis=0, tiled=True)
            far_base = 0

        attended_f, attended, probs_far, probs_own = attend_forward(
            qkv, far_kv, far_base, far_bias, own_bias, heads, scale
        )
        if pair_ctx:
            in_ring.third(attended)
            o_full = assemble(
                gate(spot, attended),
                o_ring.pieces(),
                o_aug,
                local,
                wide,
                ("columns", shard, local // 2),
                0,
                True,
            )
        core_id = core.astype(jnp.int32)[None]
        other_id = 1 - core_id
        branch_sent = send_tp(
            matmul(attended, other_id, o_full, local, False),
            matmul(attended, core_id, o_full, local, False)[0],
        )
        branch_far = branch_sent[1]
        if pair_ctx:
            in_ring.fourth(branch_sent[0])
            out_ring.first(in_ring.last, branch_sent[0])
            branch_far = gate(branch_far, in_ring.y_three, out_ring.one, out_ring.across)
        middle, two_own = row_call(
            after_attention,
            "after_attention",
            core_id,
            slots,
            half,
            [(branch_sent[0], False), (branch_far, False), (inputs, True)],
            [exit_offsets[:1], gain_two, shift_two, b_o_rows, a_up_rows],
            [(width, f32), (wide, bf16)],
        )
        two_other = on(two_own, "tp", CORE_SWAP)

        if pair_ctx:
            out_ring.second(in_ring.y_three)
            in_full = assemble(
                gate(spot, out_ring.outward, out_ring.back),
                in_ring.pieces(),
                in_aug,
                wide,
                hidden_local,
                ("rows", shard, shard // 2),
                0,
            )
        hidden, slope = expand(two_own, two_other, in_full, hidden_offset_frozen[None, :])
        if pair_ctx:
            out_ring.third()
            out_ring.fourth()
            out_full = assemble(
                gate(spot, hidden),
                out_ring.pieces(),
                out_aug,
                hidden_local,
                wide,
                ("columns", shard, hidden_local // 2),
                0,
            )

        loss_own = own_rows(loss_sensitivity)
        loss_rel = jnp.concatenate([loss_own, other_rows(loss_sensitivity)], axis=0)
        pick_rel = jnp.concatenate([pick_own, picks((1 - core) * half, half)], axis=0)
        grad_down_down = (factor * dot_nt(loss_rel, b_down_rows) * pick_rel).astype(bf16)
        loss_wide = widen(loss_rel, grad_down_down)
        grad_pre = back_hidden(loss_wide, out_full, slope)
        first_id = jnp.zeros((1,), jnp.int32)
        second_id = first_id + 1
        ff_cut = hidden_local // 2
        two_sent = send_tp(
            matmul(grad_pre, second_id, in_full, ff_cut, True),
            matmul(grad_pre, first_id, in_full, ff_cut, True)[0],
        )
        late_hidden = gate(hidden, two_sent[0])
        exit_sent = send_tp(
            matmul(late_hidden, second_id, out_full, ff_cut, False, 2),
            matmul(late_hidden, first_id, out_full, ff_cut, False)[0],
            two_sent[1],
        )
        grad_middle, back_own = row_call(
            back_middle,
            "back_middle",
            core_id,
            slots,
            half,
            [
                (two_sent[0], False),
                (gate(two_sent[1], exit_sent[0]), False),
                (middle, False),
                (loss_sensitivity, True),
            ],
            [gain_two, a_up_rows, b_o_rows],
            [(width, f32), (wide, bf16)],
        )
        back_other = on(back_own, "tp", CORE_SWAP)
        grad_attended = back_attend(core_id, back_own, back_other, o_full)

        grad_q, grad_k, grad_v, far_grads = attend_backward(
            qkv, far_kv, far_base, grad_attended, attended_f, probs_far, probs_own, heads, scale
        )
        if pair_ctx:
            more = on(far_grads, "ctx", [(1, 0)])
        else:
            more = lax.psum_scatter(far_grads, "ctx", scatter_dimension=1, tiled=True)
        layer_own, down_own = row_call(
            after_hidden,
            "after_hidden",
            core_id,
            slots,
            half,
            [(exit_sent[0], False), (exit_sent[1], False), (middle, False)],
            [exit_offsets[1:], b_down_rows],
            [(width, bf16), (AUG, bf16)],
        )
        down_other = on(down_own, "tp", CORE_SWAP)
        tiles = hidden_local // local

        def to_owners(slabs):
            pieces = [
                lax.dynamic_index_in_dim(slabs, group ^ k, 0, keepdims=False) for k in range(4)
            ]
            return jnp.stack(
                pieces[:1]
                + [on(pieces[k], "fsdp", [(i, i ^ k) for i in range(4)]) for k in range(1, 4)]
            )

        tensor_id, core_at = tensor.astype(jnp.int32), core.astype(jnp.int32)
        packed = pack_terms(
            tensor_id,
            core_at,
            (two_own, two_other),
            (back_own, back_other),
            attended,
            grad_pre,
            hidden,
            grad_down_down,
            local,
        )
        packed_layer = pack_layer(
            tensor_id, core_at, (down_own, down_other), loss_sensitivity, local
        )
        grad_k = gate(grad_k, packed, packed_layer)
        grad_qkv = jnp.concatenate(
            [
                grad_q,
                (grad_k.astype(f32) + more[0].astype(f32)).astype(bf16),
                (grad_v.astype(f32) + more[1].astype(f32)).astype(bf16),
            ],
            axis=1,
        )
        low_part = dot_nt(grad_qkv, q_full[width:]).astype(bf16)
        low_core = on(low_part, "tp", CORE_SWAP)
        low_pair = round_low(low_part.astype(f32) + low_core.astype(f32))
        low_far = on(low_pair, "tp", X_SWAP)
        low_sum = low_pair.astype(f32) + low_far.astype(f32)
        grad_down_qkv = (factor * low_sum * picks(0, tokens)).astype(bf16)
        one_other, one_own = back_project(
            gate(grad_qkv, low_part), core_id, q_full, width
        )
        one_sent = send_tp([one_other], one_own, low_far)
        layer_other = on(layer_own, "tp", CORE_SWAP)
        layer_out = place_rows(core_id, layer_own, layer_other, width)
        near = to_owners(packed)
        near_qkv = to_owners(
            jnp.concatenate(
                [
                    pack_projections(tensor_id[None], grad_down_qkv, normed_wide, grad_qkv, local),
                    packed_layer,
                ],
                axis=1,
            )
        )
        holder = jnp.stack([group ^ k for k in range(4)])
        owner = adapter_of.reshape(4, SLOTS)[holder].reshape(4 * SLOTS)
        if pair_ctx:
            adapter_grads = unpack_terms(
                context.astype(jnp.int32)[None],
                owner,
                (near, near_qkv),
                (on(near, "ctx", swap_y), on(near_qkv, "ctx", swap_y)),
                tiles,
            )
        else:
            total = lax.psum((near.astype(f32), near_qkv.astype(f32)), "ctx")
            adapter_grads = unpack_plain(
                context, owner, jnp.concatenate(total, axis=1), tiles, ctx_size
            )
        (grad_own,) = row_call(
            back_first,
            "back_first",
            core_id,
            slots,
            half,
            [
                (one_sent[0], False),
                (gate(one_sent[1], adapter_grads[0], layer_out), False),
                (grad_down_qkv, True),
                (inputs, True),
                (grad_middle, False),
            ],
            [gain_one, a_qkv_rows],
            [(width, bf16)],
        )
        grad_other = on(grad_own, "tp", CORE_SWAP)
        grad_inputs = place_rows(core_id, grad_own, grad_other, width)

        out_a_attn, out_b_attn, out_a_up, out_b_up, out_a_down, out_b_down = adapter_grads
        return (
            layer_out,
            grad_inputs,
            jnp.swapaxes(out_a_attn, 2, 3),
            out_b_attn,
            jnp.swapaxes(out_a_up, 1, 2),
            out_b_up,
            jnp.swapaxes(out_a_down, 1, 2),
            out_b_down,
        )

    return body


def solution(mesh):
    in_specs = (
        P(("fsdp", "ctx"), None),
        P(("fsdp", "ctx"), None),
        P("fsdp", None),
        P(),
        P(None, "fsdp", "tp"),
        P(None, "tp"),
        P("tp", "fsdp"),
        P(),
        P(),
        P(),
        P("fsdp", "tp"),
        P("tp"),
        P("tp", "fsdp"),
        P(),
        P(),
        P(),
        P(None, None, "tp"),
        P(None, "tp", None),
        P(),
    )
    out_specs = (
        P(("fsdp", "ctx"), None),
        P(("fsdp", "ctx"), None),
        P(None, None, ("tp", "fsdp", "ctx"), None),
        P(None, None, None, ("tp", "fsdp", "ctx")),
        P(None, ("tp", "fsdp", "ctx"), None),
        P(None, None, ("tp", "fsdp", "ctx")),
        P(None, ("tp", "fsdp", "ctx"), None),
        P(None, None, ("tp", "fsdp", "ctx")),
    )
    return jax.shard_map(
        make_body(mesh.shape["ctx"]),
        mesh=mesh,
        in_specs=in_specs,
        out_specs=out_specs,
        check_vma=False,
    )
```

```python
import jax
import jax.numpy as jnp
from jax import lax
from jax.experimental import pallas as pl
from jax.experimental.pallas import tpu as pltpu
from jax.sharding import PartitionSpec as P

HD = 128
RANK = 16
ADAPTERS = 8
SLOTS = 2
PAIR = SLOTS * RANK
BLOCK = 256
AUG = 128
ROW_CHUNK = 128
HINT = pl.CostEstimate(flops=1, transcendentals=0, bytes_accessed=1)

layer_eps = 1e-05
factor = 0.5
neg_fill = -1e30
bf16 = jnp.bfloat16
f32 = jnp.float32

CORE_SWAP = [(0, 1), (1, 0), (2, 3), (3, 2)]
SWAP_Y = [(0, 1), (1, 0)]
X_SWAP = [(0, 2), (2, 0), (1, 3), (3, 1)]


def dot_nn(a, b):
    return lax.dot_general(a, b, (((1,), (0,)), ((), ())), preferred_element_type=f32)


def dot_nt(a, b):
    return lax.dot_general(a, b, (((1,), (1,)), ((), ())), preferred_element_type=f32)


def dot_tn(a, b):
    return lax.dot_general(a, b, (((0,), (0,)), ((), ())), preferred_element_type=f32)


def round_low(v):
    return lax.reduce_precision(v, 8, 7).astype(bf16)


def standardize(rows):
    centre = rows - jnp.mean(rows, axis=-1, keepdims=True)
    spread = jnp.mean(centre * centre, axis=-1, keepdims=True)
    inverse = lax.rsqrt(spread + layer_eps)
    return centre * inverse, inverse


def norm_back(grad_scaled, unit, inverse):
    first = jnp.mean(grad_scaled, axis=-1, keepdims=True)
    second = jnp.mean(grad_scaled * unit, axis=-1, keepdims=True)
    return inverse * (grad_scaled - first - unit * second)


def ancestry(parents):
    total = parents.shape[0]
    position = jnp.arange(total, dtype=jnp.int32)
    reach = (
        (parents[:, None] == position[None, :]) | (position[:, None] == position[None, :])
    ).astype(f32)
    span = 1
    while span < total:
        reach = jnp.minimum(jnp.sum(reach[:, :, None] * reach[None, :, :], axis=1), 1.0)
        span *= 2
    roots = (parents < 0).astype(f32)
    order = jnp.sum(jnp.where(position[None, :] <= position[:, None], roots[None, :], 0.0), axis=1)
    slot = jnp.sum(reach * (roots * (order - 1.0))[None, :], axis=1)
    return reach, slot


def attend_forward(qkv, far, far_base, far_bias, own_bias, heads, scale):
    tokens = qkv.shape[0]
    far_rows = far.shape[0]
    blocks = tokens // BLOCK

    def kernel(q_ref, k_ref, v_ref, fk_ref, fv_ref, fb_ref, ob_ref, o_ref, low_ref, pf_ref, po_ref):
        far_k = fk_ref[...]
        far_v = fv_ref[...]
        for b in range(blocks):
            rows = slice(b * BLOCK, (b + 1) * BLOCK)
            width = (b + 1) * BLOCK
            q = q_ref[rows, :]
            s_far = dot_nt(q, far_k) * scale + fb_ref[b : b + 1, :]
            s_own = dot_nt(q, k_ref[:width, :]) * scale + ob_ref[b : b + 1, :width]
            q_pos = lax.broadcasted_iota(jnp.int32, (BLOCK, width), 0) + b * BLOCK
            k_pos = lax.broadcasted_iota(jnp.int32, (BLOCK, width), 1)
            s_own = jnp.where(k_pos <= q_pos, s_own, neg_fill)
            top = jnp.maximum(
                jnp.max(s_far, axis=1, keepdims=True), jnp.max(s_own, axis=1, keepdims=True)
            )
            p_far = jnp.exp(s_far - top)
            p_own = jnp.exp(s_own - top)
            total = jnp.sum(p_far, axis=1, keepdims=True) + jnp.sum(p_own, axis=1, keepdims=True)
            inverse = 1.0 / total
            p_far = (p_far * inverse).astype(bf16)
            p_own = (p_own * inverse).astype(bf16)
            pf_ref[0, rows, :] = p_far
            po_ref[0, rows, :width] = p_own
            mixed = dot_nn(p_far, far_v) + dot_nn(p_own, v_ref[:width, :])
            o_ref[rows, :] = mixed
            low_ref[rows, :] = mixed.astype(bf16)

    return pl.pallas_call(
        kernel,
        grid=(heads,),
        in_specs=[
            pl.BlockSpec((tokens, HD), lambda h: (0, h)),
            pl.BlockSpec((tokens, HD), lambda h: (0, heads + h)),
            pl.BlockSpec((tokens, HD), lambda h: (0, 2 * heads + h)),
            pl.BlockSpec((far_rows, HD), lambda h: (0, far_base + h)),
            pl.BlockSpec((far_rows, HD), lambda h: (0, far_base + heads + h)),
            pl.BlockSpec((blocks, far_rows), lambda h: (0, 0)),
            pl.BlockSpec((blocks, tokens), lambda h: (0, 0)),
        ],
        out_specs=[
            pl.BlockSpec((tokens, HD), lambda h: (0, h)),
            pl.BlockSpec((tokens, HD), lambda h: (0, h)),
            pl.BlockSpec((1, tokens, far_rows), lambda h: (h, 0, 0)),
            pl.BlockSpec((1, tokens, tokens), lambda h: (h, 0, 0)),
        ],
        out_shape=[
            jax.ShapeDtypeStruct((tokens, heads * HD), f32),
            jax.ShapeDtypeStruct((tokens, heads * HD), bf16),
            jax.ShapeDtypeStruct((heads, tokens, far_rows), bf16),
            jax.ShapeDtypeStruct((heads, tokens, tokens), bf16),
        ],
        compiler_params=pltpu.CompilerParams(vmem_limit_bytes=(44 if far_rows == tokens else 56) << 20),
        cost_estimate=HINT,
        name="attend_forward",
    )(qkv, qkv, qkv, far, far, far_bias, own_bias)


def attend_backward(qkv, far, far_base, grad_attended, attended, probs_far, probs_own, heads, scale):
    tokens = qkv.shape[0]
    far_rows = far.shape[0]
    blocks = tokens // BLOCK

    def kernel(
        q_ref, k_ref, v_ref, fk_ref, fv_ref, g_ref, o_ref, pf_ref, po_ref,
        dq_ref, dk_ref, dv_ref, far_ref,
        dk_acc, dv_acc, dfk_acc, dfv_acc,
    ):
        far_k = fk_ref[...]
        far_v = fv_ref[...]
        for b in reversed(range(blocks)):
            first = b == blocks - 1
            rows = slice(b * BLOCK, (b + 1) * BLOCK)
            width = (b + 1) * BLOCK
            q = q_ref[rows, :]
            g = g_ref[rows, :]
            row_dot = jnp.sum(g.astype(f32) * o_ref[rows, :], axis=1, keepdims=True)
            p_far = pf_ref[0, rows, :]
            p_own = po_ref[0, rows, :width]
            d_far = (p_far.astype(f32) * (dot_nt(g, far_v) - row_dot)).astype(bf16)
            d_own = (p_own.astype(f32) * (dot_nt(g, v_ref[:width, :]) - row_dot)).astype(bf16)
            dq_ref[rows, :] = (
                (dot_nn(d_far, far_k) + dot_nn(d_own, k_ref[:width, :])) * scale
            ).astype(bf16)
            if first:
                dfk_acc[...] = dot_tn(d_far, q)
                dfv_acc[...] = dot_tn(p_far, g)
                dk_acc[...] = dot_tn(d_own, q)
                dv_acc[...] = dot_tn(p_own, g)
            else:
                dfk_acc[...] += dot_tn(d_far, q)
                dfv_acc[...] += dot_tn(p_far, g)
                dk_acc[:width, :] += dot_tn(d_own, q)
                dv_acc[:width, :] += dot_tn(p_own, g)
        dk_ref[...] = (dk_acc[...] * scale).astype(bf16)
        dv_ref[...] = dv_acc[...].astype(bf16)
        far_ref[0] = (dfk_acc[...] * scale).astype(bf16)
        far_ref[1] = dfv_acc[...].astype(bf16)

    head_spec = pl.BlockSpec((tokens, HD), lambda h: (0, h))
    far_spec = pl.BlockSpec((2, far_rows, HD), lambda h: (0, 0, h))
    own_shape = jax.ShapeDtypeStruct((tokens, heads * HD), bf16)
    far_shape = jax.ShapeDtypeStruct((2, far_rows, heads * HD), bf16)
    return pl.pallas_call(
        kernel,
        grid=(heads,),
        in_specs=[
            head_spec,
            pl.BlockSpec((tokens, HD), lambda h: (0, heads + h)),
            pl.BlockSpec((tokens, HD), lambda h: (0, 2 * heads + h)),
            pl.BlockSpec((far_rows, HD), lambda h: (0, far_base + h)),
            pl.BlockSpec((far_rows, HD), lambda h: (0, far_base + heads + h)),
            head_spec,
            head_spec,
            pl.BlockSpec((1, tokens, far_rows), lambda h: (h, 0, 0)),
            pl.BlockSpec((1, tokens, tokens), lambda h: (h, 0, 0)),
        ],
        out_specs=[head_spec, head_spec, head_spec, far_spec],
        out_shape=[own_shape, own_shape, own_shape, far_shape],
        scratch_shapes=[
            pltpu.VMEM((tokens, HD), f32),
            pltpu.VMEM((tokens, HD), f32),
            pltpu.VMEM((far_rows, HD), f32),
            pltpu.VMEM((far_rows, HD), f32),
        ],
        compiler_params=pltpu.CompilerParams(vmem_limit_bytes=(44 if far_rows == tokens else 56) << 20),
        cost_estimate=HINT,
        name="attend_backward",
    )(qkv, qkv, qkv, far, far, grad_attended, attended, probs_far, probs_own)


def assemble(spot, pieces, tail, rows, columns, step, parts, straight=False):
    direction, shard, half_rows = step
    count = max(parts, 1)
    part_columns = columns // count if parts else columns
    tail_rows, tail_columns = tail.shape

    def kernel(spot_ref, *refs):
        own, one, y_one, two, y_two, three, y_three, tail_ref, out, sem = refs
        group = spot_ref[0]
        context = spot_ref[1]
        inner = (group == 1) | (group == 2)

        def moves(piece, source, which, first):
            made = []
            for i in range(count):
                src = piece.at[i] if parts else piece
                n, m = src.shape
                if direction == "rows":
                    row = pl.multiple_of(source * shard + which * half_rows, half_rows)
                    dst = out.at[pl.ds(row, n), pl.ds(i * part_columns, m)]
                else:
                    row = pl.multiple_of(which * half_rows, half_rows)
                    col = pl.multiple_of(source * shard, shard)
                    dst = out.at[pl.ds(row, n), pl.ds(col, m)]
                made.append(pltpu.make_async_copy(src, dst, sem.at[first + i]))
            return made

        fixed = moves(own, group, 0, 0)
        fixed += moves(one, group ^ 1, context, count)
        fixed += moves(y_one, group ^ 1, 1 - context, 2 * count)
        second = group ^ 2 if straight else jnp.where(inner, group ^ 3, group ^ 2)
        third = group ^ 3 if straight else jnp.where(inner, group ^ 2, group ^ 3)
        fixed += moves(two, second, context, 3 * count)
        fixed += moves(y_two, second, 1 - context, 4 * count)
        fixed += moves(three, third, context, 5 * count)
        fixed += moves(y_three, third, 1 - context, 6 * count)
        row0 = rows - tail_rows if direction == "rows" else 0
        col0 = 0 if direction == "rows" else columns - tail_columns
        fixed.append(
            pltpu.make_async_copy(
                tail_ref,
                out.at[pl.ds(row0, tail_rows), pl.ds(col0, tail_columns)],
                sem.at[7 * count],
            )
        )
        for move in fixed:
            move.start()

        for move in fixed:
            move.wait()

    return pl.pallas_call(
        kernel,
        grid_spec=pltpu.PrefetchScalarGridSpec(
            num_scalar_prefetch=1,
            grid=(),
            in_specs=[pl.BlockSpec(memory_space=pltpu.HBM)] * 8,
            out_specs=pl.BlockSpec(memory_space=pltpu.VMEM),
            scratch_shapes=[pltpu.SemaphoreType.DMA((7 * count + 1,))],
        ),
        out_shape=jax.ShapeDtypeStruct((rows, columns), bf16),
        compiler_params=pltpu.CompilerParams(vmem_limit_bytes=4 << 20),
        cost_estimate=HINT,
        name="assemble",
    )(spot, *pieces, tail)


def norm_wide(pieces, places, slots, down_rows, gain, shift, tokens):
    width = gain.shape[1]
    blocks = tokens // BLOCK
    count = len(pieces)
    quarter = tokens // 4
    steps = 4 // count

    def kernel(place_ref, slot_ref, *refs):
        down_ref, gain_ref, shift_ref, out_ref = refs[count:]
        for i in range(4):
            x_ref = refs[i // steps]
            first = (i % steps) * quarter
            rows = x_ref[first : first + quarter, :].astype(f32)
            start = pl.multiple_of(place_ref[i] * quarter, quarter)
            unit, _ = standardize(rows)
            low = (unit * gain_ref[...] + shift_ref[...]).astype(bf16)
            block = (lax.broadcasted_iota(jnp.int32, (quarter, AUG), 0) + start) // BLOCK
            lane_slot = (lax.broadcasted_iota(jnp.int32, (quarter, AUG), 1) // RANK) % SLOTS
            slot = jnp.zeros((quarter, AUG), jnp.int32)
            for b in range(blocks):
                slot = jnp.where(block == b, slot_ref[b], slot)
            down = jnp.where(slot == lane_slot, dot_nt(low, down_ref[...]), 0.0)
            out_ref[pl.ds(start, quarter), :width] = low
            out_ref[pl.ds(start, quarter), width:] = factor * down.astype(bf16)

    whole = pl.BlockSpec(memory_space=pltpu.VMEM)
    return pl.pallas_call(
        kernel,
        grid_spec=pltpu.PrefetchScalarGridSpec(
            num_scalar_prefetch=2,
            grid=(),
            in_specs=[whole] * (count + 3),
            out_specs=whole,
        ),
        out_shape=jax.ShapeDtypeStruct((tokens, width + AUG), bf16),
        compiler_params=pltpu.CompilerParams(vmem_limit_bytes=12 << 20),
        cost_estimate=HINT,
        name="norm_wide",
    )(places, slots, *pieces, down_rows, gain, shift)


def own_pick(first_row, count, slot_ref, blocks):
    block = (lax.broadcasted_iota(jnp.int32, (count, AUG), 0) + first_row) // BLOCK
    lane_slot = (lax.broadcasted_iota(jnp.int32, (count, AUG), 1) // RANK) % SLOTS
    slot = jnp.zeros((count, AUG), jnp.int32)
    for b in range(blocks):
        slot = jnp.where(block == b, slot_ref[b], slot)
    return slot == lane_slot


def row_call(body, name, core, slots, rows, moving, fixed, outs):
    chunk = ROW_CHUNK
    steps = rows // chunk
    blocks = slots.shape[0]
    n_in = len(moving) + len(fixed)

    def kernel(core_ref, slot_ref, *refs):
        first = core_ref[0] * rows + pl.program_id(0) * chunk
        pick = own_pick(first, chunk, slot_ref, blocks)
        results = body(pick, *[r[...] for r in refs[:n_in]])
        for ref, value in zip(refs[n_in:], results):
            ref[...] = value

    specs = []
    for array, offset in moving:
        if offset:
            specs.append(
                pl.BlockSpec((chunk, array.shape[1]), lambda i, c, s: (c[0] * steps + i, 0))
            )
        else:
            specs.append(pl.BlockSpec((chunk, array.shape[1]), lambda i, c, s: (i, 0)))
    for array in fixed:
        specs.append(pl.BlockSpec(array.shape, lambda i, c, s: (0, 0)))
    return pl.pallas_call(
        kernel,
        grid_spec=pltpu.PrefetchScalarGridSpec(
            num_scalar_prefetch=2,
            grid=(steps,),
            in_specs=specs,
            out_specs=[pl.BlockSpec((chunk, c), lambda i, c_, s: (i, 0)) for c, _ in outs],
        ),
        out_shape=[jax.ShapeDtypeStruct((rows, c), d) for c, d in outs],
        compiler_params=pltpu.CompilerParams(vmem_limit_bytes=12 << 20),
        cost_estimate=HINT,
        name=name,
    )(core, slots, *[a for a, _ in moving], *fixed)


def join(mine, got):
    piece = got[0].shape[0]

    def kernel(a_ref, *refs):
        out_ref, sum_ref, sem = refs[len(got) :]
        for i, b_ref in enumerate(refs[: len(got)]):
            rows = slice(i * piece, (i + 1) * piece)
            sum_ref[rows, :] = (a_ref[rows, :].astype(f32) + b_ref[...].astype(f32)).astype(bf16)
        move = pltpu.make_async_copy(sum_ref, out_ref, sem)
        move.start()
        move.wait()

    whole = pl.BlockSpec(memory_space=pltpu.VMEM)
    return pl.pallas_call(
        kernel,
        in_specs=[whole] * (1 + len(got)),
        out_specs=pl.BlockSpec(memory_space=pltpu.HBM),
        out_shape=jax.ShapeDtypeStruct(mine.shape, bf16),
        scratch_shapes=[pltpu.VMEM(mine.shape, bf16), pltpu.SemaphoreType.DMA],
        compiler_params=pltpu.CompilerParams(vmem_limit_bytes=8 << 20),
        cost_estimate=HINT,
        name="join",
    )(mine, *got)


def back_project(grad, core, weight, width):
    tokens, summed = grad.shape
    size = tokens // 2

    def kernel(core_ref, x_ref, w_ref, other_ref, own_ref):
        part = dot_nt(x_ref[...], w_ref[...]).astype(bf16)

        @pl.when(pl.program_id(0) == 0)
        def _():
            other_ref[...] = part

        @pl.when(pl.program_id(0) == 1)
        def _():
            own_ref[...] = part

    whole = pl.BlockSpec((size, width), lambda n, c: (0, 0))
    shape = jax.ShapeDtypeStruct((size, width), bf16)
    return pl.pallas_call(
        kernel,
        grid_spec=pltpu.PrefetchScalarGridSpec(
            num_scalar_prefetch=1,
            grid=(2,),
            in_specs=[
                pl.BlockSpec((size, summed), lambda n, c: (jnp.where(n == 0, 1 - c[0], c[0]), 0)),
                pl.BlockSpec((width, summed), lambda n, c: (0, 0)),
            ],
            out_specs=[whole, whole],
        ),
        out_shape=[shape, shape],
        compiler_params=pltpu.CompilerParams(vmem_limit_bytes=26 << 20),
        cost_estimate=HINT,
        name="back_project",
    )(core, grad, weight)


def place_rows(core, own, other, width):
    size = own.shape[0]

    def kernel(core_ref, own_ref, other_ref, out_ref, sem):
        moves = []
        for n, (ref, side) in enumerate(((own_ref, core_ref[0]), (other_ref, 1 - core_ref[0]))):
            start = pl.multiple_of(side * size, size)
            moves.append(
                pltpu.make_async_copy(
                    ref.at[:, pl.ds(0, width)], out_ref.at[pl.ds(start, size), :], sem.at[n]
                )
            )
        for move in moves:
            move.start()
        for move in moves:
            move.wait()

    whole = pl.BlockSpec(memory_space=pltpu.VMEM)
    return pl.pallas_call(
        kernel,
        grid_spec=pltpu.PrefetchScalarGridSpec(
            num_scalar_prefetch=1,
            grid=(),
            in_specs=[whole] * 2,
            out_specs=pl.BlockSpec(memory_space=pltpu.HBM),
            scratch_shapes=[pltpu.SemaphoreType.DMA((2,))],
        ),
        out_shape=jax.ShapeDtypeStruct((2 * size, width), bf16),
        compiler_params=pltpu.CompilerParams(vmem_limit_bytes=8 << 20),
        cost_estimate=HINT,
        name="place_rows",
    )(core, own, other)


def after_attention(pick, mine, far, rows, exit_row, gain, shift, b_o_rows, a_up_rows):
    width = rows.shape[1]
    total = mine.astype(f32) + far.astype(f32)
    down_o = factor * jnp.where(pick, total[:, width:], 0.0).astype(bf16)
    middle = rows.astype(f32) + total[:, :width] + exit_row + dot_nn(down_o, b_o_rows)
    unit, _ = standardize(middle)
    low = (unit * gain + shift).astype(bf16)
    down_up = factor * jnp.where(pick, dot_nt(low, a_up_rows), 0.0).astype(bf16)
    return middle, jnp.concatenate([low, down_up + down_o], axis=1)


def after_hidden(pick, mine, far, middle, exit_row, b_down_rows):
    width = middle.shape[1]
    total = mine.astype(f32) + far.astype(f32)
    down = factor * jnp.where(pick, total[:, width:], 0.0).astype(bf16)
    out = middle + total[:, :width] + exit_row + dot_nn(down, b_down_rows)
    return out.astype(bf16), down


def back_middle(pick, mine, far, middle, loss, gain, a_up_rows, b_o_rows):
    width = middle.shape[1]
    total = mine.astype(f32) + far.astype(f32)
    grad_down = (factor * jnp.where(pick, total[:, width:], 0.0)).astype(bf16)
    grad_normed = total[:, :width] + dot_nn(grad_down, a_up_rows)
    unit, inverse = standardize(middle)
    grad = loss.astype(f32) + norm_back(grad_normed * gain, unit, inverse)
    low = grad.astype(bf16)
    grad_o = (factor * jnp.where(pick, dot_nt(low, b_o_rows), 0.0)).astype(bf16)
    return grad, jnp.concatenate([low, grad_o + grad_down], axis=1)


def back_first(pick, mine, far, grad_down, rows, grad_middle, gain, a_rows):
    total = mine.astype(f32) + far.astype(f32)
    grad_normed = total + dot_nn(grad_down, a_rows)
    unit, inverse = standardize(rows.astype(f32))
    return ((grad_middle + norm_back(grad_normed * gain, unit, inverse)).astype(bf16),)


def pack_terms(tensor, core, two, back, attended, grad_pre, hidden, grad_dd, local):
    width = two[0].shape[1] - AUG
    half = two[0].shape[0]
    cut = local // 4

    def kernel(t_ref, two_a, two_b, back_a, back_b, att_ref, gp_ref, hid_ref, gdd_ref, out):
        lanes = pl.ds(pl.multiple_of(t_ref[0] * local, local), local)
        mine = pl.ds(pl.multiple_of(t_ref[1] * half, half), half)
        theirs = pl.ds(pl.multiple_of((1 - t_ref[1]) * half, half), half)
        halves = ((two_a, back_a, mine), (two_b, back_b, theirs))

        def both(make):
            return make(*halves[0]) + make(*halves[1])

        terms = [
            both(lambda t, b, r: dot_tn(b[:, width:], att_ref[r, :]))[PAIR : 2 * PAIR],
            both(lambda t, b, r: dot_tn(t[:, width:], b[:, lanes]))[PAIR : 2 * PAIR],
            both(lambda t, b, r: dot_tn(b[:, width:], t[:, lanes]))[:PAIR],
        ]
        for n, term in enumerate(terms):
            low = term.astype(bf16)
            for g in range(4):
                out[g, n * PAIR : (n + 1) * PAIR, :] = low[:, g * cut : (g + 1) * cut]
        base = len(terms) * PAIR
        wide_terms = (
            dot_tn(two_a[:, width:], gp_ref[:half, :]) + dot_tn(two_b[:, width:], gp_ref[half:, :]),
            dot_tn(gdd_ref[...], hid_ref[...]),
        )
        for term in wide_terms:
            low = term[:PAIR].astype(bf16)
            tiles = low.shape[1] // (4 * cut)
            for g in range(4):
                for t in range(tiles):
                    c = (g * tiles + t) * cut
                    out[g, base + t * PAIR : base + (t + 1) * PAIR, :] = low[:, c : c + cut]
            base += tiles * PAIR

    tiles = hidden.shape[1] // local
    whole = pl.BlockSpec(memory_space=pltpu.VMEM)
    return pl.pallas_call(
        kernel,
        grid_spec=pltpu.PrefetchScalarGridSpec(
            num_scalar_prefetch=1, grid=(), in_specs=[whole] * 8, out_specs=whole
        ),
        out_shape=jax.ShapeDtypeStruct((4, (3 + 2 * tiles) * PAIR, cut), bf16),
        compiler_params=pltpu.CompilerParams(vmem_limit_bytes=24 << 20),
        cost_estimate=HINT,
        name="pack_terms",
    )(jnp.stack([tensor, core]), *two, *back, attended, grad_pre, hidden, grad_dd)


def pack_layer(tensor, core, down, loss, local):
    half = down[0].shape[0]
    cut = local // 4

    def kernel(t_ref, own_ref, other_ref, loss_ref, out, low, sem):
        lanes = pl.ds(pl.multiple_of(t_ref[0] * local, local), local)
        move = pltpu.make_async_copy(loss_ref.at[:, lanes], low, sem)
        move.start()
        move.wait()
        mine = pl.ds(pl.multiple_of(t_ref[1] * half, half), half)
        theirs = pl.ds(pl.multiple_of((1 - t_ref[1]) * half, half), half)
        term = dot_tn(own_ref[...], low[mine, :]) + dot_tn(other_ref[...], low[theirs, :])
        for g in range(4):
            out[g] = term[:PAIR, g * cut : (g + 1) * cut].astype(bf16)

    whole = pl.BlockSpec(memory_space=pltpu.VMEM)
    return pl.pallas_call(
        kernel,
        grid_spec=pltpu.PrefetchScalarGridSpec(
            num_scalar_prefetch=1,
            grid=(),
            in_specs=[whole] * 2 + [pl.BlockSpec(memory_space=pltpu.HBM)],
            out_specs=whole,
            scratch_shapes=[pltpu.VMEM((2 * half, local), bf16), pltpu.SemaphoreType.DMA],
        ),
        out_shape=jax.ShapeDtypeStruct((4, PAIR, cut), bf16),
        compiler_params=pltpu.CompilerParams(vmem_limit_bytes=4 << 20),
        cost_estimate=HINT,
        name="pack_layer",
    )(jnp.stack([tensor, core]), *down, loss)


def pack_projections(tensor, grad_down, normed_wide, grad_qkv, local):
    width = normed_wide.shape[1] - AUG
    cut = local // 4

    def kernel(t_ref, gd_ref, nw_ref, gq_ref, out):
        lanes = pl.ds(pl.multiple_of(t_ref[0] * local, local), local)
        down = dot_tn(gd_ref[...], nw_ref[:, lanes]).astype(bf16)
        up = dot_tn(nw_ref[:, width:], gq_ref[...]).astype(bf16)
        for i in range(3):
            rows = slice(i * PAIR, (i + 1) * PAIR)
            for g in range(4):
                out[g, rows, :] = down[rows, g * cut : (g + 1) * cut]
                c = i * local + g * cut
                out[g, (3 + i) * PAIR : (4 + i) * PAIR, :] = up[rows, c : c + cut]

    whole = pl.BlockSpec(memory_space=pltpu.VMEM)
    return pl.pallas_call(
        kernel,
        grid_spec=pltpu.PrefetchScalarGridSpec(
            num_scalar_prefetch=1, grid=(), in_specs=[whole] * 3, out_specs=whole
        ),
        out_shape=jax.ShapeDtypeStruct((4, 6 * PAIR, cut), bf16),
        compiler_params=pltpu.CompilerParams(vmem_limit_bytes=4 << 20),
        cost_estimate=HINT,
        name="pack_projections",
    )(tensor, grad_down, normed_wide, grad_qkv)


def unpack_terms(context, owner, near, cross, tiles):
    cut = near[0].shape[2]
    half = cut // 2

    def kernel(c_ref, owner_ref, n0, n1, c0, c1, a_attn, b_attn, a_up, b_up, a_down, b_down):
        first = c_ref[0] == 0

        for k in range(4):
            for s in range(SLOTS):
                who = owner_ref[k * SLOTS + s]

                def value(row, n_ref=n0, c_ref=c0):
                    rows = slice(row + s * RANK, row + (s + 1) * RANK)
                    return n_ref[k, rows, :].astype(f32) + c_ref[k, rows, :].astype(f32)

                def narrow(row, *refs):
                    v = value(row, *refs)
                    return jnp.where(first, v[:, :half], v[:, half:])

                for i in range(3):
                    a_attn[i, pl.ds(who, 1)] = narrow(i * PAIR, n1, c1)[None]
                    b_attn[i, pl.ds(who, 1)] = narrow((3 + i) * PAIR, n1, c1)[None]
                a_attn[3, pl.ds(who, 1)] = narrow(0)[None]
                b_attn[3, pl.ds(who, 1)] = narrow(PAIR)[None]
                a_up[pl.ds(who, 1)] = narrow(2 * PAIR)[None]
                b_down[pl.ds(who, 1)] = narrow(6 * PAIR, n1, c1)[None]
                for n, ref in enumerate((b_up, a_down)):
                    start = (3 + n * tiles) * PAIR
                    for t in range(tiles // 2):
                        ref[pl.ds(who, 1), :, t * cut : (t + 1) * cut] = jnp.where(
                            first,
                            value(start + t * PAIR),
                            value(start + (tiles // 2 + t) * PAIR),
                        )[None]

    narrow_shape = (ADAPTERS, RANK, half)
    wide_shape = (ADAPTERS, RANK, tiles * half)
    whole = pl.BlockSpec(memory_space=pltpu.VMEM)
    shapes = [(4,) + narrow_shape, (4,) + narrow_shape, narrow_shape, wide_shape, wide_shape, narrow_shape]
    return pl.pallas_call(
        kernel,
        grid_spec=pltpu.PrefetchScalarGridSpec(
            num_scalar_prefetch=2, grid=(), in_specs=[whole] * 4, out_specs=[whole] * 6
        ),
        out_shape=[jax.ShapeDtypeStruct(shape, f32) for shape in shapes],
        compiler_params=pltpu.CompilerParams(vmem_limit_bytes=4 << 20),
        cost_estimate=HINT,
        name="unpack_terms",
    )(context, owner, *near, *cross)


def unpack_plain(context, owner, total, tiles, ctx_size):
    cut = total.shape[2]
    place = (jnp.arange(ADAPTERS, dtype=jnp.int32)[:, None] == owner[None, :]).astype(f32)
    parts = total.reshape(4, -1, SLOTS, RANK, cut)
    placed = jnp.einsum("ag,ngrc->narc", place, jnp.transpose(parts, (1, 0, 2, 3, 4)).reshape(
        parts.shape[1], 4 * SLOTS, RANK, cut), precision=lax.Precision.HIGHEST)

    def narrow(items):
        size = items.shape[-1] // ctx_size
        return lax.dynamic_slice_in_dim(items, context * size, size, items.ndim - 1)

    def broad(items):
        joined = jnp.transpose(items, (1, 2, 0, 3)).reshape(ADAPTERS, RANK, -1)
        return narrow(joined)

    base = 3 + 2 * tiles
    return (
        narrow(jnp.concatenate([placed[base : base + 3], placed[:1]])),
        narrow(jnp.concatenate([placed[base + 3 : base + 6], placed[1:2]])),
        narrow(placed[2]),
        broad(placed[3 : 3 + tiles]),
        broad(placed[3 + tiles : base]),
        narrow(placed[base + 6]),
    )


def project(own, far, weight, bias, local):
    tokens, wide = own.shape
    blocks = 3 + (2 if far is not None else 0)

    def column(n):
        return jnp.where(n < 3, n, n - 2)

    def kernel(*refs):
        bias_ref, w_ref, out_ref = refs[-3:]

        def write(x_ref):
            at = pl.ds(pl.multiple_of(column(pl.program_id(0)) * local, local), local)
            out_ref[...] = (dot_nn(x_ref[...], w_ref[:, at]) + bias_ref[...]).astype(bf16)

        if far is None:
            write(refs[0])
        else:
            pl.when(pl.program_id(0) < 3)(lambda: write(refs[0]))
            pl.when(pl.program_id(0) >= 3)(lambda: write(refs[1]))

    rows = [own] if far is None else [own, far]
    return pl.pallas_call(
        kernel,
        grid=(blocks,),
        in_specs=[pl.BlockSpec((tokens, wide), lambda n: (0, 0))] * len(rows)
        + [
            pl.BlockSpec((1, local), lambda n: (0, column(n))),
            pl.BlockSpec(memory_space=pltpu.VMEM),
        ],
        out_specs=pl.BlockSpec((tokens, local), lambda n: (0, n)),
        out_shape=jax.ShapeDtypeStruct((tokens, blocks * local), bf16),
        compiler_params=pltpu.CompilerParams(vmem_limit_bytes=12 << 20),
        cost_estimate=HINT,
        name="project",
    )(*rows, bias, weight)


def expand(own, other, weight, bias):
    size, wide = own.shape
    hidden = weight.shape[1]
    cut = 512
    part = 128

    def kernel(own_ref, other_ref, w_ref, b_ref, h_ref, s_ref):
        for i, x_ref in enumerate((own_ref, other_ref)):
            for r in range(0, size, part):
                pre = dot_nn(x_ref[r : r + part, :], w_ref[...]) + b_ref[...]
                phi = 0.5 * (1.0 + lax.erf(pre * (2.0**-0.5)))
                bell = jnp.exp(-0.5 * pre * pre) * (0.5 / jnp.pi) ** 0.5
                to = slice(i * size + r, i * size + r + part)
                h_ref[to, :] = (pre * phi).astype(bf16)
                s_ref[to, :] = (phi + pre * bell).astype(bf16)

    block = pl.BlockSpec((2 * size, cut), lambda n: (0, n))
    shape = jax.ShapeDtypeStruct((2 * size, hidden), bf16)
    return pl.pallas_call(
        kernel,
        grid=(hidden // cut,),
        in_specs=[
            pl.BlockSpec((size, wide), lambda n: (0, 0)),
            pl.BlockSpec((size, wide), lambda n: (0, 0)),
            pl.BlockSpec((wide, cut), lambda n: (0, n)),
            pl.BlockSpec((1, cut), lambda n: (0, n)),
        ],
        out_specs=[block, block],
        out_shape=[shape, shape],
        compiler_params=pltpu.CompilerParams(vmem_limit_bytes=14 << 20),
        cost_estimate=HINT,
        name="expand",
    )(own, other, weight, bias)


def back_hidden(loss, weight, slope):
    tokens, wide = loss.shape
    hidden = weight.shape[0]
    cut = 512

    def kernel(x_ref, w_ref, s_ref, out_ref):
        grad = dot_nt(x_ref[...], w_ref[...])
        out_ref[...] = (grad * s_ref[...].astype(f32)).astype(bf16)

    block = pl.BlockSpec((tokens, cut), lambda n: (0, n))
    return pl.pallas_call(
        kernel,
        grid=(hidden // cut,),
        in_specs=[
            pl.BlockSpec((tokens, wide), lambda n: (0, 0)),
            pl.BlockSpec((cut, wide), lambda n: (n, 0)),
            block,
        ],
        out_specs=block,
        out_shape=jax.ShapeDtypeStruct((tokens, hidden), bf16),
        compiler_params=pltpu.CompilerParams(vmem_limit_bytes=36 << 20),
        cost_estimate=HINT,
        name="back_hidden",
    )(loss, weight, slope)


class Direct:
    def __init__(self, own, half_axis, context):
        size = own.shape[half_axis] // 2
        self.own = own
        self.part = lax.dynamic_slice_in_dim(own, context * size, size, half_axis)

    def first(self, *waits):
        part = gate(self.part, *waits)
        self.near = [
            lax.ppermute(part, "fsdp", [(i, i ^ k) for i in range(4)]) for k in range(1, 4)
        ]

    def second(self, *waits):
        *self.near, _ = lax.optimization_barrier((*self.near, waits))
        self.far = [lax.ppermute(piece, "ctx", SWAP_Y) for piece in self.near]

    def pieces(self):
        return (self.own, *[p for pair in zip(self.near, self.far) for p in pair])


class Ring:
    def __init__(self, own, half_axis, context, inner):
        size = own.shape[half_axis] // 2
        self.own = own
        self.inner = inner
        self.part = lax.dynamic_slice_in_dim(own, context * size, size, half_axis)

    def first(self, *waits):
        part = gate(self.part, *waits)
        self.one = lax.ppermute(part, "fsdp", [(0, 1), (1, 0), (2, 3), (3, 2)])
        self.across = lax.ppermute(part, "fsdp", [(1, 2), (2, 1)])

    def second(self, *waits):
        self.one, self.across, *_ = lax.optimization_barrier((self.one, self.across, *waits))
        self.y_one = lax.ppermute(self.one, "ctx", SWAP_Y)
        self.outward = lax.ppermute(self.across, "fsdp", [(1, 0), (2, 3)])
        self.back = lax.ppermute(self.one, "fsdp", [(1, 2), (2, 1)])

    def third(self, *waits):
        outward, self.back, self.y_one, across, *_ = lax.optimization_barrier(
            (self.outward, self.back, self.y_one, self.across, *waits)
        )
        self.two = jnp.where(self.inner, across, outward)
        self.y_two = lax.ppermute(self.two, "ctx", SWAP_Y)
        self.last = lax.ppermute(self.back, "fsdp", [(1, 0), (2, 3)])

    def fourth(self, *waits):
        last, self.y_two, back, *_ = lax.optimization_barrier(
            (self.last, self.y_two, self.back, *waits)
        )
        self.three = jnp.where(self.inner, back, last)
        self.y_three = lax.ppermute(self.three, "ctx", SWAP_Y)

    def pieces(self):
        return (
            self.own,
            self.one,
            self.y_one,
            self.two,
            self.y_two,
            self.three,
            self.y_three,
        )


def matmul(rows, half, weight, cut, flipped, parts=1):
    summed = rows.shape[1]
    steps = summed // cut
    wide = weight.shape[0] if flipped else weight.shape[1]
    size = rows.shape[0] // 2
    piece = size // parts

    def kernel(half_ref, x_ref, w_ref, *refs):
        outs = refs[:parts]
        part = dot_nt(x_ref[...], w_ref[...]) if flipped else dot_nn(x_ref[...], w_ref[...])

        def finish(total):
            for i, out_ref in enumerate(outs):
                out_ref[...] = total[i * piece : (i + 1) * piece].astype(bf16)

        if steps == 1:
            finish(part)
            return
        acc = refs[parts]
        step = pl.program_id(0)

        @pl.when(step == 0)
        def _():
            acc[...] = part

        @pl.when((step > 0) & (step < steps - 1))
        def _():
            acc[...] += part

        @pl.when(step == steps - 1)
        def _():
            finish(acc[...] + part)

    if flipped:
        w_spec = pl.BlockSpec((wide, cut), lambda k, h: (0, k))
    else:
        w_spec = pl.BlockSpec((cut, wide), lambda k, h: (k, 0))
    return pl.pallas_call(
        kernel,
        grid_spec=pltpu.PrefetchScalarGridSpec(
            num_scalar_prefetch=1,
            grid=(steps,),
            in_specs=[pl.BlockSpec((size, cut), lambda k, h: (h[0], k)), w_spec],
            out_specs=[pl.BlockSpec((piece, wide), lambda k, h: (0, 0))] * parts,
            scratch_shapes=[pltpu.VMEM((size, wide), f32)] if steps > 1 else [],
        ),
        out_shape=[jax.ShapeDtypeStruct((piece, wide), bf16)] * parts,
        compiler_params=pltpu.CompilerParams(vmem_limit_bytes=22 << 20),
        cost_estimate=HINT,
        name="matmul",
    )(half, rows, weight)


def back_attend(core, own, other, weight):
    size = own.shape[0]
    local = weight.shape[0]

    def kernel(core_ref, own_ref, other_ref, w_ref, out_ref):
        w = w_ref[...]
        mine = pl.multiple_of(core_ref[0] * size, size)
        theirs = pl.multiple_of((1 - core_ref[0]) * size, size)
        out_ref[pl.ds(mine, size), :] = dot_nt(own_ref[...], w).astype(bf16)
        out_ref[pl.ds(theirs, size), :] = dot_nt(other_ref[...], w).astype(bf16)

    whole = pl.BlockSpec(memory_space=pltpu.VMEM)
    return pl.pallas_call(
        kernel,
        grid_spec=pltpu.PrefetchScalarGridSpec(
            num_scalar_prefetch=1, grid=(), in_specs=[whole] * 3, out_specs=whole
        ),
        out_shape=jax.ShapeDtypeStruct((2 * size, local), bf16),
        compiler_params=pltpu.CompilerParams(vmem_limit_bytes=6 << 20),
        cost_estimate=HINT,
        name="back_attend",
    )(core, own, other, weight)


def gate(value, *waits):
    if not waits:
        return value
    return lax.optimization_barrier((value,) + waits)[0]


def make_body(ctx_size):
    pair_ctx = ctx_size == 2

    def body(
        inputs,
        loss_sensitivity,
        parent_block,
        adapter_of,
        w_qkv,
        bias_qv,
        w_o,
        exit_offsets,
        ln_gain,
        ln_bias,
        w_in,
        hidden_offset_frozen,
        w_out,
        a_attn,
        b_attn,
        a_up,
        b_up,
        a_down,
        b_down,
    ):
        group = lax.axis_index("fsdp")
        context = lax.axis_index("ctx")
        tensor = lax.axis_index("tp")
        core = tensor % 2
        tokens, width = inputs.shape
        half = tokens // 2
        local = w_qkv.shape[2]
        shard = w_qkv.shape[1]
        hidden_local = w_in.shape[1]
        heads = local // HD
        blocks = tokens // BLOCK
        scale = HD ** (-0.5)
        wide = width + AUG

        def on(value, axis, pairs):
            return lax.ppermute(value, axis, pairs)

        def own_rows(matrix):
            return lax.dynamic_slice_in_dim(matrix, core * half, half, 0)

        def other_rows(matrix):
            return lax.dynamic_slice_in_dim(matrix, (1 - core) * half, half, 0)

        def natural(own, other):
            return jnp.concatenate(
                [jnp.where(core == 0, own, other), jnp.where(core == 0, other, own)], axis=0
            )

        def local_lanes(matrix):
            return lax.dynamic_slice_in_dim(matrix, tensor * local, local, matrix.ndim - 1)

        def put(buffer, piece, row, column):
            return lax.dynamic_update_slice(buffer, piece, (row, column))

        swap_y = [(0, 1), (1, 0)]
        spot = jnp.stack([group, context]).astype(jnp.int32)

        def send_tp(others, own_low, *waits):
            mine = join(own_low, [on(other, "tp", CORE_SWAP) for other in others])
            return mine, on(gate(mine, *waits), "tp", X_SWAP)

        def sum_sent(sent, waits=()):
            mine, far = sent
            return mine.astype(f32) + gate(far, *waits).astype(f32)

        pair = lax.dynamic_slice_in_dim(adapter_of, group * SLOTS, SLOTS)

        def pick_pair(array, axis):
            return jnp.concatenate(
                [lax.dynamic_slice_in_dim(array, pair[s], 1, axis) for s in range(SLOTS)], axis
            )

        a_pair = jnp.swapaxes(pick_pair(a_attn, 1), 2, 3)
        def down_up_pad(matrix, before=0):
            return jnp.pad(matrix, ((before, AUG - before - matrix.shape[0]), (0, 0)))

        a_qkv_rows = down_up_pad(a_pair[:3].reshape(3 * PAIR, width).astype(bf16))
        a_o_rows = local_lanes(a_pair[3].reshape(PAIR, width)).astype(bf16)
        b_pair = pick_pair(b_attn, 1)
        b_qkv_rows = local_lanes(b_pair[:3]).reshape(3, PAIR, local).astype(bf16)
        b_o_rows = down_up_pad(b_pair[3].reshape(PAIR, width).astype(bf16), PAIR)
        a_up_rows = down_up_pad(
            jnp.swapaxes(pick_pair(a_up, 0), 1, 2).reshape(PAIR, width).astype(bf16)
        )
        b_up_rows = pick_pair(b_up, 0).reshape(PAIR, hidden_local).astype(bf16)
        a_down_rows = (
            jnp.swapaxes(pick_pair(a_down, 0), 1, 2).reshape(PAIR, hidden_local).astype(bf16)
        )
        b_down_rows = down_up_pad(pick_pair(b_down, 0).reshape(PAIR, width).astype(bf16))

        def bias_lanes(opened):
            count = opened.shape[1]
            block = jnp.arange(count * BLOCK, dtype=jnp.int32) // BLOCK
            hit = opened[:, :, None] & (block[None, None, :] == jnp.arange(count)[None, :, None])
            return jnp.where(jnp.any(hit, axis=1), 0.0, neg_fill).astype(f32)

        reach, slot = ancestry(parent_block[0])
        all_blocks = reach.shape[0]
        first_block = context * blocks
        far_blocks = blocks if pair_ctx else all_blocks
        reach_rows = lax.dynamic_slice_in_dim(reach, first_block, blocks, 0)
        block_ids = jnp.arange(far_blocks, dtype=jnp.int32)
        far_open = (reach_rows[:, :far_blocks] > 0.5) & (block_ids[None, :] < first_block)
        own_open = lax.dynamic_slice_in_dim(reach_rows, first_block, blocks, 1) > 0.5
        far_bias = bias_lanes(far_open)
        own_bias = bias_lanes(own_open)

        slots = lax.dynamic_slice_in_dim(slot, first_block, blocks).astype(jnp.int32)
        lane_slot = (jnp.arange(AUG, dtype=jnp.int32) // RANK) % SLOTS

        def picks(first_row, count):
            block = (jnp.arange(count, dtype=jnp.int32) + first_row) // BLOCK
            row_slot = jnp.sum(
                jnp.where(block[:, None] == jnp.arange(blocks)[None, :], slots[None, :], 0), axis=1
            )
            return (row_slot[:, None] == lane_slot[None, :]).astype(f32)

        pick_own = picks(core * half, half)

        gain_one, shift_one = ln_gain[0][None, :], ln_bias[0][None, :]
        gain_two, shift_two = ln_gain[1][None, :], ln_bias[1][None, :]

        def widen(low, tail):
            return jnp.concatenate([low, tail], axis=1)

        def own_norm(places):
            return norm_wide([inputs], places, slots, a_qkv_rows, gain_one, shift_one, tokens)

        q_aug = jnp.concatenate(
            [jnp.pad(b_qkv_rows[i], ((0, 0), (i * local, (2 - i) * local))) for i in range(3)]
            + [jnp.zeros((AUG - 3 * PAIR, 3 * local), bf16)],
            axis=0,
        )
        o_aug = down_up_pad(a_o_rows, PAIR).T
        in_aug = down_up_pad(b_up_rows)
        out_aug = down_up_pad(a_down_rows).T
        if pair_ctx:
            quarter = tokens // 4
            sent = lax.dynamic_slice_in_dim(inputs, tensor * quarter, quarter, 0)
            far_quarter = on(sent, "ctx", [(0, 1)])

            far_places = jnp.stack([tensor, tensor ^ 2, tensor ^ 1, tensor ^ 3]).astype(jnp.int32)
            inner = (group == 1) | (group == 2)
            q_ring = Ring(w_qkv, 1, context, inner)
            o_ring = Direct(w_o, 0, context)
            in_ring = Ring(w_in, 0, context, inner)
            out_ring = Ring(w_out, 0, context, inner)
            q_ring.first()
            q_ring.second()
            q_ring.third(far_quarter)
            normed_wide = own_norm(gate(jnp.arange(4, dtype=jnp.int32), q_ring.y_one))
            far_quarter, _ = lax.optimization_barrier((far_quarter, q_ring.two))
            far_x = on(far_quarter, "tp", X_SWAP)
            far_core = on(far_quarter, "tp", CORE_SWAP)
            far_x, far_core, normed_wide, _ = lax.optimization_barrier(
                (far_x, far_core, normed_wide, q_ring.last)
            )
            q_ring.fourth(normed_wide)
            o_ring.first(q_ring.last)
            far_both = on(far_x, "tp", CORE_SWAP)
            far_wide = norm_wide(
                [far_quarter, far_x, far_core, far_both],
                far_places,
                slot[:blocks].astype(jnp.int32),
                a_qkv_rows,
                gain_one,
                shift_one,
                tokens,
            )
            o_ring.second(q_ring.y_three, far_wide)
            in_ring.first(*o_ring.near)
            q_full = assemble(
                gate(spot, *o_ring.near, far_wide),
                q_ring.pieces(),
                q_aug,
                wide,
                3 * local,
                ("rows", shard, shard // 2),
                3,
            )
        else:
            normed_wide = own_norm(jnp.arange(4, dtype=jnp.int32))
            own_q = jnp.transpose(w_qkv, (1, 0, 2)).reshape(shard, 3 * local)
            q_full = jnp.concatenate([lax.all_gather(own_q, "fsdp", axis=0, tiled=True), q_aug], 0)
            o_full = jnp.concatenate([lax.all_gather(w_o, "fsdp", axis=1, tiled=True), o_aug], 1)
            in_full = jnp.concatenate([lax.all_gather(w_in, "fsdp", axis=0, tiled=True), in_aug], 0)
            out_full = jnp.concatenate(
                [lax.all_gather(w_out, "fsdp", axis=1, tiled=True), out_aug], 1
            )

        normed, reduced_qkv = normed_wide[:, :width], normed_wide[:, width:]
        zero_bias = jnp.zeros((local,), f32)
        q_bias = jnp.concatenate([bias_qv[0], zero_bias, bias_qv[1]])[None, :]
        if pair_ctx:
            qkv = project(normed_wide, far_wide, q_full, q_bias, local)
            far_kv = qkv
            far_base = 3 * heads
            qkv, *_ = lax.optimization_barrier((qkv, in_ring.one, in_ring.across, *o_ring.far))
            in_ring.second(qkv)
            far_kv = qkv
        else:
            qkv = project(normed_wide, None, q_full, q_bias, local)
            far_kv = lax.all_gather(qkv[:, local:], "ctx", axis=0, tiled=True)
            far_base = 0

        attended_f, attended, probs_far, probs_own = attend_forward(
            qkv, far_kv, far_base, far_bias, own_bias, heads, scale
        )
        if pair_ctx:
            in_ring.third(attended)
            o_full = assemble(
                gate(spot, attended),
                o_ring.pieces(),
                o_aug,
                local,
                wide,
                ("columns", shard, local // 2),
                0,
                True,
            )
        core_id = core.astype(jnp.int32)[None]
        other_id = 1 - core_id
        branch_sent = send_tp(
            matmul(attended, other_id, o_full, local, False),
            matmul(attended, core_id, o_full, local, False)[0],
        )
        branch_far = branch_sent[1]
        if pair_ctx:
            in_ring.fourth(branch_sent[0])
            out_ring.first(in_ring.last, branch_sent[0])
            branch_far = gate(branch_far, in_ring.y_three, out_ring.one, out_ring.across)
        middle, two_own = row_call(
            after_attention,
            "after_attention",
            core_id,
            slots,
            half,
            [(branch_sent[0], False), (branch_far, False), (inputs, True)],
            [exit_offsets[:1], gain_two, shift_two, b_o_rows, a_up_rows],
            [(width, f32), (wide, bf16)],
        )
        two_other = on(two_own, "tp", CORE_SWAP)

        if pair_ctx:
            out_ring.second(in_ring.y_three)
            in_full = assemble(
                gate(spot, out_ring.outward, out_ring.back),
                in_ring.pieces(),
                in_aug,
                wide,
                hidden_local,
                ("rows", shard, shard // 2),
                0,
            )
        hidden, slope = expand(two_own, two_other, in_full, hidden_offset_frozen[None, :])
        if pair_ctx:
            out_ring.third()
            out_ring.fourth()
            out_full = assemble(
                gate(spot, hidden),
                out_ring.pieces(),
                out_aug,
                hidden_local,
                wide,
                ("columns", shard, hidden_local // 2),
                0,
            )

        loss_own = own_rows(loss_sensitivity)
        loss_rel = jnp.concatenate([loss_own, other_rows(loss_sensitivity)], axis=0)
        pick_rel = jnp.concatenate([pick_own, picks((1 - core) * half, half)], axis=0)
        grad_down_down = (factor * dot_nt(loss_rel, b_down_rows) * pick_rel).astype(bf16)
        loss_wide = widen(loss_rel, grad_down_down)
        grad_pre = back_hidden(loss_wide, out_full, slope)
        first_id = jnp.zeros((1,), jnp.int32)
        second_id = first_id + 1
        ff_cut = hidden_local // 2
        two_sent = send_tp(
            matmul(grad_pre, second_id, in_full, ff_cut, True),
            matmul(grad_pre, first_id, in_full, ff_cut, True)[0],
        )
        late_hidden = gate(hidden, two_sent[0])
        exit_sent = send_tp(
            matmul(late_hidden, second_id, out_full, ff_cut, False, 2),
            matmul(late_hidden, first_id, out_full, ff_cut, False)[0],
            two_sent[1],
        )
        grad_middle, back_own = row_call(
            back_middle,
            "back_middle",
            core_id,
            slots,
            half,
            [
                (two_sent[0], False),
                (gate(two_sent[1], exit_sent[0]), False),
                (middle, False),
                (loss_sensitivity, True),
            ],
            [gain_two, a_up_rows, b_o_rows],
            [(width, f32), (wide, bf16)],
        )
        back_other = on(back_own, "tp", CORE_SWAP)
        grad_attended = back_attend(core_id, back_own, back_other, o_full)

        grad_q, grad_k, grad_v, far_grads = attend_backward(
            qkv, far_kv, far_base, grad_attended, attended_f, probs_far, probs_own, heads, scale
        )
        if pair_ctx:
            more = on(far_grads, "ctx", [(1, 0)])
        else:
            more = lax.psum_scatter(far_grads, "ctx", scatter_dimension=1, tiled=True)
        layer_own, down_own = row_call(
            after_hidden,
            "after_hidden",
            core_id,
            slots,
            half,
            [(exit_sent[0], False), (exit_sent[1], False), (middle, False)],
            [exit_offsets[1:], b_down_rows],
            [(width, bf16), (AUG, bf16)],
        )
        down_other = on(down_own, "tp", CORE_SWAP)
        tiles = hidden_local // local

        def to_owners(slabs):
            pieces = [
                lax.dynamic_index_in_dim(slabs, group ^ k, 0, keepdims=False) for k in range(4)
            ]
            return jnp.stack(
                pieces[:1]
                + [on(pieces[k], "fsdp", [(i, i ^ k) for i in range(4)]) for k in range(1, 4)]
            )

        tensor_id, core_at = tensor.astype(jnp.int32), core.astype(jnp.int32)
        packed = pack_terms(
            tensor_id,
            core_at,
            (two_own, two_other),
            (back_own, back_other),
            attended,
            grad_pre,
            hidden,
            grad_down_down,
            local,
        )
        packed_layer = pack_layer(
            tensor_id, core_at, (down_own, down_other), loss_sensitivity, local
        )
        grad_k = gate(grad_k, packed, packed_layer)
        grad_qkv = jnp.concatenate(
            [
                grad_q,
                (grad_k.astype(f32) + more[0].astype(f32)).astype(bf16),
                (grad_v.astype(f32) + more[1].astype(f32)).astype(bf16),
            ],
            axis=1,
        )
        low_part = dot_nt(grad_qkv, q_full[width:]).astype(bf16)
        low_core = on(low_part, "tp", CORE_SWAP)
        low_pair = round_low(low_part.astype(f32) + low_core.astype(f32))
        low_far = on(low_pair, "tp", X_SWAP)
        low_sum = low_pair.astype(f32) + low_far.astype(f32)
        grad_down_qkv = (factor * low_sum * picks(0, tokens)).astype(bf16)
        one_other, one_own = back_project(
            gate(grad_qkv, low_part), core_id, q_full, width
        )
        one_sent = send_tp([one_other], one_own, low_far)
        layer_other = on(layer_own, "tp", CORE_SWAP)
        layer_out = place_rows(core_id, layer_own, layer_other, width)
        near = to_owners(packed)
        near_qkv = to_owners(
            jnp.concatenate(
                [
                    pack_projections(tensor_id[None], grad_down_qkv, normed_wide, grad_qkv, local),
                    packed_layer,
                ],
                axis=1,
            )
        )
        holder = jnp.stack([group ^ k for k in range(4)])
        owner = adapter_of.reshape(4, SLOTS)[holder].reshape(4 * SLOTS)
        if pair_ctx:
            adapter_grads = unpack_terms(
                context.astype(jnp.int32)[None],
                owner,
                (near, near_qkv),
                (on(near, "ctx", swap_y), on(near_qkv, "ctx", swap_y)),
                tiles,
            )
        else:
            total = lax.psum((near.astype(f32), near_qkv.astype(f32)), "ctx")
            adapter_grads = unpack_plain(
                context, owner, jnp.concatenate(total, axis=1), tiles, ctx_size
            )
        (grad_own,) = row_call(
            back_first,
            "back_first",
            core_id,
            slots,
            half,
            [
                (one_sent[0], False),
                (gate(one_sent[1], adapter_grads[0], layer_out), False),
                (grad_down_qkv, True),
                (inputs, True),
                (grad_middle, False),
            ],
            [gain_one, a_qkv_rows],
            [(width, bf16)],
        )
        grad_other = on(grad_own, "tp", CORE_SWAP)
        grad_inputs = place_rows(core_id, grad_own, grad_other, width)

        out_a_attn, out_b_attn, out_a_up, out_b_up, out_a_down, out_b_down = adapter_grads
        return (
            layer_out,
            grad_inputs,
            jnp.swapaxes(out_a_attn, 2, 3),
            out_b_attn,
            jnp.swapaxes(out_a_up, 1, 2),
            out_b_up,
            jnp.swapaxes(out_a_down, 1, 2),
            out_b_down,
        )

    return body


def solution(mesh):
    in_specs = (
        P(("fsdp", "ctx"), None),
        P(("fsdp", "ctx"), None),
        P("fsdp", None),
        P(),
        P(None, "fsdp", "tp"),
        P(None, "tp"),
        P("tp", "fsdp"),
        P(),
        P(),
        P(),
        P("fsdp", "tp"),
        P("tp"),
        P("tp", "fsdp"),
        P(),
        P(),
        P(),
        P(None, None, "tp"),
        P(None, "tp", None),
        P(),
    )
    out_specs = (
        P(("fsdp", "ctx"), None),
        P(("fsdp", "ctx"), None),
        P(None, None, ("tp", "fsdp", "ctx"), None),
        P(None, None, None, ("tp", "fsdp", "ctx")),
        P(None, ("tp", "fsdp", "ctx"), None),
        P(None, None, ("tp", "fsdp", "ctx")),
        P(None, ("tp", "fsdp", "ctx"), None),
        P(None, None, ("tp", "fsdp", "ctx")),
    )
    return jax.shard_map(
        make_body(mesh.shape["ctx"]),
        mesh=mesh,
        in_specs=in_specs,
        out_specs=out_specs,
        check_vma=False,
    )
```

```python
import jax
import jax.numpy as jnp
from jax import lax
from jax.experimental import pallas as pl
from jax.experimental.pallas import tpu as pltpu
from jax.sharding import PartitionSpec as P

HD = 128
RANK = 16
ADAPTERS = 8
SLOTS = 2
PAIR = SLOTS * RANK
BLOCK = 256
AUG = 128
ROW_CHUNK = 128
HINT = pl.CostEstimate(flops=1, transcendentals=0, bytes_accessed=1)

layer_eps = 1e-05
factor = 0.5
neg_fill = -1e30
bf16 = jnp.bfloat16
f32 = jnp.float32

CORE_SWAP = [(0, 1), (1, 0), (2, 3), (3, 2)]
SWAP_Y = [(0, 1), (1, 0)]
X_SWAP = [(0, 2), (2, 0), (1, 3), (3, 1)]


def dot_nn(a, b):
    return lax.dot_general(a, b, (((1,), (0,)), ((), ())), preferred_element_type=f32)


def dot_nt(a, b):
    return lax.dot_general(a, b, (((1,), (1,)), ((), ())), preferred_element_type=f32)


def dot_tn(a, b):
    return lax.dot_general(a, b, (((0,), (0,)), ((), ())), preferred_element_type=f32)


def round_low(v):
    return lax.reduce_precision(v, 8, 7).astype(bf16)


def standardize(rows):
    centre = rows - jnp.mean(rows, axis=-1, keepdims=True)
    spread = jnp.mean(centre * centre, axis=-1, keepdims=True)
    inverse = lax.rsqrt(spread + layer_eps)
    return centre * inverse, inverse


def norm_back(grad_scaled, unit, inverse):
    first = jnp.mean(grad_scaled, axis=-1, keepdims=True)
    second = jnp.mean(grad_scaled * unit, axis=-1, keepdims=True)
    return inverse * (grad_scaled - first - unit * second)


def ancestry(parents):
    total = parents.shape[0]
    position = jnp.arange(total, dtype=jnp.int32)
    reach = (
        (parents[:, None] == position[None, :]) | (position[:, None] == position[None, :])
    ).astype(f32)
    span = 1
    while span < total:
        reach = jnp.minimum(jnp.sum(reach[:, :, None] * reach[None, :, :], axis=1), 1.0)
        span *= 2
    roots = (parents < 0).astype(f32)
    order = jnp.sum(jnp.where(position[None, :] <= position[:, None], roots[None, :], 0.0), axis=1)
    slot = jnp.sum(reach * (roots * (order - 1.0))[None, :], axis=1)
    return reach, slot


def attend_forward(qkv, far, far_base, far_bias, own_bias, heads, scale):
    tokens = qkv.shape[0]
    far_rows = far.shape[0]
    blocks = tokens // BLOCK

    def kernel(q_ref, k_ref, v_ref, fk_ref, fv_ref, fb_ref, ob_ref, o_ref, low_ref, pf_ref, po_ref):
        far_k = fk_ref[...]
        far_v = fv_ref[...]
        for b in range(blocks):
            rows = slice(b * BLOCK, (b + 1) * BLOCK)
            width = (b + 1) * BLOCK
            q = q_ref[rows, :]
            s_far = dot_nt(q, far_k) * scale + fb_ref[b : b + 1, :]
            s_own = dot_nt(q, k_ref[:width, :]) * scale + ob_ref[b : b + 1, :width]
            q_pos = lax.broadcasted_iota(jnp.int32, (BLOCK, width), 0) + b * BLOCK
            k_pos = lax.broadcasted_iota(jnp.int32, (BLOCK, width), 1)
            s_own = jnp.where(k_pos <= q_pos, s_own, neg_fill)
            top = jnp.maximum(
                jnp.max(s_far, axis=1, keepdims=True), jnp.max(s_own, axis=1, keepdims=True)
            )
            p_far = jnp.exp(s_far - top)
            p_own = jnp.exp(s_own - top)
            total = jnp.sum(p_far, axis=1, keepdims=True) + jnp.sum(p_own, axis=1, keepdims=True)
            inverse = 1.0 / total
            p_far = (p_far * inverse).astype(bf16)
            p_own = (p_own * inverse).astype(bf16)
            pf_ref[0, rows, :] = p_far
            po_ref[0, rows, :width] = p_own
            mixed = dot_nn(p_far, far_v) + dot_nn(p_own, v_ref[:width, :])
            o_ref[rows, :] = mixed
            low_ref[rows, :] = mixed.astype(bf16)

    return pl.pallas_call(
        kernel,
        grid=(heads,),
        in_specs=[
            pl.BlockSpec((tokens, HD), lambda h: (0, h)),
            pl.BlockSpec((tokens, HD), lambda h: (0, heads + h)),
            pl.BlockSpec((tokens, HD), lambda h: (0, 2 * heads + h)),
            pl.BlockSpec((far_rows, HD), lambda h: (0, far_base + h)),
            pl.BlockSpec((far_rows, HD), lambda h: (0, far_base + heads + h)),
            pl.BlockSpec((blocks, far_rows), lambda h: (0, 0)),
            pl.BlockSpec((blocks, tokens), lambda h: (0, 0)),
        ],
        out_specs=[
            pl.BlockSpec((tokens, HD), lambda h: (0, h)),
            pl.BlockSpec((tokens, HD), lambda h: (0, h)),
            pl.BlockSpec((1, tokens, far_rows), lambda h: (h, 0, 0)),
            pl.BlockSpec((1, tokens, tokens), lambda h: (h, 0, 0)),
        ],
        out_shape=[
            jax.ShapeDtypeStruct((tokens, heads * HD), f32),
            jax.ShapeDtypeStruct((tokens, heads * HD), bf16),
            jax.ShapeDtypeStruct((heads, tokens, far_rows), bf16),
            jax.ShapeDtypeStruct((heads, tokens, tokens), bf16),
        ],
        compiler_params=pltpu.CompilerParams(vmem_limit_bytes=(44 if far_rows == tokens else 56) << 20),
        cost_estimate=HINT,
        name="attend_forward",
    )(qkv, qkv, qkv, far, far, far_bias, own_bias)


def attend_backward(qkv, far, far_base, grad_attended, attended, probs_far, probs_own, heads, scale):
    tokens = qkv.shape[0]
    far_rows = far.shape[0]
    blocks = tokens // BLOCK

    def kernel(
        q_ref, k_ref, v_ref, fk_ref, fv_ref, g_ref, o_ref, pf_ref, po_ref,
        dq_ref, dk_ref, dv_ref, far_ref,
        dk_acc, dv_acc, dfk_acc, dfv_acc,
    ):
        far_k = fk_ref[...]
        far_v = fv_ref[...]
        for b in reversed(range(blocks)):
            first = b == blocks - 1
            rows = slice(b * BLOCK, (b + 1) * BLOCK)
            width = (b + 1) * BLOCK
            q = q_ref[rows, :]
            g = g_ref[rows, :]
            row_dot = jnp.sum(g.astype(f32) * o_ref[rows, :], axis=1, keepdims=True)
            p_far = pf_ref[0, rows, :]
            p_own = po_ref[0, rows, :width]
            d_far = (p_far.astype(f32) * (dot_nt(g, far_v) - row_dot)).astype(bf16)
            d_own = (p_own.astype(f32) * (dot_nt(g, v_ref[:width, :]) - row_dot)).astype(bf16)
            dq_ref[rows, :] = (
                (dot_nn(d_far, far_k) + dot_nn(d_own, k_ref[:width, :])) * scale
            ).astype(bf16)
            if first:
                dfk_acc[...] = dot_tn(d_far, q)
                dfv_acc[...] = dot_tn(p_far, g)
                dk_acc[...] = dot_tn(d_own, q)
                dv_acc[...] = dot_tn(p_own, g)
            else:
                dfk_acc[...] += dot_tn(d_far, q)
                dfv_acc[...] += dot_tn(p_far, g)
                dk_acc[:width, :] += dot_tn(d_own, q)
                dv_acc[:width, :] += dot_tn(p_own, g)
        dk_ref[...] = (dk_acc[...] * scale).astype(bf16)
        dv_ref[...] = dv_acc[...].astype(bf16)
        far_ref[0] = (dfk_acc[...] * scale).astype(bf16)
        far_ref[1] = dfv_acc[...].astype(bf16)

    head_spec = pl.BlockSpec((tokens, HD), lambda h: (0, h))
    far_spec = pl.BlockSpec((2, far_rows, HD), lambda h: (0, 0, h))
    own_shape = jax.ShapeDtypeStruct((tokens, heads * HD), bf16)
    far_shape = jax.ShapeDtypeStruct((2, far_rows, heads * HD), bf16)
    return pl.pallas_call(
        kernel,
        grid=(heads,),
        in_specs=[
            head_spec,
            pl.BlockSpec((tokens, HD), lambda h: (0, heads + h)),
            pl.BlockSpec((tokens, HD), lambda h: (0, 2 * heads + h)),
            pl.BlockSpec((far_rows, HD), lambda h: (0, far_base + h)),
            pl.BlockSpec((far_rows, HD), lambda h: (0, far_base + heads + h)),
            head_spec,
            head_spec,
            pl.BlockSpec((1, tokens, far_rows), lambda h: (h, 0, 0)),
            pl.BlockSpec((1, tokens, tokens), lambda h: (h, 0, 0)),
        ],
        out_specs=[head_spec, head_spec, head_spec, far_spec],
        out_shape=[own_shape, own_shape, own_shape, far_shape],
        scratch_shapes=[
            pltpu.VMEM((tokens, HD), f32),
            pltpu.VMEM((tokens, HD), f32),
            pltpu.VMEM((far_rows, HD), f32),
            pltpu.VMEM((far_rows, HD), f32),
        ],
        compiler_params=pltpu.CompilerParams(vmem_limit_bytes=(44 if far_rows == tokens else 56) << 20),
        cost_estimate=HINT,
        name="attend_backward",
    )(qkv, qkv, qkv, far, far, grad_attended, attended, probs_far, probs_own)


def assemble(spot, pieces, tail, rows, columns, step, parts, straight=False):
    direction, shard, half_rows = step
    count = max(parts, 1)
    part_columns = columns // count if parts else columns
    tail_rows, tail_columns = tail.shape

    def kernel(spot_ref, *refs):
        own, one, y_one, two, y_two, three, y_three, tail_ref, out, sem = refs
        group = spot_ref[0]
        context = spot_ref[1]
        inner = (group == 1) | (group == 2)

        def moves(piece, source, which, first):
            made = []
            for i in range(count):
                src = piece.at[i] if parts else piece
                n, m = src.shape
                if direction == "rows":
                    row = pl.multiple_of(source * shard + which * half_rows, half_rows)
                    dst = out.at[pl.ds(row, n), pl.ds(i * part_columns, m)]
                else:
                    row = pl.multiple_of(which * half_rows, half_rows)
                    col = pl.multiple_of(source * shard, shard)
                    dst = out.at[pl.ds(row, n), pl.ds(col, m)]
                made.append(pltpu.make_async_copy(src, dst, sem.at[first + i]))
            return made

        fixed = moves(own, group, 0, 0)
        fixed += moves(one, group ^ 1, context, count)
        fixed += moves(y_one, group ^ 1, 1 - context, 2 * count)
        second = group ^ 2 if straight else jnp.where(inner, group ^ 3, group ^ 2)
        third = group ^ 3 if straight else jnp.where(inner, group ^ 2, group ^ 3)
        fixed += moves(two, second, context, 3 * count)
        fixed += moves(y_two, second, 1 - context, 4 * count)
        fixed += moves(three, third, context, 5 * count)
        fixed += moves(y_three, third, 1 - context, 6 * count)
        row0 = rows - tail_rows if direction == "rows" else 0
        col0 = 0 if direction == "rows" else columns - tail_columns
        fixed.append(
            pltpu.make_async_copy(
                tail_ref,
                out.at[pl.ds(row0, tail_rows), pl.ds(col0, tail_columns)],
                sem.at[7 * count],
            )
        )
        for move in fixed:
            move.start()

        for move in fixed:
            move.wait()

    return pl.pallas_call(
        kernel,
        grid_spec=pltpu.PrefetchScalarGridSpec(
            num_scalar_prefetch=1,
            grid=(),
            in_specs=[pl.BlockSpec(memory_space=pltpu.HBM)] * 8,
            out_specs=pl.BlockSpec(memory_space=pltpu.VMEM),
            scratch_shapes=[pltpu.SemaphoreType.DMA((7 * count + 1,))],
        ),
        out_shape=jax.ShapeDtypeStruct((rows, columns), bf16),
        compiler_params=pltpu.CompilerParams(vmem_limit_bytes=4 << 20),
        cost_estimate=HINT,
        name="assemble",
    )(spot, *pieces, tail)


def norm_wide(pieces, places, slots, down_rows, gain, shift, tokens):
    width = gain.shape[1]
    blocks = tokens // BLOCK
    count = len(pieces)
    quarter = tokens // 4
    steps = 4 // count

    def kernel(place_ref, slot_ref, *refs):
        down_ref, gain_ref, shift_ref, out_ref = refs[count:]
        for i in range(4):
            x_ref = refs[i // steps]
            first = (i % steps) * quarter
            rows = x_ref[first : first + quarter, :].astype(f32)
            start = pl.multiple_of(place_ref[i] * quarter, quarter)
            unit, _ = standardize(rows)
            low = (unit * gain_ref[...] + shift_ref[...]).astype(bf16)
            block = (lax.broadcasted_iota(jnp.int32, (quarter, AUG), 0) + start) // BLOCK
            lane_slot = (lax.broadcasted_iota(jnp.int32, (quarter, AUG), 1) // RANK) % SLOTS
            slot = jnp.zeros((quarter, AUG), jnp.int32)
            for b in range(blocks):
                slot = jnp.where(block == b, slot_ref[b], slot)
            down = jnp.where(slot == lane_slot, dot_nt(low, down_ref[...]), 0.0)
            out_ref[pl.ds(start, quarter), :width] = low
            out_ref[pl.ds(start, quarter), width:] = factor * down.astype(bf16)

    whole = pl.BlockSpec(memory_space=pltpu.VMEM)
    return pl.pallas_call(
        kernel,
        grid_spec=pltpu.PrefetchScalarGridSpec(
            num_scalar_prefetch=2,
            grid=(),
            in_specs=[whole] * (count + 3),
            out_specs=whole,
        ),
        out_shape=jax.ShapeDtypeStruct((tokens, width + AUG), bf16),
        compiler_params=pltpu.CompilerParams(vmem_limit_bytes=12 << 20),
        cost_estimate=HINT,
        name="norm_wide",
    )(places, slots, *pieces, down_rows, gain, shift)


def own_pick(first_row, count, slot_ref, blocks):
    block = (lax.broadcasted_iota(jnp.int32, (count, AUG), 0) + first_row) // BLOCK
    lane_slot = (lax.broadcasted_iota(jnp.int32, (count, AUG), 1) // RANK) % SLOTS
    slot = jnp.zeros((count, AUG), jnp.int32)
    for b in range(blocks):
        slot = jnp.where(block == b, slot_ref[b], slot)
    return slot == lane_slot


def row_call(body, name, core, slots, rows, moving, fixed, outs):
    chunk = ROW_CHUNK
    steps = rows // chunk
    blocks = slots.shape[0]
    n_in = len(moving) + len(fixed)

    def kernel(core_ref, slot_ref, *refs):
        first = core_ref[0] * rows + pl.program_id(0) * chunk
        pick = own_pick(first, chunk, slot_ref, blocks)
        results = body(pick, *[r[...] for r in refs[:n_in]])
        for ref, value in zip(refs[n_in:], results):
            ref[...] = value

    specs = []
    for array, offset in moving:
        if offset:
            specs.append(
                pl.BlockSpec((chunk, array.shape[1]), lambda i, c, s: (c[0] * steps + i, 0))
            )
        else:
            specs.append(pl.BlockSpec((chunk, array.shape[1]), lambda i, c, s: (i, 0)))
    for array in fixed:
        specs.append(pl.BlockSpec(array.shape, lambda i, c, s: (0, 0)))
    return pl.pallas_call(
        kernel,
        grid_spec=pltpu.PrefetchScalarGridSpec(
            num_scalar_prefetch=2,
            grid=(steps,),
            in_specs=specs,
            out_specs=[pl.BlockSpec((chunk, c), lambda i, c_, s: (i, 0)) for c, _ in outs],
        ),
        out_shape=[jax.ShapeDtypeStruct((rows, c), d) for c, d in outs],
        compiler_params=pltpu.CompilerParams(vmem_limit_bytes=12 << 20),
        cost_estimate=HINT,
        name=name,
    )(core, slots, *[a for a, _ in moving], *fixed)


def join(mine, got):
    piece = got[0].shape[0]

    def kernel(a_ref, *refs):
        out_ref, sum_ref, sem = refs[len(got) :]
        for i, b_ref in enumerate(refs[: len(got)]):
            rows = slice(i * piece, (i + 1) * piece)
            sum_ref[rows, :] = (a_ref[rows, :].astype(f32) + b_ref[...].astype(f32)).astype(bf16)
        move = pltpu.make_async_copy(sum_ref, out_ref, sem)
        move.start()
        move.wait()

    whole = pl.BlockSpec(memory_space=pltpu.VMEM)
    return pl.pallas_call(
        kernel,
        in_specs=[whole] * (1 + len(got)),
        out_specs=pl.BlockSpec(memory_space=pltpu.HBM),
        out_shape=jax.ShapeDtypeStruct(mine.shape, bf16),
        scratch_shapes=[pltpu.VMEM(mine.shape, bf16), pltpu.SemaphoreType.DMA],
        compiler_params=pltpu.CompilerParams(vmem_limit_bytes=8 << 20),
        cost_estimate=HINT,
        name="join",
    )(mine, *got)


def back_project(grad, core, weight, width):
    tokens, summed = grad.shape
    size = tokens // 2

    def kernel(core_ref, x_ref, w_ref, other_ref, own_ref):
        part = dot_nt(x_ref[...], w_ref[...]).astype(bf16)

        @pl.when(pl.program_id(0) == 0)
        def _():
            other_ref[...] = part

        @pl.when(pl.program_id(0) == 1)
        def _():
            own_ref[...] = part

    whole = pl.BlockSpec((size, width), lambda n, c: (0, 0))
    shape = jax.ShapeDtypeStruct((size, width), bf16)
    return pl.pallas_call(
        kernel,
        grid_spec=pltpu.PrefetchScalarGridSpec(
            num_scalar_prefetch=1,
            grid=(2,),
            in_specs=[
                pl.BlockSpec((size, summed), lambda n, c: (jnp.where(n == 0, 1 - c[0], c[0]), 0)),
                pl.BlockSpec((width, summed), lambda n, c: (0, 0)),
            ],
            out_specs=[whole, whole],
        ),
        out_shape=[shape, shape],
        compiler_params=pltpu.CompilerParams(vmem_limit_bytes=26 << 20),
        cost_estimate=HINT,
        name="back_project",
    )(core, grad, weight)


def place_rows(core, own, other, width):
    size = own.shape[0]

    def kernel(core_ref, own_ref, other_ref, out_ref, sem):
        moves = []
        for n, (ref, side) in enumerate(((own_ref, core_ref[0]), (other_ref, 1 - core_ref[0]))):
            start = pl.multiple_of(side * size, size)
            moves.append(
                pltpu.make_async_copy(
                    ref.at[:, pl.ds(0, width)], out_ref.at[pl.ds(start, size), :], sem.at[n]
                )
            )
        for move in moves:
            move.start()
        for move in moves:
            move.wait()

    whole = pl.BlockSpec(memory_space=pltpu.VMEM)
    return pl.pallas_call(
        kernel,
        grid_spec=pltpu.PrefetchScalarGridSpec(
            num_scalar_prefetch=1,
            grid=(),
            in_specs=[whole] * 2,
            out_specs=pl.BlockSpec(memory_space=pltpu.HBM),
            scratch_shapes=[pltpu.SemaphoreType.DMA((2,))],
        ),
        out_shape=jax.ShapeDtypeStruct((2 * size, width), bf16),
        compiler_params=pltpu.CompilerParams(vmem_limit_bytes=8 << 20),
        cost_estimate=HINT,
        name="place_rows",
    )(core, own, other)


def after_attention(pick, mine, far, rows, exit_row, gain, shift, b_o_rows, a_up_rows):
    width = rows.shape[1]
    total = mine.astype(f32) + far.astype(f32)
    down_o = factor * jnp.where(pick, total[:, width:], 0.0).astype(bf16)
    middle = rows.astype(f32) + total[:, :width] + exit_row + dot_nn(down_o, b_o_rows)
    unit, _ = standardize(middle)
    low = (unit * gain + shift).astype(bf16)
    down_up = factor * jnp.where(pick, dot_nt(low, a_up_rows), 0.0).astype(bf16)
    return middle, jnp.concatenate([low, down_up + down_o], axis=1)


def after_hidden(pick, mine, far, middle, exit_row, b_down_rows):
    width = middle.shape[1]
    total = mine.astype(f32) + far.astype(f32)
    down = factor * jnp.where(pick, total[:, width:], 0.0).astype(bf16)
    out = middle + total[:, :width] + exit_row + dot_nn(down, b_down_rows)
    return out.astype(bf16), down


def back_middle(pick, mine, far, middle, loss, gain, a_up_rows, b_o_rows):
    width = middle.shape[1]
    total = mine.astype(f32) + far.astype(f32)
    grad_down = (factor * jnp.where(pick, total[:, width:], 0.0)).astype(bf16)
    grad_normed = total[:, :width] + dot_nn(grad_down, a_up_rows)
    unit, inverse = standardize(middle)
    grad = loss.astype(f32) + norm_back(grad_normed * gain, unit, inverse)
    low = grad.astype(bf16)
    grad_o = (factor * jnp.where(pick, dot_nt(low, b_o_rows), 0.0)).astype(bf16)
    return grad, jnp.concatenate([low, grad_o + grad_down], axis=1)


def back_first(pick, mine, far, grad_down, rows, grad_middle, gain, a_rows):
    total = mine.astype(f32) + far.astype(f32)
    grad_normed = total + dot_nn(grad_down, a_rows)
    unit, inverse = standardize(rows.astype(f32))
    return ((grad_middle + norm_back(grad_normed * gain, unit, inverse)).astype(bf16),)


def pack_terms(tensor, core, two, back, attended, grad_pre, hidden, grad_dd, local):
    width = two[0].shape[1] - AUG
    half = two[0].shape[0]
    cut = local // 4

    def kernel(t_ref, two_a, two_b, back_a, back_b, att_ref, gp_ref, hid_ref, gdd_ref, out):
        lanes = pl.ds(pl.multiple_of(t_ref[0] * local, local), local)
        mine = pl.ds(pl.multiple_of(t_ref[1] * half, half), half)
        theirs = pl.ds(pl.multiple_of((1 - t_ref[1]) * half, half), half)
        halves = ((two_a, back_a, mine), (two_b, back_b, theirs))

        def both(make):
            return make(*halves[0]) + make(*halves[1])

        terms = [
            both(lambda t, b, r: dot_tn(b[:, width:], att_ref[r, :]))[PAIR : 2 * PAIR],
            both(lambda t, b, r: dot_tn(t[:, width:], b[:, lanes]))[PAIR : 2 * PAIR],
            both(lambda t, b, r: dot_tn(b[:, width:], t[:, lanes]))[:PAIR],
        ]
        for n, term in enumerate(terms):
            low = term.astype(bf16)
            for g in range(4):
                out[g, n * PAIR : (n + 1) * PAIR, :] = low[:, g * cut : (g + 1) * cut]
        base = len(terms) * PAIR
        wide_terms = (
            dot_tn(two_a[:, width:], gp_ref[:half, :]) + dot_tn(two_b[:, width:], gp_ref[half:, :]),
            dot_tn(gdd_ref[...], hid_ref[...]),
        )
        for term in wide_terms:
            low = term[:PAIR].astype(bf16)
            tiles = low.shape[1] // (4 * cut)
            for g in range(4):
                for t in range(tiles):
                    c = (g * tiles + t) * cut
                    out[g, base + t * PAIR : base + (t + 1) * PAIR, :] = low[:, c : c + cut]
            base += tiles * PAIR

    tiles = hidden.shape[1] // local
    whole = pl.BlockSpec(memory_space=pltpu.VMEM)
    return pl.pallas_call(
        kernel,
        grid_spec=pltpu.PrefetchScalarGridSpec(
            num_scalar_prefetch=1, grid=(), in_specs=[whole] * 8, out_specs=whole
        ),
        out_shape=jax.ShapeDtypeStruct((4, (3 + 2 * tiles) * PAIR, cut), bf16),
        compiler_params=pltpu.CompilerParams(vmem_limit_bytes=24 << 20),
        cost_estimate=HINT,
        name="pack_terms",
    )(jnp.stack([tensor, core]), *two, *back, attended, grad_pre, hidden, grad_dd)


def pack_layer(tensor, core, down, loss, local):
    half = down[0].shape[0]
    cut = local // 4

    def kernel(t_ref, own_ref, other_ref, loss_ref, out, low, sem):
        lanes = pl.ds(pl.multiple_of(t_ref[0] * local, local), local)
        move = pltpu.make_async_copy(loss_ref.at[:, lanes], low, sem)
        move.start()
        move.wait()
        mine = pl.ds(pl.multiple_of(t_ref[1] * half, half), half)
        theirs = pl.ds(pl.multiple_of((1 - t_ref[1]) * half, half), half)
        term = dot_tn(own_ref[...], low[mine, :]) + dot_tn(other_ref[...], low[theirs, :])
        for g in range(4):
            out[g] = term[:PAIR, g * cut : (g + 1) * cut].astype(bf16)

    whole = pl.BlockSpec(memory_space=pltpu.VMEM)
    return pl.pallas_call(
        kernel,
        grid_spec=pltpu.PrefetchScalarGridSpec(
            num_scalar_prefetch=1,
            grid=(),
            in_specs=[whole] * 2 + [pl.BlockSpec(memory_space=pltpu.HBM)],
            out_specs=whole,
            scratch_shapes=[pltpu.VMEM((2 * half, local), bf16), pltpu.SemaphoreType.DMA],
        ),
        out_shape=jax.ShapeDtypeStruct((4, PAIR, cut), bf16),
        compiler_params=pltpu.CompilerParams(vmem_limit_bytes=4 << 20),
        cost_estimate=HINT,
        name="pack_layer",
    )(jnp.stack([tensor, core]), *down, loss)


def pack_projections(tensor, grad_down, normed_wide, grad_qkv, local):
    width = normed_wide.shape[1] - AUG
    cut = local // 4

    def kernel(t_ref, gd_ref, nw_ref, gq_ref, out):
        lanes = pl.ds(pl.multiple_of(t_ref[0] * local, local), local)
        down = dot_tn(gd_ref[...], nw_ref[:, lanes]).astype(bf16)
        up = dot_tn(nw_ref[:, width:], gq_ref[...]).astype(bf16)
        for i in range(3):
            rows = slice(i * PAIR, (i + 1) * PAIR)
            for g in range(4):
                out[g, rows, :] = down[rows, g * cut : (g + 1) * cut]
                c = i * local + g * cut
                out[g, (3 + i) * PAIR : (4 + i) * PAIR, :] = up[rows, c : c + cut]

    whole = pl.BlockSpec(memory_space=pltpu.VMEM)
    return pl.pallas_call(
        kernel,
        grid_spec=pltpu.PrefetchScalarGridSpec(
            num_scalar_prefetch=1, grid=(), in_specs=[whole] * 3, out_specs=whole
        ),
        out_shape=jax.ShapeDtypeStruct((4, 6 * PAIR, cut), bf16),
        compiler_params=pltpu.CompilerParams(vmem_limit_bytes=4 << 20),
        cost_estimate=HINT,
        name="pack_projections",
    )(tensor, grad_down, normed_wide, grad_qkv)


def unpack_terms(context, owner, near, cross, tiles):
    cut = near[0].shape[2]
    half = cut // 2

    def kernel(c_ref, owner_ref, n0, n1, c0, c1, a_attn, b_attn, a_up, b_up, a_down, b_down):
        first = c_ref[0] == 0

        for k in range(4):
            for s in range(SLOTS):
                who = owner_ref[k * SLOTS + s]

                def value(row, n_ref=n0, c_ref=c0):
                    rows = slice(row + s * RANK, row + (s + 1) * RANK)
                    return n_ref[k, rows, :].astype(f32) + c_ref[k, rows, :].astype(f32)

                def narrow(row, *refs):
                    v = value(row, *refs)
                    return jnp.where(first, v[:, :half], v[:, half:])

                for i in range(3):
                    a_attn[i, pl.ds(who, 1)] = narrow(i * PAIR, n1, c1)[None]
                    b_attn[i, pl.ds(who, 1)] = narrow((3 + i) * PAIR, n1, c1)[None]
                a_attn[3, pl.ds(who, 1)] = narrow(0)[None]
                b_attn[3, pl.ds(who, 1)] = narrow(PAIR)[None]
                a_up[pl.ds(who, 1)] = narrow(2 * PAIR)[None]
                b_down[pl.ds(who, 1)] = narrow(6 * PAIR, n1, c1)[None]
                for n, ref in enumerate((b_up, a_down)):
                    start = (3 + n * tiles) * PAIR
                    for t in range(tiles // 2):
                        ref[pl.ds(who, 1), :, t * cut : (t + 1) * cut] = jnp.where(
                            first,
                            value(start + t * PAIR),
                            value(start + (tiles // 2 + t) * PAIR),
                        )[None]

    narrow_shape = (ADAPTERS, RANK, half)
    wide_shape = (ADAPTERS, RANK, tiles * half)
    whole = pl.BlockSpec(memory_space=pltpu.VMEM)
    shapes = [(4,) + narrow_shape, (4,) + narrow_shape, narrow_shape, wide_shape, wide_shape, narrow_shape]
    return pl.pallas_call(
        kernel,
        grid_spec=pltpu.PrefetchScalarGridSpec(
            num_scalar_prefetch=2, grid=(), in_specs=[whole] * 4, out_specs=[whole] * 6
        ),
        out_shape=[jax.ShapeDtypeStruct(shape, f32) for shape in shapes],
        compiler_params=pltpu.CompilerParams(vmem_limit_bytes=4 << 20),
        cost_estimate=HINT,
        name="unpack_terms",
    )(context, owner, *near, *cross)


def unpack_plain(context, owner, total, tiles, ctx_size):
    cut = total.shape[2]
    place = (jnp.arange(ADAPTERS, dtype=jnp.int32)[:, None] == owner[None, :]).astype(f32)
    parts = total.reshape(4, -1, SLOTS, RANK, cut)
    placed = jnp.einsum("ag,ngrc->narc", place, jnp.transpose(parts, (1, 0, 2, 3, 4)).reshape(
        parts.shape[1], 4 * SLOTS, RANK, cut), precision=lax.Precision.HIGHEST)

    def narrow(items):
        size = items.shape[-1] // ctx_size
        return lax.dynamic_slice_in_dim(items, context * size, size, items.ndim - 1)

    def broad(items):
        joined = jnp.transpose(items, (1, 2, 0, 3)).reshape(ADAPTERS, RANK, -1)
        return narrow(joined)

    base = 3 + 2 * tiles
    return (
        narrow(jnp.concatenate([placed[base : base + 3], placed[:1]])),
        narrow(jnp.concatenate([placed[base + 3 : base + 6], placed[1:2]])),
        narrow(placed[2]),
        broad(placed[3 : 3 + tiles]),
        broad(placed[3 + tiles : base]),
        narrow(placed[base + 6]),
    )


def project(own, far, weight, bias, local):
    tokens, wide = own.shape
    blocks = 3 + (2 if far is not None else 0)

    def column(n):
        return jnp.where(n < 3, n, n - 2)

    def kernel(*refs):
        bias_ref, w_ref, out_ref = refs[-3:]

        def write(x_ref):
            at = pl.ds(pl.multiple_of(column(pl.program_id(0)) * local, local), local)
            out_ref[...] = (dot_nn(x_ref[...], w_ref[:, at]) + bias_ref[...]).astype(bf16)

        if far is None:
            write(refs[0])
        else:
            pl.when(pl.program_id(0) < 3)(lambda: write(refs[0]))
            pl.when(pl.program_id(0) >= 3)(lambda: write(refs[1]))

    rows = [own] if far is None else [own, far]
    return pl.pallas_call(
        kernel,
        grid=(blocks,),
        in_specs=[pl.BlockSpec((tokens, wide), lambda n: (0, 0))] * len(rows)
        + [
            pl.BlockSpec((1, local), lambda n: (0, column(n))),
            pl.BlockSpec(memory_space=pltpu.VMEM),
        ],
        out_specs=pl.BlockSpec((tokens, local), lambda n: (0, n)),
        out_shape=jax.ShapeDtypeStruct((tokens, blocks * local), bf16),
        compiler_params=pltpu.CompilerParams(vmem_limit_bytes=12 << 20),
        cost_estimate=HINT,
        name="project",
    )(*rows, bias, weight)


def expand(own, other, weight, bias):
    size, wide = own.shape
    hidden = weight.shape[1]
    cut = 512
    part = 128

    def kernel(own_ref, other_ref, w_ref, b_ref, h_ref, s_ref):
        for i, x_ref in enumerate((own_ref, other_ref)):
            for r in range(0, size, part):
                pre = dot_nn(x_ref[r : r + part, :], w_ref[...]) + b_ref[...]
                phi = 0.5 * (1.0 + lax.erf(pre * (2.0**-0.5)))
                bell = jnp.exp(-0.5 * pre * pre) * (0.5 / jnp.pi) ** 0.5
                to = slice(i * size + r, i * size + r + part)
                h_ref[to, :] = (pre * phi).astype(bf16)
                s_ref[to, :] = (phi + pre * bell).astype(bf16)

    block = pl.BlockSpec((2 * size, cut), lambda n: (0, n))
    shape = jax.ShapeDtypeStruct((2 * size, hidden), bf16)
    return pl.pallas_call(
        kernel,
        grid=(hidden // cut,),
        in_specs=[
            pl.BlockSpec((size, wide), lambda n: (0, 0)),
            pl.BlockSpec((size, wide), lambda n: (0, 0)),
            pl.BlockSpec((wide, cut), lambda n: (0, n)),
            pl.BlockSpec((1, cut), lambda n: (0, n)),
        ],
        out_specs=[block, block],
        out_shape=[shape, shape],
        compiler_params=pltpu.CompilerParams(vmem_limit_bytes=14 << 20),
        cost_estimate=HINT,
        name="expand",
    )(own, other, weight, bias)


def back_hidden(loss, weight, slope):
    tokens, wide = loss.shape
    hidden = weight.shape[0]
    cut = 512

    def kernel(x_ref, w_ref, s_ref, out_ref):
        grad = dot_nt(x_ref[...], w_ref[...])
        out_ref[...] = (grad * s_ref[...].astype(f32)).astype(bf16)

    block = pl.BlockSpec((tokens, cut), lambda n: (0, n))
    return pl.pallas_call(
        kernel,
        grid=(hidden // cut,),
        in_specs=[
            pl.BlockSpec((tokens, wide), lambda n: (0, 0)),
            pl.BlockSpec((cut, wide), lambda n: (n, 0)),
            block,
        ],
        out_specs=block,
        out_shape=jax.ShapeDtypeStruct((tokens, hidden), bf16),
        compiler_params=pltpu.CompilerParams(vmem_limit_bytes=36 << 20),
        cost_estimate=HINT,
        name="back_hidden",
    )(loss, weight, slope)


class Direct:
    def __init__(self, own, half_axis, context):
        size = own.shape[half_axis] // 2
        self.own = own
        self.part = lax.dynamic_slice_in_dim(own, context * size, size, half_axis)

    def first(self, *waits):
        part = gate(self.part, *waits)
        self.near = [
            lax.ppermute(part, "fsdp", [(i, i ^ k) for i in range(4)]) for k in range(1, 4)
        ]

    def second(self, *waits):
        *self.near, _ = lax.optimization_barrier((*self.near, waits))
        self.far = [lax.ppermute(piece, "ctx", SWAP_Y) for piece in self.near]

    def pieces(self):
        return (self.own, *[p for pair in zip(self.near, self.far) for p in pair])


class Ring:
    def __init__(self, own, half_axis, context, inner):
        size = own.shape[half_axis] // 2
        self.own = own
        self.inner = inner
        self.part = lax.dynamic_slice_in_dim(own, context * size, size, half_axis)

    def first(self, *waits):
        part = gate(self.part, *waits)
        self.one = lax.ppermute(part, "fsdp", [(0, 1), (1, 0), (2, 3), (3, 2)])
        self.across = lax.ppermute(part, "fsdp", [(1, 2), (2, 1)])

    def second(self, *waits):
        self.one, self.across, *_ = lax.optimization_barrier((self.one, self.across, *waits))
        self.y_one = lax.ppermute(self.one, "ctx", SWAP_Y)
        self.outward = lax.ppermute(self.across, "fsdp", [(1, 0), (2, 3)])
        self.back = lax.ppermute(self.one, "fsdp", [(1, 2), (2, 1)])

    def third(self, *waits):
        outward, self.back, self.y_one, across, *_ = lax.optimization_barrier(
            (self.outward, self.back, self.y_one, self.across, *waits)
        )
        self.two = jnp.where(self.inner, across, outward)
        self.y_two = lax.ppermute(self.two, "ctx", SWAP_Y)
        self.last = lax.ppermute(self.back, "fsdp", [(1, 0), (2, 3)])

    def fourth(self, *waits):
        last, self.y_two, back, *_ = lax.optimization_barrier(
            (self.last, self.y_two, self.back, *waits)
        )
        self.three = jnp.where(self.inner, back, last)
        self.y_three = lax.ppermute(self.three, "ctx", SWAP_Y)

    def pieces(self):
        return (
            self.own,
            self.one,
            self.y_one,
            self.two,
            self.y_two,
            self.three,
            self.y_three,
        )


def matmul(rows, half, weight, cut, flipped, parts=1):
    summed = rows.shape[1]
    steps = summed // cut
    wide = weight.shape[0] if flipped else weight.shape[1]
    size = rows.shape[0] // 2
    piece = size // parts

    def kernel(half_ref, x_ref, w_ref, *refs):
        outs = refs[:parts]
        part = dot_nt(x_ref[...], w_ref[...]) if flipped else dot_nn(x_ref[...], w_ref[...])

        def finish(total):
            for i, out_ref in enumerate(outs):
                out_ref[...] = total[i * piece : (i + 1) * piece].astype(bf16)

        if steps == 1:
            finish(part)
            return
        acc = refs[parts]
        step = pl.program_id(0)

        @pl.when(step == 0)
        def _():
            acc[...] = part

        @pl.when((step > 0) & (step < steps - 1))
        def _():
            acc[...] += part

        @pl.when(step == steps - 1)
        def _():
            finish(acc[...] + part)

    if flipped:
        w_spec = pl.BlockSpec((wide, cut), lambda k, h: (0, k))
    else:
        w_spec = pl.BlockSpec((cut, wide), lambda k, h: (k, 0))
    return pl.pallas_call(
        kernel,
        grid_spec=pltpu.PrefetchScalarGridSpec(
            num_scalar_prefetch=1,
            grid=(steps,),
            in_specs=[pl.BlockSpec((size, cut), lambda k, h: (h[0], k)), w_spec],
            out_specs=[pl.BlockSpec((piece, wide), lambda k, h: (0, 0))] * parts,
            scratch_shapes=[pltpu.VMEM((size, wide), f32)] if steps > 1 else [],
        ),
        out_shape=[jax.ShapeDtypeStruct((piece, wide), bf16)] * parts,
        compiler_params=pltpu.CompilerParams(vmem_limit_bytes=22 << 20),
        cost_estimate=HINT,
        name="matmul",
    )(half, rows, weight)


def back_attend(core, own, other, weight):
    size = own.shape[0]
    local = weight.shape[0]

    def kernel(core_ref, own_ref, other_ref, w_ref, out_ref):
        w = w_ref[...]
        mine = pl.multiple_of(core_ref[0] * size, size)
        theirs = pl.multiple_of((1 - core_ref[0]) * size, size)
        out_ref[pl.ds(mine, size), :] = dot_nt(own_ref[...], w).astype(bf16)
        out_ref[pl.ds(theirs, size), :] = dot_nt(other_ref[...], w).astype(bf16)

    whole = pl.BlockSpec(memory_space=pltpu.VMEM)
    return pl.pallas_call(
        kernel,
        grid_spec=pltpu.PrefetchScalarGridSpec(
            num_scalar_prefetch=1, grid=(), in_specs=[whole] * 3, out_specs=whole
        ),
        out_shape=jax.ShapeDtypeStruct((2 * size, local), bf16),
        compiler_params=pltpu.CompilerParams(vmem_limit_bytes=6 << 20),
        cost_estimate=HINT,
        name="back_attend",
    )(core, own, other, weight)


def gate(value, *waits):
    if not waits:
        return value
    return lax.optimization_barrier((value,) + waits)[0]


def make_body(ctx_size):
    pair_ctx = ctx_size == 2

    def body(
        inputs,
        loss_sensitivity,
        parent_block,
        adapter_of,
        w_qkv,
        bias_qv,
        w_o,
        exit_offsets,
        ln_gain,
        ln_bias,
        w_in,
        hidden_offset_frozen,
        w_out,
        a_attn,
        b_attn,
        a_up,
        b_up,
        a_down,
        b_down,
    ):
        group = lax.axis_index("fsdp")
        context = lax.axis_index("ctx")
        tensor = lax.axis_index("tp")
        core = tensor % 2
        tokens, width = inputs.shape
        half = tokens // 2
        local = w_qkv.shape[2]
        shard = w_qkv.shape[1]
        hidden_local = w_in.shape[1]
        heads = local // HD
        blocks = tokens // BLOCK
        scale = HD ** (-0.5)
        wide = width + AUG

        def on(value, axis, pairs):
            return lax.ppermute(value, axis, pairs)

        def own_rows(matrix):
            return lax.dynamic_slice_in_dim(matrix, core * half, half, 0)

        def other_rows(matrix):
            return lax.dynamic_slice_in_dim(matrix, (1 - core) * half, half, 0)

        def natural(own, other):
            return jnp.concatenate(
                [jnp.where(core == 0, own, other), jnp.where(core == 0, other, own)], axis=0
            )

        def local_lanes(matrix):
            return lax.dynamic_slice_in_dim(matrix, tensor * local, local, matrix.ndim - 1)

        def put(buffer, piece, row, column):
            return lax.dynamic_update_slice(buffer, piece, (row, column))

        swap_y = [(0, 1), (1, 0)]
        spot = jnp.stack([group, context]).astype(jnp.int32)

        def send_tp(others, own_low, *waits):
            mine = join(own_low, [on(other, "tp", CORE_SWAP) for other in others])
            return mine, on(gate(mine, *waits), "tp", X_SWAP)

        def sum_sent(sent, waits=()):
            mine, far = sent
            return mine.astype(f32) + gate(far, *waits).astype(f32)

        pair = lax.dynamic_slice_in_dim(adapter_of, group * SLOTS, SLOTS)

        def pick_pair(array, axis):
            return jnp.concatenate(
                [lax.dynamic_slice_in_dim(array, pair[s], 1, axis) for s in range(SLOTS)], axis
            )

        a_pair = jnp.swapaxes(pick_pair(a_attn, 1), 2, 3)
        def down_up_pad(matrix, before=0):
            return jnp.pad(matrix, ((before, AUG - before - matrix.shape[0]), (0, 0)))

        a_qkv_rows = down_up_pad(a_pair[:3].reshape(3 * PAIR, width).astype(bf16))
        a_o_rows = local_lanes(a_pair[3].reshape(PAIR, width)).astype(bf16)
        b_pair = pick_pair(b_attn, 1)
        b_qkv_rows = local_lanes(b_pair[:3]).reshape(3, PAIR, local).astype(bf16)
        b_o_rows = down_up_pad(b_pair[3].reshape(PAIR, width).astype(bf16), PAIR)
        a_up_rows = down_up_pad(
            jnp.swapaxes(pick_pair(a_up, 0), 1, 2).reshape(PAIR, width).astype(bf16)
        )
        b_up_rows = pick_pair(b_up, 0).reshape(PAIR, hidden_local).astype(bf16)
        a_down_rows = (
            jnp.swapaxes(pick_pair(a_down, 0), 1, 2).reshape(PAIR, hidden_local).astype(bf16)
        )
        b_down_rows = down_up_pad(pick_pair(b_down, 0).reshape(PAIR, width).astype(bf16))

        def bias_lanes(opened):
            count = opened.shape[1]
            block = jnp.arange(count * BLOCK, dtype=jnp.int32) // BLOCK
            hit = opened[:, :, None] & (block[None, None, :] == jnp.arange(count)[None, :, None])
            return jnp.where(jnp.any(hit, axis=1), 0.0, neg_fill).astype(f32)

        reach, slot = ancestry(parent_block[0])
        all_blocks = reach.shape[0]
        first_block = context * blocks
        far_blocks = blocks if pair_ctx else all_blocks
        reach_rows = lax.dynamic_slice_in_dim(reach, first_block, blocks, 0)
        block_ids = jnp.arange(far_blocks, dtype=jnp.int32)
        far_open = (reach_rows[:, :far_blocks] > 0.5) & (block_ids[None, :] < first_block)
        own_open = lax.dynamic_slice_in_dim(reach_rows, first_block, blocks, 1) > 0.5
        far_bias = bias_lanes(far_open)
        own_bias = bias_lanes(own_open)

        slots = lax.dynamic_slice_in_dim(slot, first_block, blocks).astype(jnp.int32)
        lane_slot = (jnp.arange(AUG, dtype=jnp.int32) // RANK) % SLOTS

        def picks(first_row, count):
            block = (jnp.arange(count, dtype=jnp.int32) + first_row) // BLOCK
            row_slot = jnp.sum(
                jnp.where(block[:, None] == jnp.arange(blocks)[None, :], slots[None, :], 0), axis=1
            )
            return (row_slot[:, None] == lane_slot[None, :]).astype(f32)

        pick_own = picks(core * half, half)

        gain_one, shift_one = ln_gain[0][None, :], ln_bias[0][None, :]
        gain_two, shift_two = ln_gain[1][None, :], ln_bias[1][None, :]

        def widen(low, tail):
            return jnp.concatenate([low, tail], axis=1)

        def own_norm(places):
            return norm_wide([inputs], places, slots, a_qkv_rows, gain_one, shift_one, tokens)

        q_aug = jnp.concatenate(
            [jnp.pad(b_qkv_rows[i], ((0, 0), (i * local, (2 - i) * local))) for i in range(3)]
            + [jnp.zeros((AUG - 3 * PAIR, 3 * local), bf16)],
            axis=0,
        )
        o_aug = down_up_pad(a_o_rows, PAIR).T
        in_aug = down_up_pad(b_up_rows)
        out_aug = down_up_pad(a_down_rows).T
        if pair_ctx:
            quarter = tokens // 4
            sent = lax.dynamic_slice_in_dim(inputs, tensor * quarter, quarter, 0)
            far_quarter = on(sent, "ctx", [(0, 1)])

            far_places = jnp.stack([tensor, tensor ^ 2, tensor ^ 1, tensor ^ 3]).astype(jnp.int32)
            inner = (group == 1) | (group == 2)
            q_ring = Ring(w_qkv, 1, context, inner)
            o_ring = Direct(w_o, 0, context)
            in_ring = Ring(w_in, 0, context, inner)
            out_ring = Ring(w_out, 0, context, inner)
            q_ring.first()
            q_ring.second()
            q_ring.third(far_quarter)
            normed_wide = own_norm(gate(jnp.arange(4, dtype=jnp.int32), q_ring.y_one))
            far_quarter, _ = lax.optimization_barrier((far_quarter, q_ring.two))
            far_x = on(far_quarter, "tp", X_SWAP)
            far_core = on(far_quarter, "tp", CORE_SWAP)
            far_x, far_core, normed_wide, _ = lax.optimization_barrier(
                (far_x, far_core, normed_wide, q_ring.last)
            )
            q_ring.fourth(normed_wide)
            o_ring.first(q_ring.last)
            far_both = on(far_x, "tp", CORE_SWAP)
            far_wide = norm_wide(
                [far_quarter, far_x, far_core, far_both],
                far_places,
                slot[:blocks].astype(jnp.int32),
                a_qkv_rows,
                gain_one,
                shift_one,
                tokens,
            )
            o_ring.second(q_ring.y_three, far_wide)
            in_ring.first(*o_ring.near)
            q_full = assemble(
                gate(spot, *o_ring.near, far_wide),
                q_ring.pieces(),
                q_aug,
                wide,
                3 * local,
                ("rows", shard, shard // 2),
                3,
            )
        else:
            normed_wide = own_norm(jnp.arange(4, dtype=jnp.int32))
            own_q = jnp.transpose(w_qkv, (1, 0, 2)).reshape(shard, 3 * local)
            q_full = jnp.concatenate([lax.all_gather(own_q, "fsdp", axis=0, tiled=True), q_aug], 0)
            o_full = jnp.concatenate([lax.all_gather(w_o, "fsdp", axis=1, tiled=True), o_aug], 1)
            in_full = jnp.concatenate([lax.all_gather(w_in, "fsdp", axis=0, tiled=True), in_aug], 0)
            out_full = jnp.concatenate(
                [lax.all_gather(w_out, "fsdp", axis=1, tiled=True), out_aug], 1
            )

        normed, reduced_qkv = normed_wide[:, :width], normed_wide[:, width:]
        zero_bias = jnp.zeros((local,), f32)
        q_bias = jnp.concatenate([bias_qv[0], zero_bias, bias_qv[1]])[None, :]
        if pair_ctx:
            qkv = project(normed_wide, far_wide, q_full, q_bias, local)
            far_kv = qkv
            far_base = 3 * heads
            qkv, *_ = lax.optimization_barrier((qkv, in_ring.one, in_ring.across, *o_ring.far))
            in_ring.second(qkv)
            far_kv = qkv
        else:
            qkv = project(normed_wide, None, q_full, q_bias, local)
            far_kv = lax.all_gather(qkv[:, local:], "ctx", axis=0, tiled=True)
            far_base = 0

        attended_f, attended, probs_far, probs_own = attend_forward(
            qkv, far_kv, far_base, far_bias, own_bias, heads, scale
        )
        if pair_ctx:
            in_ring.third(attended)
            o_full = assemble(
                gate(spot, attended),
                o_ring.pieces(),
                o_aug,
                local,
                wide,
                ("columns", shard, local // 2),
                0,
                True,
            )
        core_id = core.astype(jnp.int32)[None]
        other_id = 1 - core_id
        branch_sent = send_tp(
            matmul(attended, other_id, o_full, local, False),
            matmul(attended, core_id, o_full, local, False)[0],
        )
        branch_far = branch_sent[1]
        if pair_ctx:
            in_ring.fourth(branch_sent[0])
            out_ring.first(in_ring.last, branch_sent[0])
            branch_far = gate(branch_far, in_ring.y_three, out_ring.one, out_ring.across)
        middle, two_own = row_call(
            after_attention,
            "after_attention",
            core_id,
            slots,
            half,
            [(branch_sent[0], False), (branch_far, False), (inputs, True)],
            [exit_offsets[:1], gain_two, shift_two, b_o_rows, a_up_rows],
            [(width, f32), (wide, bf16)],
        )
        two_other = on(two_own, "tp", CORE_SWAP)

        if pair_ctx:
            out_ring.second(branch_far)
            in_full = assemble(
                gate(spot, out_ring.outward, out_ring.back),
                in_ring.pieces(),
                in_aug,
                wide,
                hidden_local,
                ("rows", shard, shard // 2),
                0,
            )
        hidden, slope = expand(two_own, two_other, in_full, hidden_offset_frozen[None, :])
        if pair_ctx:
            out_ring.third()
            out_ring.fourth()
            out_full = assemble(
                gate(spot, hidden),
                out_ring.pieces(),
                out_aug,
                hidden_local,
                wide,
                ("columns", shard, hidden_local // 2),
                0,
            )

        loss_own = own_rows(loss_sensitivity)
        loss_rel = jnp.concatenate([loss_own, other_rows(loss_sensitivity)], axis=0)
        pick_rel = jnp.concatenate([pick_own, picks((1 - core) * half, half)], axis=0)
        grad_down_down = (factor * dot_nt(loss_rel, b_down_rows) * pick_rel).astype(bf16)
        loss_wide = widen(loss_rel, grad_down_down)
        grad_pre = back_hidden(loss_wide, out_full, slope)
        first_id = jnp.zeros((1,), jnp.int32)
        second_id = first_id + 1
        ff_cut = hidden_local // 2
        two_sent = send_tp(
            matmul(grad_pre, second_id, in_full, ff_cut, True),
            matmul(grad_pre, first_id, in_full, ff_cut, True)[0],
        )
        late_hidden = gate(hidden, two_sent[0])
        exit_sent = send_tp(
            matmul(late_hidden, second_id, out_full, ff_cut, False, 2),
            matmul(late_hidden, first_id, out_full, ff_cut, False)[0],
            two_sent[1],
        )
        grad_middle, back_own = row_call(
            back_middle,
            "back_middle",
            core_id,
            slots,
            half,
            [
                (two_sent[0], False),
                (gate(two_sent[1], exit_sent[0]), False),
                (middle, False),
                (loss_sensitivity, True),
            ],
            [gain_two, a_up_rows, b_o_rows],
            [(width, f32), (wide, bf16)],
        )
        back_other = on(back_own, "tp", CORE_SWAP)
        grad_attended = back_attend(core_id, back_own, back_other, o_full)

        grad_q, grad_k, grad_v, far_grads = attend_backward(
            qkv, far_kv, far_base, grad_attended, attended_f, probs_far, probs_own, heads, scale
        )
        if pair_ctx:
            more = on(far_grads, "ctx", [(1, 0)])
        else:
            more = lax.psum_scatter(far_grads, "ctx", scatter_dimension=1, tiled=True)
        layer_own, down_own = row_call(
            after_hidden,
            "after_hidden",
            core_id,
            slots,
            half,
            [(exit_sent[0], False), (exit_sent[1], False), (middle, False)],
            [exit_offsets[1:], b_down_rows],
            [(width, bf16), (AUG, bf16)],
        )
        down_other = on(down_own, "tp", CORE_SWAP)
        tiles = hidden_local // local

        def to_owners(slabs):
            pieces = [
                lax.dynamic_index_in_dim(slabs, group ^ k, 0, keepdims=False) for k in range(4)
            ]
            return jnp.stack(
                pieces[:1]
                + [on(pieces[k], "fsdp", [(i, i ^ k) for i in range(4)]) for k in range(1, 4)]
            )

        tensor_id, core_at = tensor.astype(jnp.int32), core.astype(jnp.int32)
        packed = pack_terms(
            tensor_id,
            core_at,
            (two_own, two_other),
            (back_own, back_other),
            attended,
            grad_pre,
            hidden,
            grad_down_down,
            local,
        )
        packed_layer = pack_layer(
            tensor_id, core_at, (down_own, down_other), loss_sensitivity, local
        )
        grad_k = gate(grad_k, packed, packed_layer)
        grad_qkv = jnp.concatenate(
            [
                grad_q,
                (grad_k.astype(f32) + more[0].astype(f32)).astype(bf16),
                (grad_v.astype(f32) + more[1].astype(f32)).astype(bf16),
            ],
            axis=1,
        )
        low_part = dot_nt(grad_qkv, q_full[width:]).astype(bf16)
        low_core = on(low_part, "tp", CORE_SWAP)
        low_pair = round_low(low_part.astype(f32) + low_core.astype(f32))
        low_far = on(low_pair, "tp", X_SWAP)
        low_sum = low_pair.astype(f32) + low_far.astype(f32)
        grad_down_qkv = (factor * low_sum * picks(0, tokens)).astype(bf16)
        one_other, one_own = back_project(
            gate(grad_qkv, low_part), core_id, q_full, width
        )
        one_sent = send_tp([one_other], one_own, low_far)
        layer_other = on(layer_own, "tp", CORE_SWAP)
        layer_out = place_rows(core_id, layer_own, layer_other, width)
        near = to_owners(packed)
        near_qkv = to_owners(
            jnp.concatenate(
                [
                    pack_projections(tensor_id[None], grad_down_qkv, normed_wide, grad_qkv, local),
                    packed_layer,
                ],
                axis=1,
            )
        )
        holder = jnp.stack([group ^ k for k in range(4)])
        owner = adapter_of.reshape(4, SLOTS)[holder].reshape(4 * SLOTS)
        if pair_ctx:
            adapter_grads = unpack_terms(
                context.astype(jnp.int32)[None],
                owner,
                (near, near_qkv),
                (on(near, "ctx", swap_y), on(near_qkv, "ctx", swap_y)),
                tiles,
            )
        else:
            total = lax.psum((near.astype(f32), near_qkv.astype(f32)), "ctx")
            adapter_grads = unpack_plain(
                context, owner, jnp.concatenate(total, axis=1), tiles, ctx_size
            )
        (grad_own,) = row_call(
            back_first,
            "back_first",
            core_id,
            slots,
            half,
            [
                (one_sent[0], False),
                (gate(one_sent[1], adapter_grads[0], layer_out), False),
                (grad_down_qkv, True),
                (inputs, True),
                (grad_middle, False),
            ],
            [gain_one, a_qkv_rows],
            [(width, bf16)],
        )
        grad_other = on(grad_own, "tp", CORE_SWAP)
        grad_inputs = place_rows(core_id, grad_own, grad_other, width)

        out_a_attn, out_b_attn, out_a_up, out_b_up, out_a_down, out_b_down = adapter_grads
        return (
            layer_out,
            grad_inputs,
            jnp.swapaxes(out_a_attn, 2, 3),
            out_b_attn,
            jnp.swapaxes(out_a_up, 1, 2),
            out_b_up,
            jnp.swapaxes(out_a_down, 1, 2),
            out_b_down,
        )

    return body


def solution(mesh):
    in_specs = (
        P(("fsdp", "ctx"), None),
        P(("fsdp", "ctx"), None),
        P("fsdp", None),
        P(),
        P(None, "fsdp", "tp"),
        P(None, "tp"),
        P("tp", "fsdp"),
        P(),
        P(),
        P(),
        P("fsdp", "tp"),
        P("tp"),
        P("tp", "fsdp"),
        P(),
        P(),
        P(),
        P(None, None, "tp"),
        P(None, "tp", None),
        P(),
    )
    out_specs = (
        P(("fsdp", "ctx"), None),
        P(("fsdp", "ctx"), None),
        P(None, None, ("tp", "fsdp", "ctx"), None),
        P(None, None, None, ("tp", "fsdp", "ctx")),
        P(None, ("tp", "fsdp", "ctx"), None),
        P(None, None, ("tp", "fsdp", "ctx")),
        P(None, ("tp", "fsdp", "ctx"), None),
        P(None, None, ("tp", "fsdp", "ctx")),
    )
    return jax.shard_map(
        make_body(mesh.shape["ctx"]),
        mesh=mesh,
        in_specs=in_specs,
        out_specs=out_specs,
        check_vma=False,
    )
```
